512 devices in a mesh: gx: 8 (over z_lo), gy: 8 (over x, z_hi), gz: 8 (over y, core).
Axes of the slice: x: 4, y: 4, z: 16 (z_hi: 2, z_lo: 8; z = z_hi * 8 + z_lo), core: 2. Of those that a mesh axis runs over, the one named last changes fastest.
Arguments:
- eigvecs: bfloat16 [16, 32, 32, 2, 3, 256], P('gx', 'gy', 'gz'), may hold values from -6 to 6
- links: float32 [16, 32, 32, 3, 2, 3, 3], P('gx', 'gy', 'gz'), may hold values from -6 to 6
- directions: int32 [4], replicated, may hold values from 0 to 2
- spin_mats: float32 [4, 4, 4], replicated, may hold values from -6 to 6
- forward_peram: bfloat16 [2, 1024, 1024], P(None, 'gx', 'gy'), may hold values from -0.1875 to 0.1875
- backward_peram: bfloat16 [2, 1024, 1024], P(None, 'gx', 'gy'), may hold values from -0.1875 to 0.1875
- chain_order: int32 [16, 2], P('gz'), may hold values from 0 to 3
Outputs:
- operators: bfloat16 [16, 2, 1024, 1024], P('gz', None, 'gx', 'gy')
The draws below stay inside these ranges and needn't reach their ends.
All inputs are finite; a program needn't handle non-finite values.
Results may differ from the reference program's by a relative error of at most 0.012.
Values may be sent and summed in bfloat16 or wider, within the bound.
A program may use at most 192 MiB of HBM per device.

```python
import math
import jax
import jax.numpy as jnp
from jax import lax

NV = 256
NB = 1024
OPS = 16
NX = 16
NY = 32
NZ = 32


def touch_ends(drawn, key, low, high):
    longest = drawn.shape.index(max(drawn.shape))
    spots = []
    for shift in (0, 1):
        where = [jax.random.randint(jax.random.fold_in(key, axis), (), 0, length) for axis, length in enumerate(drawn.shape)]
        where[longest] = (where[longest] + shift) % drawn.shape[longest]
        spots.append(tuple(where))
    return drawn.at[spots[0]].set(low).at[spots[1]].set(high)


def block_scale(own_key, extent, cuts, smallest, top_value):
    def one(axis_at, shards_of):
        draws = jax.random.uniform(jax.random.fold_in(jax.random.fold_in(own_key, 6), axis_at), (shards_of,), jnp.float32, smallest / len(cuts), top_value / len(cuts))
        return jnp.repeat(jnp.exp(draws), extent[axis_at] // shards_of).reshape((-1,) + (1,) * (len(extent) - axis_at - 1))

    level = one(*cuts[0])
    for cut in cuts[1:]:
        level = level * one(*cut)
    return level


def bell_draw(key, extent, scale, reach, cuts=(), held_as=jnp.bfloat16):
    entries = jax.random.normal(key, extent, jnp.float32) * scale
    if len(cuts) > 0:
        entries = block_scale(key, extent, cuts, -0.22, 0.18) * entries
    return jnp.clip(entries, min=-reach, max=reach).astype(held_as)


def setup_inputs(seed: int = 0) -> dict:
    key_of = jax.random.split(jax.random.key(seed), 8)
    return {
        "eigvecs": bell_draw(key_of[0], (NX, NY, NZ, 2, 3, NV), 1.0, 6.0, ((0, 8), (1, 8), (2, 8))),
        "links": bell_draw(key_of[1], (NX, NY, NZ, 3, 2, 3, 3), 0.408, 6.0, ((0, 8), (1, 8), (2, 8)), jnp.float32),
        "directions": touch_ends(jax.random.randint(key_of[2], (4,), 0, 3), jax.random.fold_in(key_of[2], 1), 0, 2).astype(jnp.int32),
        "spin_mats": bell_draw(key_of[3], (4, 4, 4), 0.5, 6.0, (), jnp.float32),
        "forward_peram": bell_draw(key_of[4], (2, NB, NB), NB ** -0.5, 0.1875, ((1, 8), (2, 8))),
        "backward_peram": bell_draw(key_of[5], (2, NB, NB), NB ** -0.5, 0.1875, ((1, 8), (2, 8))),
        "chain_order": touch_ends(jax.random.randint(key_of[6], (OPS, 2), 0, 4), jax.random.fold_in(key_of[6], 1), 0, 3).astype(jnp.int32),
    }


def transport(link_dir, shifted):
    highest = lax.Precision.HIGHEST
    real_v = shifted[..., 0, :, :].astype(jnp.float32)
    imag_v = shifted[..., 1, :, :].astype(jnp.float32)
    real_u = link_dir[..., 0, :, :]
    imag_u = link_dir[..., 1, :, :]

    def apply_link(matrix, vector):
        return jnp.einsum('...ab,...bn->...an', matrix, vector, precision=highest)
    moved_re = apply_link(real_u, real_v) - apply_link(imag_u, imag_v)
    moved_im = apply_link(real_u, imag_v) + apply_link(imag_u, real_v)
    moved = jnp.stack([moved_re, moved_im], axis=-3).astype(jnp.bfloat16)
    turned = jnp.stack([moved_im, -moved_re], axis=-3).astype(jnp.bfloat16)
    return (moved, turned)

def correlation(vec_part, moved, turned):
    width = vec_part.shape[-1]
    left_side = vec_part.reshape(-1, width)
    right_side = jnp.concatenate([moved.reshape(-1, width), turned.reshape(-1, width)], axis=1)
    product = lax.dot_general(left_side, right_side, (((0,), (0,)), ((), ())), preferred_element_type=jnp.float32)
    return jnp.stack([product[:, :width], product[:, width:]])

def complex_product(left_mat, right_mat):
    row_count = left_mat.shape[1]
    stacked = left_mat.reshape(2 * row_count, left_mat.shape[2])
    first_half = jnp.dot(stacked, right_mat[0], preferred_element_type=jnp.float32)
    second_half = jnp.dot(stacked, right_mat[1], preferred_element_type=jnp.float32)
    return jnp.stack([first_half[:row_count] - second_half[row_count:], second_half[:row_count] + first_half[row_count:]])

def reference(eigvecs, links, directions, spin_mats, forward_peram, backward_peram, chain_order):
    highest = lax.Precision.HIGHEST

    def plane_terms(plane_index, total):
        plane = lax.dynamic_index_in_dim(eigvecs, plane_index, 0, keepdims=False)
        after = lax.dynamic_index_in_dim(eigvecs, (plane_index + 1) % NX, 0, keepdims=False)
        link_plane = lax.dynamic_index_in_dim(links, plane_index, 0, keepdims=False)
        shifted = [after, jnp.roll(plane, -1, axis=0), jnp.roll(plane, -1, axis=1)]
        terms = []
        for direction in range(3):
            moved, turned = transport(link_plane[:, :, direction], shifted[direction])
            terms.append(correlation(plane, moved, turned))
        return total + jnp.stack(terms)
    elem_dir = lax.fori_loop(0, NX, plane_terms, jnp.zeros((3, 2, NV, NV), jnp.float32))
    elem_dir = elem_dir * (1.0 / math.sqrt(12.0 * NX * NY * NZ))
    chooser = (directions[:, None] == jnp.arange(3, dtype=jnp.int32)[None, :]).astype(jnp.float32)
    elementals = jnp.einsum('ke,ecij->kcij', chooser, elem_dir, precision=highest)
    spin_elem = jnp.einsum('kcij,kst->kcisjt', elementals, spin_mats, precision=highest)
    spin_elem = spin_elem.reshape(4, 2, NB, NB).astype(jnp.bfloat16)
    inverse = 1.0 / math.sqrt(NB)

    def one_operator(pair):
        left_elem = lax.dynamic_index_in_dim(spin_elem, pair[0], 0, keepdims=False)
        right_elem = lax.dynamic_index_in_dim(spin_elem, pair[1], 0, keepdims=False)
        first = complex_product(forward_peram, right_elem).astype(jnp.bfloat16)
        second = (complex_product(left_elem, first) * inverse).astype(jnp.bfloat16)
        return complex_product(second, backward_peram).astype(jnp.bfloat16)
    return lax.map(one_operator, chain_order)
```

```python
import functools
import math

import jax
import jax.numpy as jnp
from jax import lax
from jax.experimental import pallas as pl
from jax.experimental.pallas import tpu as pltpu
from jax.sharding import PartitionSpec as P

MESH_ID = pl.DeviceIdType.MESH


def passed_along(value, axis, steps):
    count = lax.axis_size(axis)
    pairs = [(source, (source + steps) % count) for source in range(count)]
    return lax.ppermute(value, axis, pairs)


def exchange_kernel(axis, n, scatter, x_ref, o_ref, send_sem, recv_sem):
    me = lax.axis_index(axis)
    barrier = pltpu.get_barrier_semaphore()
    for step in range(1, n):
        peer = lax.rem(me + step, n)
        pl.semaphore_signal(barrier, inc=1, device_id={axis: peer}, device_id_type=MESH_ID)
    pl.semaphore_wait(barrier, n - 1)
    own = x_ref.at[me] if scatter else x_ref
    local = pltpu.make_async_copy(own, o_ref.at[me], send_sem.at[0])
    local.start()
    copies = []
    for step in range(1, n):
        peer = lax.rem(me + step, n)
        source = x_ref.at[peer] if scatter else x_ref
        copy = pltpu.make_async_remote_copy(
            src_ref=source,
            dst_ref=o_ref.at[me],
            send_sem=send_sem.at[step],
            recv_sem=recv_sem.at[step],
            device_id={axis: peer},
            device_id_type=MESH_ID,
        )
        copy.start()
        copies.append(copy)
    local.wait()
    for copy in copies:
        copy.wait()


def exchange(value, axis, scatter, collective_id):
    n = lax.axis_size(axis)
    out_shape = value.shape if scatter else (n,) + value.shape
    return pl.pallas_call(
        functools.partial(exchange_kernel, axis, n, scatter),
        out_shape=jax.ShapeDtypeStruct(out_shape, value.dtype),
        in_specs=[pl.BlockSpec(memory_space=pltpu.VMEM)],
        out_specs=pl.BlockSpec(memory_space=pltpu.VMEM),
        scratch_shapes=[pltpu.SemaphoreType.DMA((n,)), pltpu.SemaphoreType.DMA((n,))],
        compiler_params=pltpu.CompilerParams(collective_id=collective_id, has_side_effects=True),
    )(value)


def transport(link_dir, shifted):
    highest = lax.Precision.HIGHEST
    real_v = shifted[..., 0, :, :].astype(jnp.float32)
    imag_v = shifted[..., 1, :, :].astype(jnp.float32)
    real_u = link_dir[..., 0, :, :]
    imag_u = link_dir[..., 1, :, :]

    def apply_link(matrix, vector):
        return jnp.einsum("...ab,...bn->...an", matrix, vector, precision=highest)

    moved_re = apply_link(real_u, real_v) - apply_link(imag_u, imag_v)
    moved_im = apply_link(real_u, imag_v) + apply_link(imag_u, real_v)
    moved = jnp.stack([moved_re, moved_im], axis=-3).astype(jnp.bfloat16)
    turned = jnp.stack([moved_im, -moved_re], axis=-3).astype(jnp.bfloat16)
    return (moved, turned)


def correlation(vec_part, moved, turned):
    width = vec_part.shape[-1]
    left_side = vec_part.reshape(-1, width)
    right_side = jnp.concatenate([moved.reshape(-1, width), turned.reshape(-1, width)], axis=1)
    product = lax.dot_general(
        left_side, right_side, (((0,), (0,)), ((), ())), preferred_element_type=jnp.float32
    )
    return jnp.stack([product[:, :width], product[:, width:]])


def complex_product(left_mat, right_mat):
    row_count = left_mat.shape[1]
    stacked = left_mat.reshape(2 * row_count, left_mat.shape[2])
    first_half = jnp.dot(stacked, right_mat[0], preferred_element_type=jnp.float32)
    second_half = jnp.dot(stacked, right_mat[1], preferred_element_type=jnp.float32)
    return jnp.stack(
        [
            first_half[:row_count] - second_half[row_count:],
            second_half[:row_count] + first_half[row_count:],
        ]
    )


def spin_block(elem, spin):
    highest = lax.Precision.HIGHEST
    expanded = jnp.einsum("cij,st->cisjt", elem, spin, precision=highest)
    return expanded.reshape(2, 4 * elem.shape[1], 4 * elem.shape[2]).astype(jnp.bfloat16)


def on_device(eigvecs, links, directions, spin_mats, forward_peram, backward_peram, chain_order):
    face_one = passed_along(lax.slice_in_dim(eigvecs, 0, 1, axis=0), "gx", -1)
    face_two = passed_along(lax.slice_in_dim(eigvecs, 0, 1, axis=1), "gy", -1)
    face_three = passed_along(lax.slice_in_dim(eigvecs, 0, 1, axis=2), "gz", -1)
    shifted = [
        jnp.concatenate([eigvecs[1:], face_one], axis=0),
        jnp.concatenate([eigvecs[:, 1:], face_two], axis=1),
        jnp.concatenate([eigvecs[:, :, 1:], face_three], axis=2),
    ]
    terms = []
    for direction in range(3):
        moved, turned = transport(links[:, :, :, direction], shifted[direction])
        terms.append(correlation(eigvecs, moved, turned))
    partial_dirs = jnp.stack(terms)
    num_vecs = eigvecs.shape[-1]
    nx, ny, nz = lax.axis_size("gx"), lax.axis_size("gy"), lax.axis_size("gz")
    volume = eigvecs.shape[0] * eigvecs.shape[1] * eigvecs.shape[2] * nx * ny * nz

    full_shape = partial_dirs.shape
    lanes = 128
    rows = partial_dirs.size // lanes
    chunk = partial_dirs.reshape(nz, rows // nz, lanes)
    chunk = exchange(chunk, "gz", True, 0).sum(axis=0)
    chunk = chunk.reshape(ny, rows // (nz * ny), lanes)
    chunk = exchange(chunk, "gy", True, 1).sum(axis=0)
    chunk = exchange(chunk, "gx", False, 2).sum(axis=0)
    chunk = exchange(chunk, "gy", False, 3).reshape(rows // nz, lanes)
    summed = exchange(chunk, "gz", False, 4).reshape(full_shape)
    elem_dirs = summed * (1.0 / math.sqrt(12.0 * volume))

    row_tile = num_vecs // nx
    col_tile = num_vecs // ny
    row_start = lax.axis_index("gx") * row_tile
    col_start = lax.axis_index("gy") * col_tile
    inverse = 1.0 / math.sqrt(4 * num_vecs)

    tile = forward_peram.shape[1]
    forward_rows = exchange(forward_peram, "gy", False, 5)
    forward_rows = jnp.transpose(forward_rows, (1, 2, 0, 3)).reshape(2, tile, ny * tile)
    backward_cols = exchange(backward_peram, "gx", False, 6)
    backward_cols = jnp.transpose(backward_cols, (1, 0, 2, 3)).reshape(2, nx * tile, tile)

    op_count = chain_order.shape[0]
    firsts = []
    lefts = []
    for op_index in range(op_count):
        left_k = chain_order[op_index, 0]
        right_k = chain_order[op_index, 1]
        left_dir = lax.dynamic_index_in_dim(elem_dirs, directions[left_k], 0, keepdims=False)
        right_dir = lax.dynamic_index_in_dim(elem_dirs, directions[right_k], 0, keepdims=False)
        left_spin = lax.dynamic_index_in_dim(spin_mats, left_k, 0, keepdims=False)
        right_spin = lax.dynamic_index_in_dim(spin_mats, right_k, 0, keepdims=False)
        left_rows = lax.dynamic_slice_in_dim(left_dir, row_start, row_tile, axis=1)
        right_cols = lax.dynamic_slice_in_dim(right_dir, col_start, col_tile, axis=2)
        lefts.append(spin_block(left_rows, left_spin))
        right_elem = spin_block(right_cols, right_spin)
        firsts.append(complex_product(forward_rows, right_elem).astype(jnp.bfloat16))
    first_cols = exchange(jnp.stack(firsts), "gx", False, 7)
    first_cols = jnp.transpose(first_cols, (1, 2, 0, 3, 4)).reshape(op_count, 2, nx * tile, tile)
    seconds = []
    for op_index in range(op_count):
        second = complex_product(lefts[op_index], first_cols[op_index])
        seconds.append((second * inverse).astype(jnp.bfloat16))
    second_rows = exchange(jnp.stack(seconds), "gy", False, 8)
    second_rows = jnp.transpose(second_rows, (1, 2, 3, 0, 4)).reshape(op_count, 2, tile, ny * tile)
    results = []
    for op_index in range(op_count):
        final = complex_product(second_rows[op_index], backward_cols)
        results.append(final.astype(jnp.bfloat16))
    return jnp.stack(results)


def solution(mesh):
    in_specs = (
        P("gx", "gy", "gz", None, None, None),
        P("gx", "gy", "gz", None, None, None, None),
        P(),
        P(),
        P(None, "gx", "gy"),
        P(None, "gx", "gy"),
        P("gz", None),
    )
    out_specs = P("gz", None, "gx", "gy")
    return jax.shard_map(
        on_device, mesh=mesh, in_specs=in_specs, out_specs=out_specs, check_vma=False
    )
```

```python
import functools
import math

import jax
import jax.numpy as jnp
from jax import lax
from jax.experimental import pallas as pl
from jax.experimental.pallas import tpu as pltpu
from jax.sharding import PartitionSpec as P

MESH_ID = pl.DeviceIdType.MESH


def passed_along(value, axis, steps):
    count = lax.axis_size(axis)
    pairs = [(source, (source + steps) % count) for source in range(count)]
    return lax.ppermute(value, axis, pairs)


def job_peer(axes, sizes, linear):
    coords = {}
    for axis, size in zip(reversed(axes), reversed(sizes)):
        coords[axis] = lax.rem(linear, size)
        linear = linear // size
    return coords


def exchange_kernel(jobs, *refs):
    count = len(jobs)
    in_refs = refs[:count]
    out_refs = refs[count : 2 * count]
    send_sems = refs[2 * count : 3 * count]
    recv_sems = refs[3 * count :]
    barrier = pltpu.get_barrier_semaphore()
    places = []
    expected = 0
    for axes, sizes, _ in jobs:
        n = math.prod(sizes)
        me = 0
        for axis, size in zip(axes, sizes):
            me = me * size + lax.axis_index(axis)
        places.append((n, me))
        for step in range(1, n):
            peer = job_peer(axes, sizes, lax.rem(me + step, n))
            pl.semaphore_signal(barrier, inc=1, device_id=peer, device_id_type=MESH_ID)
        expected += n - 1
    pl.semaphore_wait(barrier, expected)
    waits = []
    for job, (axes, sizes, scatter) in enumerate(jobs):
        n, me = places[job]
        x_ref, o_ref = in_refs[job], out_refs[job]
        own = x_ref.at[me] if scatter else x_ref
        local = pltpu.make_async_copy(own, o_ref.at[me], send_sems[job].at[0])
        local.start()
        waits.append(local)
        for step in range(1, n):
            linear = lax.rem(me + step, n)
            source = x_ref.at[linear] if scatter else x_ref
            copy = pltpu.make_async_remote_copy(
                src_ref=source,
                dst_ref=o_ref.at[me],
                send_sem=send_sems[job].at[step],
                recv_sem=recv_sems[job].at[step],
                device_id=job_peer(axes, sizes, linear),
                device_id_type=MESH_ID,
            )
            copy.start()
            waits.append(copy)
    for copy in waits:
        copy.wait()


def exchange(jobs, collective_id):
    specs = []
    values = []
    out_shapes = []
    sems = []
    for value, axes, scatter in jobs:
        sizes = tuple(lax.axis_size(axis) for axis in axes)
        n = math.prod(sizes)
        specs.append((tuple(axes), sizes, scatter))
        values.append(value)
        shape = value.shape if scatter else (n,) + value.shape
        out_shapes.append(jax.ShapeDtypeStruct(shape, value.dtype))
        sems.append(pltpu.SemaphoreType.DMA((n,)))
    vmem = pl.BlockSpec(memory_space=pltpu.VMEM)
    return pl.pallas_call(
        functools.partial(exchange_kernel, tuple(specs)),
        out_shape=tuple(out_shapes),
        in_specs=[vmem] * len(jobs),
        out_specs=tuple([vmem] * len(jobs)),
        scratch_shapes=sems + sems,
        compiler_params=pltpu.CompilerParams(collective_id=collective_id, has_side_effects=True),
    )(*values)


def transport(link_dir, shifted):
    highest = lax.Precision.HIGHEST
    real_v = shifted[..., 0, :, :].astype(jnp.float32)
    imag_v = shifted[..., 1, :, :].astype(jnp.float32)
    real_u = link_dir[..., 0, :, :]
    imag_u = link_dir[..., 1, :, :]

    def apply_link(matrix, vector):
        return jnp.einsum("...ab,...bn->...an", matrix, vector, precision=highest)

    moved_re = apply_link(real_u, real_v) - apply_link(imag_u, imag_v)
    moved_im = apply_link(real_u, imag_v) + apply_link(imag_u, real_v)
    moved = jnp.stack([moved_re, moved_im], axis=-3).astype(jnp.bfloat16)
    turned = jnp.stack([moved_im, -moved_re], axis=-3).astype(jnp.bfloat16)
    return (moved, turned)


def correlation(vec_part, moved, turned):
    width = vec_part.shape[-1]
    left_side = vec_part.reshape(-1, width)
    right_side = jnp.concatenate([moved.reshape(-1, width), turned.reshape(-1, width)], axis=1)
    product = lax.dot_general(
        left_side, right_side, (((0,), (0,)), ((), ())), preferred_element_type=jnp.float32
    )
    return jnp.stack([product[:, :width], product[:, width:]])


def complex_product(left_mat, right_mat):
    row_count = left_mat.shape[1]
    stacked = left_mat.reshape(2 * row_count, left_mat.shape[2])
    first_half = jnp.dot(stacked, right_mat[0], preferred_element_type=jnp.float32)
    second_half = jnp.dot(stacked, right_mat[1], preferred_element_type=jnp.float32)
    return jnp.stack(
        [
            first_half[:row_count] - second_half[row_count:],
            second_half[:row_count] + first_half[row_count:],
        ]
    )


def spin_block(elem, spin):
    highest = lax.Precision.HIGHEST
    rows, cols = elem.shape[1], elem.shape[2]
    big_rows = lax.broadcasted_iota(jnp.int32, (4 * rows, rows), 0)
    row_expand = (big_rows // 4 == lax.broadcasted_iota(jnp.int32, (4 * rows, rows), 1)).astype(jnp.float32)
    big_cols = lax.broadcasted_iota(jnp.int32, (cols, 4 * cols), 1)
    col_expand = (big_cols // 4 == lax.broadcasted_iota(jnp.int32, (cols, 4 * cols), 0)).astype(jnp.float32)
    spin_rows = (
        lax.broadcasted_iota(jnp.int32, (4 * rows, 4), 0) % 4
        == lax.broadcasted_iota(jnp.int32, (4 * rows, 4), 1)
    ).astype(jnp.float32)
    spin_cols = (
        lax.broadcasted_iota(jnp.int32, (4, 4 * cols), 1) % 4
        == lax.broadcasted_iota(jnp.int32, (4, 4 * cols), 0)
    ).astype(jnp.float32)
    repeated = jnp.einsum("ar,crq->caq", row_expand, elem, precision=highest)
    repeated = jnp.einsum("caq,qb->cab", repeated, col_expand, precision=highest)
    tiled = jnp.dot(jnp.dot(spin_rows, spin, precision=highest), spin_cols, precision=highest)
    return (repeated * tiled[None]).astype(jnp.bfloat16)


def on_device(eigvecs, links, directions, spin_mats, forward_peram, backward_peram, chain_order):
    face_one = passed_along(lax.slice_in_dim(eigvecs, 0, 1, axis=0), "gx", -1)
    face_two = passed_along(lax.slice_in_dim(eigvecs, 0, 1, axis=1), "gy", -1)
    face_three = passed_along(lax.slice_in_dim(eigvecs, 0, 1, axis=2), "gz", -1)
    shifted = [
        jnp.concatenate([eigvecs[1:], face_one], axis=0),
        jnp.concatenate([eigvecs[:, 1:], face_two], axis=1),
        jnp.concatenate([eigvecs[:, :, 1:], face_three], axis=2),
    ]
    terms = []
    for direction in range(3):
        moved, turned = transport(links[:, :, :, direction], shifted[direction])
        terms.append(correlation(eigvecs, moved, turned))
    partial_dirs = jnp.stack(terms)
    num_vecs = eigvecs.shape[-1]
    nx, ny, nz = lax.axis_size("gx"), lax.axis_size("gy"), lax.axis_size("gz")
    volume = eigvecs.shape[0] * eigvecs.shape[1] * eigvecs.shape[2] * nx * ny * nz

    full_shape = partial_dirs.shape
    lanes = 128
    rows = partial_dirs.size // lanes
    plane = ("gx", "gy")
    chunk = partial_dirs.reshape(nz, rows // nz, lanes)
    tile = forward_peram.shape[1]
    chunk, forward_rows, backward_cols = exchange(
        [(chunk, ("gz",), True), (forward_peram, ("gy",), False), (backward_peram, ("gx",), False)], 0
    )
    chunk = chunk.sum(axis=0).reshape(nx * ny, rows // (nz * nx * ny), lanes)
    (chunk,) = exchange([(chunk, plane, True)], 1)
    (chunk,) = exchange([(chunk.sum(axis=0), plane, False)], 2)
    (summed,) = exchange([(chunk.reshape(rows // nz, lanes), ("gz",), False)], 3)
    elem_dirs = summed.reshape(full_shape) * (1.0 / math.sqrt(12.0 * volume))

    row_tile = num_vecs // nx
    col_tile = num_vecs // ny
    row_start = lax.axis_index("gx") * row_tile
    col_start = lax.axis_index("gy") * col_tile
    inverse = 1.0 / math.sqrt(4 * num_vecs)

    forward_rows = jnp.transpose(forward_rows, (1, 2, 0, 3)).reshape(2, tile, ny * tile)
    backward_cols = jnp.transpose(backward_cols, (1, 0, 2, 3)).reshape(2, nx * tile, tile)

    op_count = chain_order.shape[0]
    firsts = []
    lefts = []
    for op_index in range(op_count):
        left_k = chain_order[op_index, 0]
        right_k = chain_order[op_index, 1]
        left_dir = lax.dynamic_index_in_dim(elem_dirs, directions[left_k], 0, keepdims=False)
        right_dir = lax.dynamic_index_in_dim(elem_dirs, directions[right_k], 0, keepdims=False)
        left_spin = lax.dynamic_index_in_dim(spin_mats, left_k, 0, keepdims=False)
        right_spin = lax.dynamic_index_in_dim(spin_mats, right_k, 0, keepdims=False)
        left_rows = lax.dynamic_slice_in_dim(left_dir, row_start, row_tile, axis=1)
        right_cols = lax.dynamic_slice_in_dim(right_dir, col_start, col_tile, axis=2)
        lefts.append(spin_block(left_rows, left_spin))
        right_elem = spin_block(right_cols, right_spin)
        firsts.append(complex_product(forward_rows, right_elem).astype(jnp.bfloat16))
    (first_cols,) = exchange([(jnp.stack(firsts), ("gx",), False)], 4)
    first_cols = jnp.transpose(first_cols, (1, 2, 0, 3, 4)).reshape(op_count, 2, nx * tile, tile)
    seconds = []
    for op_index in range(op_count):
        second = complex_product(lefts[op_index], first_cols[op_index])
        seconds.append((second * inverse).astype(jnp.bfloat16))
    (second_rows,) = exchange([(jnp.stack(seconds), ("gy",), False)], 5)
    second_rows = jnp.transpose(second_rows, (1, 2, 3, 0, 4)).reshape(op_count, 2, tile, ny * tile)
    results = []
    for op_index in range(op_count):
        final = complex_product(second_rows[op_index], backward_cols)
        results.append(final.astype(jnp.bfloat16))
    return jnp.stack(results)


def solution(mesh):
    in_specs = (
        P("gx", "gy", "gz", None, None, None),
        P("gx", "gy", "gz", None, None, None, None),
        P(),
        P(),
        P(None, "gx", "gy"),
        P(None, "gx", "gy"),
        P("gz", None),
    )
    out_specs = P("gz", None, "gx", "gy")
    return jax.shard_map(
        on_device, mesh=mesh, in_specs=in_specs, out_specs=out_specs, check_vma=False
    )
```

```python
import functools
import math

import jax
import jax.numpy as jnp
from jax import lax
from jax.experimental import pallas as pl
from jax.experimental.pallas import tpu as pltpu
from jax.sharding import PartitionSpec as P

MESH_ID = pl.DeviceIdType.MESH


def passed_along(value, axis, steps):
    count = lax.axis_size(axis)
    pairs = [(source, (source + steps) % count) for source in range(count)]
    return lax.ppermute(value, axis, pairs)


def job_peer(axes, sizes, linear):
    coords = {}
    for axis, size in zip(reversed(axes), reversed(sizes)):
        coords[axis] = lax.rem(linear, size)
        linear = linear // size
    return coords


def exchange_kernel(jobs, *refs):
    count = len(jobs)
    in_refs = refs[:count]
    out_refs = refs[count : 2 * count]
    send_sems = refs[2 * count : 3 * count]
    recv_sems = refs[3 * count :]
    barrier = pltpu.get_barrier_semaphore()
    places = []
    expected = 0
    for axes, sizes, _ in jobs:
        n = math.prod(sizes)
        me = 0
        for axis, size in zip(axes, sizes):
            me = me * size + lax.axis_index(axis)
        places.append((n, me))
        for step in range(1, n):
            peer = job_peer(axes, sizes, lax.rem(me + step, n))
            pl.semaphore_signal(barrier, inc=1, device_id=peer, device_id_type=MESH_ID)
        expected += n - 1
    pl.semaphore_wait(barrier, expected)
    waits = []
    for job, (axes, sizes, scatter) in enumerate(jobs):
        n, me = places[job]
        x_ref, o_ref = in_refs[job], out_refs[job]
        own = x_ref.at[me] if scatter else x_ref
        local = pltpu.make_async_copy(own, o_ref.at[me], send_sems[job].at[0])
        local.start()
        waits.append(local)
        for step in range(1, n):
            linear = lax.rem(me + step, n)
            source = x_ref.at[linear] if scatter else x_ref
            copy = pltpu.make_async_remote_copy(
                src_ref=source,
                dst_ref=o_ref.at[me],
                send_sem=send_sems[job].at[step],
                recv_sem=recv_sems[job].at[step],
                device_id=job_peer(axes, sizes, linear),
                device_id_type=MESH_ID,
            )
            copy.start()
            waits.append(copy)
    for copy in waits:
        copy.wait()


def exchange(jobs, collective_id):
    specs = []
    values = []
    out_shapes = []
    sems = []
    for value, axes, scatter in jobs:
        sizes = tuple(lax.axis_size(axis) for axis in axes)
        n = math.prod(sizes)
        specs.append((tuple(axes), sizes, scatter))
        values.append(value)
        shape = value.shape if scatter else (n,) + value.shape
        out_shapes.append(jax.ShapeDtypeStruct(shape, value.dtype))
        sems.append(pltpu.SemaphoreType.DMA((n,)))
    vmem = pl.BlockSpec(memory_space=pltpu.VMEM)
    return pl.pallas_call(
        functools.partial(exchange_kernel, tuple(specs)),
        out_shape=tuple(out_shapes),
        in_specs=[vmem] * len(jobs),
        out_specs=tuple([vmem] * len(jobs)),
        scratch_shapes=sems + sems,
        compiler_params=pltpu.CompilerParams(collective_id=collective_id, has_side_effects=True),
    )(*values)


def reduce_kernel(sizes, part_ref, fwd_ref, bwd_ref, out_ref, fwd_out, bwd_out,
                  first_buf, first_sum, second_buf, third_buf, sems):
    nx, ny, nz = sizes
    plane = ("gx", "gy")
    plane_sizes = (nx, ny)
    n_plane = nx * ny
    me_x = lax.axis_index("gx")
    me_y = lax.axis_index("gy")
    me_z = lax.axis_index("gz")
    me_p = me_x * ny + me_y
    barrier = pltpu.get_barrier_semaphore()
    for step in range(1, nz):
        peer = {"gz": lax.rem(me_z + step, nz)}
        pl.semaphore_signal(barrier, inc=1, device_id=peer, device_id_type=MESH_ID)
    for step in range(1, n_plane):
        peer = job_peer(plane, plane_sizes, lax.rem(me_p + step, n_plane))
        pl.semaphore_signal(barrier, inc=1, device_id=peer, device_id_type=MESH_ID)
    pl.semaphore_wait(barrier, nz - 1 + n_plane - 1)

    def send_all(axes, axis_sizes, me, src_of, dst_of, slot):
        n = math.prod(axis_sizes)
        copies = []
        local = pltpu.make_async_copy(src_of(me), dst_of(me), sems.at[slot, 0, 0])
        local.start()
        copies.append(local)
        for step in range(1, n):
            linear = lax.rem(me + step, n)
            copy = pltpu.make_async_remote_copy(
                src_ref=src_of(linear),
                dst_ref=dst_of(me),
                send_sem=sems.at[slot, 0, step],
                recv_sem=sems.at[slot, 1, step],
                device_id=job_peer(axes, axis_sizes, linear),
                device_id_type=MESH_ID,
            )
            copy.start()
            copies.append(copy)
        return copies

    gathers = send_all(("gy",), (ny,), me_y, lambda k: fwd_ref, lambda k: fwd_out.at[k], 4)
    gathers += send_all(("gx",), (nx,), me_x, lambda k: bwd_ref, lambda k: bwd_out.at[k], 5)
    stage = send_all(("gz",), (nz,), me_z, lambda k: part_ref.at[k], lambda k: first_buf.at[k], 0)
    for copy in stage:
        copy.wait()
    first_sum[...] = jnp.sum(first_buf[...], axis=0)
    stage = send_all(plane, plane_sizes, me_p, lambda k: first_sum.at[k], lambda k: second_buf.at[k], 1)
    for copy in stage:
        copy.wait()
    first_sum[0] = jnp.sum(second_buf[...], axis=0)
    stage = send_all(plane, plane_sizes, me_p, lambda k: first_sum.at[0], lambda k: third_buf.at[k], 2)
    for copy in stage:
        copy.wait()
    stage = send_all(("gz",), (nz,), me_z, lambda k: third_buf, lambda k: out_ref.at[k], 3)
    for copy in stage:
        copy.wait()
    for copy in gathers:
        copy.wait()


def reduce_everywhere(parts, forward_peram, backward_peram):
    nx, ny, nz = lax.axis_size("gx"), lax.axis_size("gy"), lax.axis_size("gz")
    widest = max(nx * ny, nz)
    piece = parts.shape[1:]
    vmem = pl.BlockSpec(memory_space=pltpu.VMEM)
    return pl.pallas_call(
        functools.partial(reduce_kernel, (nx, ny, nz)),
        out_shape=(
            jax.ShapeDtypeStruct(parts.shape, parts.dtype),
            jax.ShapeDtypeStruct((ny,) + forward_peram.shape, forward_peram.dtype),
            jax.ShapeDtypeStruct((nx,) + backward_peram.shape, backward_peram.dtype),
        ),
        in_specs=[vmem] * 3,
        out_specs=(vmem, vmem, vmem),
        scratch_shapes=[
            pltpu.VMEM(parts.shape, parts.dtype),
            pltpu.VMEM(piece, parts.dtype),
            pltpu.VMEM(piece, parts.dtype),
            pltpu.VMEM(piece, parts.dtype),
            pltpu.SemaphoreType.DMA((6, 2, widest)),
        ],
        compiler_params=pltpu.CompilerParams(collective_id=0, has_side_effects=True),
    )(parts, forward_peram, backward_peram)


def transport(link_dir, shifted):
    highest = lax.Precision.HIGHEST
    real_v = shifted[..., 0, :, :].astype(jnp.float32)
    imag_v = shifted[..., 1, :, :].astype(jnp.float32)
    real_u = link_dir[..., 0, :, :]
    imag_u = link_dir[..., 1, :, :]

    def apply_link(matrix, vector):
        return jnp.einsum("...ab,...bn->...an", matrix, vector, precision=highest)

    moved_re = apply_link(real_u, real_v) - apply_link(imag_u, imag_v)
    moved_im = apply_link(real_u, imag_v) + apply_link(imag_u, real_v)
    moved = jnp.stack([moved_re, moved_im], axis=-3).astype(jnp.bfloat16)
    turned = jnp.stack([moved_im, -moved_re], axis=-3).astype(jnp.bfloat16)
    return (moved, turned)


def correlation(vec_part, moved, turned):
    width = vec_part.shape[-1]
    left_side = vec_part.reshape(-1, width)
    right_side = jnp.concatenate([moved.reshape(-1, width), turned.reshape(-1, width)], axis=1)
    product = lax.dot_general(
        left_side, right_side, (((0,), (0,)), ((), ())), preferred_element_type=jnp.float32
    )
    return jnp.stack([product[:, :width], product[:, width:]])


def complex_product(left_mat, right_mat):
    row_count = left_mat.shape[1]
    stacked = left_mat.reshape(2 * row_count, left_mat.shape[2])
    first_half = jnp.dot(stacked, right_mat[0], preferred_element_type=jnp.float32)
    second_half = jnp.dot(stacked, right_mat[1], preferred_element_type=jnp.float32)
    return jnp.stack(
        [
            first_half[:row_count] - second_half[row_count:],
            second_half[:row_count] + first_half[row_count:],
        ]
    )


def spin_block(elem, spin):
    highest = lax.Precision.HIGHEST
    rows, cols = elem.shape[1], elem.shape[2]
    big_rows = lax.broadcasted_iota(jnp.int32, (4 * rows, rows), 0)
    row_expand = (big_rows // 4 == lax.broadcasted_iota(jnp.int32, (4 * rows, rows), 1)).astype(jnp.float32)
    big_cols = lax.broadcasted_iota(jnp.int32, (cols, 4 * cols), 1)
    col_expand = (big_cols // 4 == lax.broadcasted_iota(jnp.int32, (cols, 4 * cols), 0)).astype(jnp.float32)
    spin_rows = (
        lax.broadcasted_iota(jnp.int32, (4 * rows, 4), 0) % 4
        == lax.broadcasted_iota(jnp.int32, (4 * rows, 4), 1)
    ).astype(jnp.float32)
    spin_cols = (
        lax.broadcasted_iota(jnp.int32, (4, 4 * cols), 1) % 4
        == lax.broadcasted_iota(jnp.int32, (4, 4 * cols), 0)
    ).astype(jnp.float32)
    repeated = jnp.einsum("ar,crq->caq", row_expand, elem, precision=highest)
    repeated = jnp.einsum("caq,qb->cab", repeated, col_expand, precision=highest)
    tiled = jnp.dot(jnp.dot(spin_rows, spin, precision=highest), spin_cols, precision=highest)
    return (repeated * tiled[None]).astype(jnp.bfloat16)


def on_device(eigvecs, links, directions, spin_mats, forward_peram, backward_peram, chain_order):
    face_one = passed_along(lax.slice_in_dim(eigvecs, 0, 1, axis=0), "gx", -1)
    face_two = passed_along(lax.slice_in_dim(eigvecs, 0, 1, axis=1), "gy", -1)
    face_three = passed_along(lax.slice_in_dim(eigvecs, 0, 1, axis=2), "gz", -1)
    shifted = [
        jnp.concatenate([eigvecs[1:], face_one], axis=0),
        jnp.concatenate([eigvecs[:, 1:], face_two], axis=1),
        jnp.concatenate([eigvecs[:, :, 1:], face_three], axis=2),
    ]
    terms = []
    for direction in range(3):
        moved, turned = transport(links[:, :, :, direction], shifted[direction])
        terms.append(correlation(eigvecs, moved, turned))
    partial_dirs = jnp.stack(terms)
    num_vecs = eigvecs.shape[-1]
    nx, ny, nz = lax.axis_size("gx"), lax.axis_size("gy"), lax.axis_size("gz")
    volume = eigvecs.shape[0] * eigvecs.shape[1] * eigvecs.shape[2] * nx * ny * nz

    full_shape = partial_dirs.shape
    lanes = 128
    rows = partial_dirs.size // lanes
    parts = partial_dirs.reshape(nz, nx * ny, rows // (nz * nx * ny), lanes)
    tile = forward_peram.shape[1]
    summed, forward_rows, backward_cols = reduce_everywhere(parts, forward_peram, backward_peram)
    elem_dirs = summed.reshape(full_shape) * (1.0 / math.sqrt(12.0 * volume))

    row_tile = num_vecs // nx
    col_tile = num_vecs // ny
    row_start = lax.axis_index("gx") * row_tile
    col_start = lax.axis_index("gy") * col_tile
    inverse = 1.0 / math.sqrt(4 * num_vecs)

    forward_rows = jnp.transpose(forward_rows, (1, 2, 0, 3)).reshape(2, tile, ny * tile)
    backward_cols = jnp.transpose(backward_cols, (1, 0, 2, 3)).reshape(2, nx * tile, tile)

    op_count = chain_order.shape[0]
    firsts = []
    lefts = []
    for op_index in range(op_count):
        left_k = chain_order[op_index, 0]
        right_k = chain_order[op_index, 1]
        left_dir = lax.dynamic_index_in_dim(elem_dirs, directions[left_k], 0, keepdims=False)
        right_dir = lax.dynamic_index_in_dim(elem_dirs, directions[right_k], 0, keepdims=False)
        left_spin = lax.dynamic_index_in_dim(spin_mats, left_k, 0, keepdims=False)
        right_spin = lax.dynamic_index_in_dim(spin_mats, right_k, 0, keepdims=False)
        left_rows = lax.dynamic_slice_in_dim(left_dir, row_start, row_tile, axis=1)
        right_cols = lax.dynamic_slice_in_dim(right_dir, col_start, col_tile, axis=2)
        lefts.append(spin_block(left_rows, left_spin))
        right_elem = spin_block(right_cols, right_spin)
        firsts.append(complex_product(forward_rows, right_elem).astype(jnp.bfloat16))
    (first_cols,) = exchange([(jnp.stack(firsts), ("gx",), False)], 1)
    first_cols = jnp.transpose(first_cols, (1, 2, 0, 3, 4)).reshape(op_count, 2, nx * tile, tile)
    seconds = []
    for op_index in range(op_count):
        second = complex_product(lefts[op_index], first_cols[op_index])
        seconds.append((second * inverse).astype(jnp.bfloat16))
    (second_rows,) = exchange([(jnp.stack(seconds), ("gy",), False)], 2)
    second_rows = jnp.transpose(second_rows, (1, 2, 3, 0, 4)).reshape(op_count, 2, tile, ny * tile)
    results = []
    for op_index in range(op_count):
        final = complex_product(second_rows[op_index], backward_cols)
        results.append(final.astype(jnp.bfloat16))
    return jnp.stack(results)


def solution(mesh):
    in_specs = (
        P("gx", "gy", "gz", None, None, None),
        P("gx", "gy", "gz", None, None, None, None),
        P(),
        P(),
        P(None, "gx", "gy"),
        P(None, "gx", "gy"),
        P("gz", None),
    )
    out_specs = P("gz", None, "gx", "gy")
    return jax.shard_map(
        on_device, mesh=mesh, in_specs=in_specs, out_specs=out_specs, check_vma=False
    )
```

```python
import functools
import math

import jax
import jax.numpy as jnp
from jax import lax
from jax.experimental import pallas as pl
from jax.experimental.pallas import tpu as pltpu
from jax.sharding import PartitionSpec as P

MESH_ID = pl.DeviceIdType.MESH


def job_peer(axes, sizes, linear):
    coords = {}
    for axis, size in zip(reversed(axes), reversed(sizes)):
        coords[axis] = lax.rem(linear, size)
        linear = linear // size
    return coords


def exchange_kernel(jobs, *refs):
    count = len(jobs)
    in_refs = refs[:count]
    out_refs = refs[count : 2 * count]
    send_sems = refs[2 * count : 3 * count]
    recv_sems = refs[3 * count :]
    barrier = pltpu.get_barrier_semaphore()
    places = []
    expected = 0
    for axes, sizes, _ in jobs:
        n = math.prod(sizes)
        me = 0
        for axis, size in zip(axes, sizes):
            me = me * size + lax.axis_index(axis)
        places.append((n, me))
        for step in range(1, n):
            peer = job_peer(axes, sizes, lax.rem(me + step, n))
            pl.semaphore_signal(barrier, inc=1, device_id=peer, device_id_type=MESH_ID)
        expected += n - 1
    pl.semaphore_wait(barrier, expected)
    waits = []
    for job, (axes, sizes, scatter) in enumerate(jobs):
        n, me = places[job]
        x_ref, o_ref = in_refs[job], out_refs[job]
        own = x_ref.at[me] if scatter else x_ref
        local = pltpu.make_async_copy(own, o_ref.at[me], send_sems[job].at[0])
        local.start()
        waits.append(local)
        for step in range(1, n):
            linear = lax.rem(me + step, n)
            source = x_ref.at[linear] if scatter else x_ref
            copy = pltpu.make_async_remote_copy(
                src_ref=source,
                dst_ref=o_ref.at[me],
                send_sem=send_sems[job].at[step],
                recv_sem=recv_sems[job].at[step],
                device_id=job_peer(axes, sizes, linear),
                device_id_type=MESH_ID,
            )
            copy.start()
            waits.append(copy)
    for copy in waits:
        copy.wait()


def exchange(jobs, collective_id):
    specs = []
    values = []
    out_shapes = []
    sems = []
    for value, axes, scatter in jobs:
        sizes = tuple(lax.axis_size(axis) for axis in axes)
        n = math.prod(sizes)
        specs.append((tuple(axes), sizes, scatter))
        values.append(value)
        shape = value.shape if scatter else (n,) + value.shape
        out_shapes.append(jax.ShapeDtypeStruct(shape, value.dtype))
        sems.append(pltpu.SemaphoreType.DMA((n,)))
    vmem = pl.BlockSpec(memory_space=pltpu.VMEM)
    return pl.pallas_call(
        functools.partial(exchange_kernel, tuple(specs)),
        out_shape=tuple(out_shapes),
        in_specs=[vmem] * len(jobs),
        out_specs=tuple([vmem] * len(jobs)),
        scratch_shapes=sems + sems,
        compiler_params=pltpu.CompilerParams(collective_id=collective_id, has_side_effects=True),
    )(*values)


def reduce_kernel(sizes, part_ref, fwd_ref, bwd_ref, out_ref, fwd_out, bwd_out,
                  first_buf, first_sum, second_buf, third_buf, sems):
    nx, ny, nz = sizes
    plane = ("gx", "gy")
    plane_sizes = (nx, ny)
    n_plane = nx * ny
    me_x = lax.axis_index("gx")
    me_y = lax.axis_index("gy")
    me_z = lax.axis_index("gz")
    me_p = me_x * ny + me_y
    barrier = pltpu.get_barrier_semaphore()
    for step in range(1, nz):
        peer = {"gz": lax.rem(me_z + step, nz)}
        pl.semaphore_signal(barrier, inc=1, device_id=peer, device_id_type=MESH_ID)
    for step in range(1, n_plane):
        peer = job_peer(plane, plane_sizes, lax.rem(me_p + step, n_plane))
        pl.semaphore_signal(barrier, inc=1, device_id=peer, device_id_type=MESH_ID)
    pl.semaphore_wait(barrier, nz - 1 + n_plane - 1)

    def send_all(axes, axis_sizes, me, src_of, dst_of, slot):
        n = math.prod(axis_sizes)
        copies = []
        local = pltpu.make_async_copy(src_of(me), dst_of(me), sems.at[slot, 0, 0])
        local.start()
        copies.append(local)
        for step in range(1, n):
            linear = lax.rem(me + step, n)
            copy = pltpu.make_async_remote_copy(
                src_ref=src_of(linear),
                dst_ref=dst_of(me),
                send_sem=sems.at[slot, 0, step],
                recv_sem=sems.at[slot, 1, step],
                device_id=job_peer(axes, axis_sizes, linear),
                device_id_type=MESH_ID,
            )
            copy.start()
            copies.append(copy)
        return copies

    gathers = send_all(("gy",), (ny,), me_y, lambda k: fwd_ref, lambda k: fwd_out.at[k], 4)
    gathers += send_all(("gx",), (nx,), me_x, lambda k: bwd_ref, lambda k: bwd_out.at[k], 5)
    stage = send_all(("gz",), (nz,), me_z, lambda k: part_ref.at[k], lambda k: first_buf.at[k], 0)
    for copy in stage:
        copy.wait()
    first_sum[...] = jnp.sum(first_buf[...], axis=0)
    stage = send_all(plane, plane_sizes, me_p, lambda k: first_sum.at[k], lambda k: second_buf.at[k], 1)
    for copy in stage:
        copy.wait()
    first_sum[0] = jnp.sum(second_buf[...], axis=0)
    stage = send_all(plane, plane_sizes, me_p, lambda k: first_sum.at[0], lambda k: third_buf.at[k], 2)
    for copy in stage:
        copy.wait()
    stage = send_all(("gz",), (nz,), me_z, lambda k: third_buf, lambda k: out_ref.at[k], 3)
    for copy in stage:
        copy.wait()
    for copy in gathers:
        copy.wait()


def reduce_everywhere(parts, forward_peram, backward_peram):
    nx, ny, nz = lax.axis_size("gx"), lax.axis_size("gy"), lax.axis_size("gz")
    widest = max(nx * ny, nz)
    piece = parts.shape[1:]
    vmem = pl.BlockSpec(memory_space=pltpu.VMEM)
    return pl.pallas_call(
        functools.partial(reduce_kernel, (nx, ny, nz)),
        out_shape=(
            jax.ShapeDtypeStruct(parts.shape, parts.dtype),
            jax.ShapeDtypeStruct((ny,) + forward_peram.shape, forward_peram.dtype),
            jax.ShapeDtypeStruct((nx,) + backward_peram.shape, backward_peram.dtype),
        ),
        in_specs=[vmem] * 3,
        out_specs=(vmem, vmem, vmem),
        scratch_shapes=[
            pltpu.VMEM(parts.shape, parts.dtype),
            pltpu.VMEM(piece, parts.dtype),
            pltpu.VMEM(piece, parts.dtype),
            pltpu.VMEM(piece, parts.dtype),
            pltpu.SemaphoreType.DMA((6, 2, widest)),
        ],
        compiler_params=pltpu.CompilerParams(collective_id=0, has_side_effects=True),
    )(parts, forward_peram, backward_peram)


def halo_kernel(sizes, one_ref, two_ref, three_ref, one_out, two_out, three_out, send_sem, recv_sem):
    axes = ("gx", "gy", "gz")
    barrier = pltpu.get_barrier_semaphore()
    for axis, n in zip(axes, sizes):
        me = lax.axis_index(axis)
        for peer in (lax.rem(me + n - 1, n), lax.rem(me + 1, n)):
            pl.semaphore_signal(barrier, inc=1, device_id={axis: peer}, device_id_type=MESH_ID)
    pl.semaphore_wait(barrier, 2 * len(axes))
    copies = []
    for slot, (axis, n, src, dst) in enumerate(
        zip(axes, sizes, (one_ref, two_ref, three_ref), (one_out, two_out, three_out))
    ):
        me = lax.axis_index(axis)
        copy = pltpu.make_async_remote_copy(
            src_ref=src,
            dst_ref=dst,
            send_sem=send_sem.at[slot],
            recv_sem=recv_sem.at[slot],
            device_id={axis: lax.rem(me + n - 1, n)},
            device_id_type=MESH_ID,
        )
        copy.start()
        copies.append(copy)
    for copy in copies:
        copy.wait()


def halo_exchange(faces):
    sizes = tuple(lax.axis_size(axis) for axis in ("gx", "gy", "gz"))
    flat = [face.reshape(-1, face.shape[-1]) for face in faces]
    vmem = pl.BlockSpec(memory_space=pltpu.VMEM)
    got = pl.pallas_call(
        functools.partial(halo_kernel, sizes),
        out_shape=tuple(jax.ShapeDtypeStruct(face.shape, face.dtype) for face in flat),
        in_specs=[vmem] * 3,
        out_specs=(vmem, vmem, vmem),
        scratch_shapes=[pltpu.SemaphoreType.DMA((3,)), pltpu.SemaphoreType.DMA((3,))],
        compiler_params=pltpu.CompilerParams(collective_id=3, has_side_effects=True),
    )(*flat)
    return [value.reshape(face.shape) for value, face in zip(got, faces)]


def transport(link_dir, shifted):
    highest = lax.Precision.HIGHEST
    real_v = shifted[..., 0, :, :].astype(jnp.float32)
    imag_v = shifted[..., 1, :, :].astype(jnp.float32)
    real_u = link_dir[..., 0, :, :]
    imag_u = link_dir[..., 1, :, :]

    def apply_link(matrix, vector):
        return jnp.einsum("...ab,...bn->...an", matrix, vector, precision=highest)

    moved_re = apply_link(real_u, real_v) - apply_link(imag_u, imag_v)
    moved_im = apply_link(real_u, imag_v) + apply_link(imag_u, real_v)
    moved = jnp.stack([moved_re, moved_im], axis=-3).astype(jnp.bfloat16)
    turned = jnp.stack([moved_im, -moved_re], axis=-3).astype(jnp.bfloat16)
    return (moved, turned)


def correlation(vec_part, moved, turned):
    width = vec_part.shape[-1]
    left_side = vec_part.reshape(-1, width)
    right_side = jnp.concatenate([moved.reshape(-1, width), turned.reshape(-1, width)], axis=1)
    product = lax.dot_general(
        left_side, right_side, (((0,), (0,)), ((), ())), preferred_element_type=jnp.float32
    )
    return jnp.stack([product[:, :width], product[:, width:]])


def complex_product(left_mat, right_mat):
    row_count = left_mat.shape[1]
    stacked = left_mat.reshape(2 * row_count, left_mat.shape[2])
    first_half = jnp.dot(stacked, right_mat[0], preferred_element_type=jnp.float32)
    second_half = jnp.dot(stacked, right_mat[1], preferred_element_type=jnp.float32)
    return jnp.stack(
        [
            first_half[:row_count] - second_half[row_count:],
            second_half[:row_count] + first_half[row_count:],
        ]
    )


def spin_block(elem, spin):
    highest = lax.Precision.HIGHEST
    rows, cols = elem.shape[1], elem.shape[2]
    big_rows = lax.broadcasted_iota(jnp.int32, (4 * rows, rows), 0)
    row_expand = (big_rows // 4 == lax.broadcasted_iota(jnp.int32, (4 * rows, rows), 1)).astype(jnp.float32)
    big_cols = lax.broadcasted_iota(jnp.int32, (cols, 4 * cols), 1)
    col_expand = (big_cols // 4 == lax.broadcasted_iota(jnp.int32, (cols, 4 * cols), 0)).astype(jnp.float32)
    spin_rows = (
        lax.broadcasted_iota(jnp.int32, (4 * rows, 4), 0) % 4
        == lax.broadcasted_iota(jnp.int32, (4 * rows, 4), 1)
    ).astype(jnp.float32)
    spin_cols = (
        lax.broadcasted_iota(jnp.int32, (4, 4 * cols), 1) % 4
        == lax.broadcasted_iota(jnp.int32, (4, 4 * cols), 0)
    ).astype(jnp.float32)
    repeated = jnp.einsum("ar,crq->caq", row_expand, elem, precision=highest)
    repeated = jnp.einsum("caq,qb->cab", repeated, col_expand, precision=highest)
    tiled = jnp.dot(jnp.dot(spin_rows, spin, precision=highest), spin_cols, precision=highest)
    return (repeated * tiled[None]).astype(jnp.bfloat16)


def on_device(eigvecs, links, directions, spin_mats, forward_peram, backward_peram, chain_order):
    face_one, face_two, face_three = halo_exchange(
        [
            lax.slice_in_dim(eigvecs, 0, 1, axis=0),
            lax.slice_in_dim(eigvecs, 0, 1, axis=1),
            lax.slice_in_dim(eigvecs, 0, 1, axis=2),
        ]
    )
    shifted = [
        jnp.concatenate([eigvecs[1:], face_one], axis=0),
        jnp.concatenate([eigvecs[:, 1:], face_two], axis=1),
        jnp.concatenate([eigvecs[:, :, 1:], face_three], axis=2),
    ]
    terms = []
    for direction in range(3):
        moved, turned = transport(links[:, :, :, direction], shifted[direction])
        terms.append(correlation(eigvecs, moved, turned))
    partial_dirs = jnp.stack(terms)
    num_vecs = eigvecs.shape[-1]
    nx, ny, nz = lax.axis_size("gx"), lax.axis_size("gy"), lax.axis_size("gz")
    volume = eigvecs.shape[0] * eigvecs.shape[1] * eigvecs.shape[2] * nx * ny * nz

    full_shape = partial_dirs.shape
    lanes = 128
    rows = partial_dirs.size // lanes
    parts = partial_dirs.reshape(nz, nx * ny, rows // (nz * nx * ny), lanes)
    tile = forward_peram.shape[1]
    summed, forward_rows, backward_cols = reduce_everywhere(parts, forward_peram, backward_peram)
    elem_dirs = summed.reshape(full_shape) * (1.0 / math.sqrt(12.0 * volume))

    row_tile = num_vecs // nx
    col_tile = num_vecs // ny
    row_start = lax.axis_index("gx") * row_tile
    col_start = lax.axis_index("gy") * col_tile
    inverse = 1.0 / math.sqrt(4 * num_vecs)

    forward_rows = jnp.transpose(forward_rows, (1, 2, 0, 3)).reshape(2, tile, ny * tile)
    backward_cols = jnp.transpose(backward_cols, (1, 0, 2, 3)).reshape(2, nx * tile, tile)

    op_count = chain_order.shape[0]
    firsts = []
    lefts = []
    for op_index in range(op_count):
        left_k = chain_order[op_index, 0]
        right_k = chain_order[op_index, 1]
        left_dir = lax.dynamic_index_in_dim(elem_dirs, directions[left_k], 0, keepdims=False)
        right_dir = lax.dynamic_index_in_dim(elem_dirs, directions[right_k], 0, keepdims=False)
        left_spin = lax.dynamic_index_in_dim(spin_mats, left_k, 0, keepdims=False)
        right_spin = lax.dynamic_index_in_dim(spin_mats, right_k, 0, keepdims=False)
        left_rows = lax.dynamic_slice_in_dim(left_dir, row_start, row_tile, axis=1)
        right_cols = lax.dynamic_slice_in_dim(right_dir, col_start, col_tile, axis=2)
        lefts.append(spin_block(left_rows, left_spin))
        right_elem = spin_block(right_cols, right_spin)
        firsts.append(complex_product(forward_rows, right_elem).astype(jnp.bfloat16))
    (first_cols,) = exchange([(jnp.stack(firsts), ("gx",), False)], 1)
    first_cols = jnp.transpose(first_cols, (1, 2, 0, 3, 4)).reshape(op_count, 2, nx * tile, tile)
    seconds = []
    for op_index in range(op_count):
        second = complex_product(lefts[op_index], first_cols[op_index])
        seconds.append((second * inverse).astype(jnp.bfloat16))
    (second_rows,) = exchange([(jnp.stack(seconds), ("gy",), False)], 2)
    second_rows = jnp.transpose(second_rows, (1, 2, 3, 0, 4)).reshape(op_count, 2, tile, ny * tile)
    results = []
    for op_index in range(op_count):
        final = complex_product(second_rows[op_index], backward_cols)
        results.append(final.astype(jnp.bfloat16))
    return jnp.stack(results)


def solution(mesh):
    in_specs = (
        P("gx", "gy", "gz", None, None, None),
        P("gx", "gy", "gz", None, None, None, None),
        P(),
        P(),
        P(None, "gx", "gy"),
        P(None, "gx", "gy"),
        P("gz", None),
    )
    out_specs = P("gz", None, "gx", "gy")
    return jax.shard_map(
        on_device, mesh=mesh, in_specs=in_specs, out_specs=out_specs, check_vma=False
    )
```

```python
import functools
import math

import jax
import jax.numpy as jnp
from jax import lax
from jax.experimental import pallas as pl
from jax.experimental.pallas import tpu as pltpu
from jax.sharding import PartitionSpec as P

MESH_ID = pl.DeviceIdType.MESH


def job_peer(axes, sizes, linear):
    coords = {}
    for axis, size in zip(reversed(axes), reversed(sizes)):
        coords[axis] = lax.rem(linear, size)
        linear = linear // size
    return coords


def exchange_kernel(jobs, *refs):
    count = len(jobs)
    in_refs = refs[:count]
    out_refs = refs[count : 2 * count]
    send_sems = refs[2 * count : 3 * count]
    recv_sems = refs[3 * count :]
    barrier = pltpu.get_barrier_semaphore()
    places = []
    expected = 0
    for axes, sizes, _ in jobs:
        n = math.prod(sizes)
        me = 0
        for axis, size in zip(axes, sizes):
            me = me * size + lax.axis_index(axis)
        places.append((n, me))
        for step in range(1, n):
            peer = job_peer(axes, sizes, lax.rem(me + step, n))
            pl.semaphore_signal(barrier, inc=1, device_id=peer, device_id_type=MESH_ID)
        expected += n - 1
    pl.semaphore_wait(barrier, expected)
    waits = []
    for job, (axes, sizes, scatter) in enumerate(jobs):
        n, me = places[job]
        x_ref, o_ref = in_refs[job], out_refs[job]
        own = x_ref.at[me] if scatter else x_ref
        local = pltpu.make_async_copy(own, o_ref.at[me], send_sems[job].at[0])
        local.start()
        waits.append(local)
        for step in range(1, n):
            linear = lax.rem(me + step, n)
            source = x_ref.at[linear] if scatter else x_ref
            copy = pltpu.make_async_remote_copy(
                src_ref=source,
                dst_ref=o_ref.at[me],
                send_sem=send_sems[job].at[step],
                recv_sem=recv_sems[job].at[step],
                device_id=job_peer(axes, sizes, linear),
                device_id_type=MESH_ID,
            )
            copy.start()
            waits.append(copy)
    for copy in waits:
        copy.wait()


def exchange(jobs, collective_id):
    specs = []
    values = []
    out_shapes = []
    sems = []
    for value, axes, scatter in jobs:
        sizes = tuple(lax.axis_size(axis) for axis in axes)
        n = math.prod(sizes)
        specs.append((tuple(axes), sizes, scatter))
        values.append(value)
        shape = value.shape if scatter else (n,) + value.shape
        out_shapes.append(jax.ShapeDtypeStruct(shape, value.dtype))
        sems.append(pltpu.SemaphoreType.DMA((n,)))
    vmem = pl.BlockSpec(memory_space=pltpu.VMEM)
    return pl.pallas_call(
        functools.partial(exchange_kernel, tuple(specs)),
        out_shape=tuple(out_shapes),
        in_specs=[vmem] * len(jobs),
        out_specs=tuple([vmem] * len(jobs)),
        scratch_shapes=sems + sems,
        compiler_params=pltpu.CompilerParams(collective_id=collective_id, has_side_effects=True),
    )(*values)


def reduce_kernel(sizes, part_ref, fwd_ref, bwd_ref, out_ref, fwd_out, bwd_out,
                  first_buf, first_sum, second_buf, third_buf, sems):
    nx, ny, nz = sizes
    plane = ("gx", "gy")
    plane_sizes = (nx, ny)
    n_plane = nx * ny
    me_x = lax.axis_index("gx")
    me_y = lax.axis_index("gy")
    me_z = lax.axis_index("gz")
    me_p = me_x * ny + me_y
    barrier = pltpu.get_barrier_semaphore()
    for step in range(1, nz):
        peer = {"gz": lax.rem(me_z + step, nz)}
        pl.semaphore_signal(barrier, inc=1, device_id=peer, device_id_type=MESH_ID)
    for step in range(1, n_plane):
        peer = job_peer(plane, plane_sizes, lax.rem(me_p + step, n_plane))
        pl.semaphore_signal(barrier, inc=1, device_id=peer, device_id_type=MESH_ID)
    pl.semaphore_wait(barrier, nz - 1 + n_plane - 1)

    def send_all(axes, axis_sizes, me, src_of, dst_of, slot):
        n = math.prod(axis_sizes)
        copies = []
        local = pltpu.make_async_copy(src_of(me), dst_of(me), sems.at[slot, 0, 0])
        local.start()
        copies.append(local)
        for step in range(1, n):
            linear = lax.rem(me + step, n)
            copy = pltpu.make_async_remote_copy(
                src_ref=src_of(linear),
                dst_ref=dst_of(me),
                send_sem=sems.at[slot, 0, step],
                recv_sem=sems.at[slot, 1, step],
                device_id=job_peer(axes, axis_sizes, linear),
                device_id_type=MESH_ID,
            )
            copy.start()
            copies.append(copy)
        return copies

    gathers = send_all(("gy",), (ny,), me_y, lambda k: fwd_ref, lambda k: fwd_out.at[k], 4)
    gathers += send_all(("gx",), (nx,), me_x, lambda k: bwd_ref, lambda k: bwd_out.at[k], 5)
    stage = send_all(("gz",), (nz,), me_z, lambda k: part_ref.at[k], lambda k: first_buf.at[k], 0)
    for copy in stage:
        copy.wait()
    first_sum[...] = jnp.sum(first_buf[...], axis=0)
    stage = send_all(plane, plane_sizes, me_p, lambda k: first_sum.at[k], lambda k: second_buf.at[k], 1)
    for copy in stage:
        copy.wait()
    first_sum[0] = jnp.sum(second_buf[...], axis=0)
    stage = send_all(plane, plane_sizes, me_p, lambda k: first_sum.at[0], lambda k: third_buf.at[k], 2)
    for copy in stage:
        copy.wait()
    stage = send_all(("gz",), (nz,), me_z, lambda k: third_buf, lambda k: out_ref.at[k], 3)
    for copy in stage:
        copy.wait()
    for copy in gathers:
        copy.wait()


def reduce_everywhere(parts, forward_peram, backward_peram):
    nx, ny, nz = lax.axis_size("gx"), lax.axis_size("gy"), lax.axis_size("gz")
    widest = max(nx * ny, nz)
    piece = parts.shape[1:]
    vmem = pl.BlockSpec(memory_space=pltpu.VMEM)
    return pl.pallas_call(
        functools.partial(reduce_kernel, (nx, ny, nz)),
        out_shape=(
            jax.ShapeDtypeStruct(parts.shape, parts.dtype),
            jax.ShapeDtypeStruct((ny,) + forward_peram.shape, forward_peram.dtype),
            jax.ShapeDtypeStruct((nx,) + backward_peram.shape, backward_peram.dtype),
        ),
        in_specs=[vmem] * 3,
        out_specs=(vmem, vmem, vmem),
        scratch_shapes=[
            pltpu.VMEM(parts.shape, parts.dtype),
            pltpu.VMEM(piece, parts.dtype),
            pltpu.VMEM(piece, parts.dtype),
            pltpu.VMEM(piece, parts.dtype),
            pltpu.SemaphoreType.DMA((6, 2, widest)),
        ],
        compiler_params=pltpu.CompilerParams(collective_id=0, has_side_effects=True),
    )(parts, forward_peram, backward_peram)


def halo_kernel(sizes, one_ref, two_ref, three_ref, one_out, two_out, three_out, send_sem, recv_sem):
    axes = ("gx", "gy", "gz")
    barrier = pltpu.get_barrier_semaphore()
    for axis, n in zip(axes, sizes):
        me = lax.axis_index(axis)
        for peer in (lax.rem(me + n - 1, n), lax.rem(me + 1, n)):
            pl.semaphore_signal(barrier, inc=1, device_id={axis: peer}, device_id_type=MESH_ID)
    pl.semaphore_wait(barrier, 2 * len(axes))
    copies = []
    for slot, (axis, n, src, dst) in enumerate(
        zip(axes, sizes, (one_ref, two_ref, three_ref), (one_out, two_out, three_out))
    ):
        me = lax.axis_index(axis)
        copy = pltpu.make_async_remote_copy(
            src_ref=src,
            dst_ref=dst,
            send_sem=send_sem.at[slot],
            recv_sem=recv_sem.at[slot],
            device_id={axis: lax.rem(me + n - 1, n)},
            device_id_type=MESH_ID,
        )
        copy.start()
        copies.append(copy)
    for copy in copies:
        copy.wait()


def halo_exchange(faces):
    sizes = tuple(lax.axis_size(axis) for axis in ("gx", "gy", "gz"))
    flat = [face.reshape(-1, face.shape[-1]) for face in faces]
    vmem = pl.BlockSpec(memory_space=pltpu.VMEM)
    got = pl.pallas_call(
        functools.partial(halo_kernel, sizes),
        out_shape=tuple(jax.ShapeDtypeStruct(face.shape, face.dtype) for face in flat),
        in_specs=[vmem] * 3,
        out_specs=(vmem, vmem, vmem),
        scratch_shapes=[pltpu.SemaphoreType.DMA((3,)), pltpu.SemaphoreType.DMA((3,))],
        compiler_params=pltpu.CompilerParams(collective_id=3, has_side_effects=True),
    )(*flat)
    return [value.reshape(face.shape) for value, face in zip(got, faces)]


def transport(link_dir, shifted):
    highest = lax.Precision.HIGHEST
    real_v = shifted[..., 0, :, :].astype(jnp.float32)
    imag_v = shifted[..., 1, :, :].astype(jnp.float32)
    real_u = link_dir[..., 0, :, :]
    imag_u = link_dir[..., 1, :, :]

    def apply_link(matrix, vector):
        return jnp.einsum("...ab,...bn->...an", matrix, vector, precision=highest)

    moved_re = apply_link(real_u, real_v) - apply_link(imag_u, imag_v)
    moved_im = apply_link(real_u, imag_v) + apply_link(imag_u, real_v)
    moved = jnp.stack([moved_re, moved_im], axis=-3).astype(jnp.bfloat16)
    turned = jnp.stack([moved_im, -moved_re], axis=-3).astype(jnp.bfloat16)
    return (moved, turned)


def correlation(vec_part, moved, turned):
    width = vec_part.shape[-1]
    left_side = vec_part.reshape(-1, width)
    right_side = jnp.concatenate([moved.reshape(-1, width), turned.reshape(-1, width)], axis=1)
    product = lax.dot_general(
        left_side, right_side, (((0,), (0,)), ((), ())), preferred_element_type=jnp.float32
    )
    return jnp.stack([product[:, :width], product[:, width:]])


def complex_product(left_mat, right_mat):
    row_count = left_mat.shape[1]
    stacked = left_mat.reshape(2 * row_count, left_mat.shape[2])
    first_half = jnp.dot(stacked, right_mat[0], preferred_element_type=jnp.float32)
    second_half = jnp.dot(stacked, right_mat[1], preferred_element_type=jnp.float32)
    return jnp.stack(
        [
            first_half[:row_count] - second_half[row_count:],
            second_half[:row_count] + first_half[row_count:],
        ]
    )


def spin_block(elem, spin):
    highest = lax.Precision.HIGHEST
    rows, cols = elem.shape[1], elem.shape[2]
    big_rows = lax.broadcasted_iota(jnp.int32, (4 * rows, rows), 0)
    row_expand = (big_rows // 4 == lax.broadcasted_iota(jnp.int32, (4 * rows, rows), 1)).astype(jnp.float32)
    big_cols = lax.broadcasted_iota(jnp.int32, (cols, 4 * cols), 1)
    col_expand = (big_cols // 4 == lax.broadcasted_iota(jnp.int32, (cols, 4 * cols), 0)).astype(jnp.float32)
    spin_rows = (
        lax.broadcasted_iota(jnp.int32, (4 * rows, 4), 0) % 4
        == lax.broadcasted_iota(jnp.int32, (4 * rows, 4), 1)
    ).astype(jnp.float32)
    spin_cols = (
        lax.broadcasted_iota(jnp.int32, (4, 4 * cols), 1) % 4
        == lax.broadcasted_iota(jnp.int32, (4, 4 * cols), 0)
    ).astype(jnp.float32)
    repeated = jnp.einsum("ar,crq->caq", row_expand, elem, precision=highest)
    repeated = jnp.einsum("caq,qb->cab", repeated, col_expand, precision=highest)
    tiled = jnp.dot(jnp.dot(spin_rows, spin, precision=highest), spin_cols, precision=highest)
    return (repeated * tiled[None]).astype(jnp.bfloat16)


def spin_times(elem, spin, right):
    n = elem.shape[1]
    highest = lax.Precision.HIGHEST
    wide = 4 * n
    pick = (
        lax.broadcasted_iota(jnp.int32, (4, n, wide), 2)
        == 4 * lax.broadcasted_iota(jnp.int32, (4, n, wide), 1) + lax.broadcasted_iota(jnp.int32, (4, n, wide), 0)
    ).astype(right.dtype)
    split = jnp.einsum("tcm,xmn->xtcn", pick, right, preferred_element_type=jnp.float32).astype(right.dtype)
    split = split.astype(jnp.float32)

    def mul(a, b):
        return jnp.einsum("rc,tcn->trn", a, b, precision=highest)

    real = mul(elem[0], split[0]) - mul(elem[1], split[1])
    imag = mul(elem[0], split[1]) + mul(elem[1], split[0])
    mixed = jnp.einsum("st,xtrn->xsrn", spin, jnp.stack([real, imag]), precision=highest)
    place = (
        lax.broadcasted_iota(jnp.int32, (wide, 4, n), 0)
        == 4 * lax.broadcasted_iota(jnp.int32, (wide, 4, n), 2) + lax.broadcasted_iota(jnp.int32, (wide, 4, n), 1)
    ).astype(jnp.float32)
    placed = jnp.einsum("msr,xsrn->xmn", place, mixed, precision=highest)
    return placed.astype(jnp.bfloat16)


def on_device(eigvecs, links, directions, spin_mats, forward_peram, backward_peram, chain_order):
    face_one, face_two, face_three = halo_exchange(
        [
            lax.slice_in_dim(eigvecs, 0, 1, axis=0),
            lax.slice_in_dim(eigvecs, 0, 1, axis=1),
            lax.slice_in_dim(eigvecs, 0, 1, axis=2),
        ]
    )
    shifted = [
        jnp.concatenate([eigvecs[1:], face_one], axis=0),
        jnp.concatenate([eigvecs[:, 1:], face_two], axis=1),
        jnp.concatenate([eigvecs[:, :, 1:], face_three], axis=2),
    ]
    terms = []
    for direction in range(3):
        moved, turned = transport(links[:, :, :, direction], shifted[direction])
        terms.append(correlation(eigvecs, moved, turned))
    partial_dirs = jnp.stack(terms)
    num_vecs = eigvecs.shape[-1]
    nx, ny, nz = lax.axis_size("gx"), lax.axis_size("gy"), lax.axis_size("gz")
    volume = eigvecs.shape[0] * eigvecs.shape[1] * eigvecs.shape[2] * nx * ny * nz

    full_shape = partial_dirs.shape
    lanes = 128
    rows = partial_dirs.size // lanes
    parts = partial_dirs.reshape(nz, nx * ny, rows // (nz * nx * ny), lanes)
    tile = forward_peram.shape[1]
    summed, forward_rows, backward_cols = reduce_everywhere(parts, forward_peram, backward_peram)
    elem_dirs = summed.reshape(full_shape) * (1.0 / math.sqrt(12.0 * volume))

    row_tile = num_vecs // nx
    col_tile = num_vecs // ny
    row_start = lax.axis_index("gx") * row_tile
    col_start = lax.axis_index("gy") * col_tile
    inverse = 1.0 / math.sqrt(4 * num_vecs)

    forward_rows = jnp.transpose(forward_rows, (1, 2, 0, 3)).reshape(2, tile, ny * tile)
    backward_cols = jnp.transpose(backward_cols, (1, 0, 2, 3)).reshape(2, nx * tile, tile)

    op_count = chain_order.shape[0]
    lefts = []
    tails = []
    for op_index in range(op_count):
        left_k = chain_order[op_index, 0]
        right_k = chain_order[op_index, 1]
        left_dir = lax.dynamic_index_in_dim(elem_dirs, directions[left_k], 0, keepdims=False)
        right_dir = lax.dynamic_index_in_dim(elem_dirs, directions[right_k], 0, keepdims=False)
        left_spin = lax.dynamic_index_in_dim(spin_mats, left_k, 0, keepdims=False)
        right_spin = lax.dynamic_index_in_dim(spin_mats, right_k, 0, keepdims=False)
        left_rows = lax.dynamic_slice_in_dim(left_dir, row_start, row_tile, axis=1)
        lefts.append(spin_block(left_rows, left_spin))
        right_back = spin_times(right_dir, right_spin, backward_cols)
        tails.append(complex_product(forward_rows, right_back).astype(jnp.bfloat16))
    (tail_cols,) = exchange([(jnp.stack(tails), ("gx",), False)], 1)
    tail_cols = jnp.transpose(tail_cols, (1, 2, 0, 3, 4)).reshape(op_count, 2, nx * tile, tile)
    results = []
    for op_index in range(op_count):
        final = complex_product(lefts[op_index], tail_cols[op_index]) * inverse
        results.append(final.astype(jnp.bfloat16))
    return jnp.stack(results)


def solution(mesh):
    in_specs = (
        P("gx", "gy", "gz", None, None, None),
        P("gx", "gy", "gz", None, None, None, None),
        P(),
        P(),
        P(None, "gx", "gy"),
        P(None, "gx", "gy"),
        P("gz", None),
    )
    out_specs = P("gz", None, "gx", "gy")
    return jax.shard_map(
        on_device, mesh=mesh, in_specs=in_specs, out_specs=out_specs, check_vma=False
    )
```

```python
import functools
import math

import jax
import jax.numpy as jnp
from jax import lax
from jax.experimental import pallas as pl
from jax.experimental.pallas import tpu as pltpu
from jax.sharding import PartitionSpec as P

MESH_ID = pl.DeviceIdType.MESH


def job_peer(axes, sizes, linear):
    coords = {}
    for axis, size in zip(reversed(axes), reversed(sizes)):
        coords[axis] = lax.rem(linear, size)
        linear = linear // size
    return coords


def exchange_kernel(jobs, *refs):
    count = len(jobs)
    in_refs = refs[:count]
    out_refs = refs[count : 2 * count]
    send_sems = refs[2 * count : 3 * count]
    recv_sems = refs[3 * count :]
    barrier = pltpu.get_barrier_semaphore()
    places = []
    expected = 0
    for axes, sizes, _ in jobs:
        n = math.prod(sizes)
        me = 0
        for axis, size in zip(axes, sizes):
            me = me * size + lax.axis_index(axis)
        places.append((n, me))
        for step in range(1, n):
            peer = job_peer(axes, sizes, lax.rem(me + step, n))
            pl.semaphore_signal(barrier, inc=1, device_id=peer, device_id_type=MESH_ID)
        expected += n - 1
    pl.semaphore_wait(barrier, expected)
    waits = []
    for job, (axes, sizes, scatter) in enumerate(jobs):
        n, me = places[job]
        x_ref, o_ref = in_refs[job], out_refs[job]
        own = x_ref.at[me] if scatter else x_ref
        local = pltpu.make_async_copy(own, o_ref.at[me], send_sems[job].at[0])
        local.start()
        waits.append(local)
        for step in range(1, n):
            linear = lax.rem(me + step, n)
            source = x_ref.at[linear] if scatter else x_ref
            copy = pltpu.make_async_remote_copy(
                src_ref=source,
                dst_ref=o_ref.at[me],
                send_sem=send_sems[job].at[step],
                recv_sem=recv_sems[job].at[step],
                device_id=job_peer(axes, sizes, linear),
                device_id_type=MESH_ID,
            )
            copy.start()
            waits.append(copy)
    for copy in waits:
        copy.wait()


def exchange(jobs, collective_id):
    specs = []
    values = []
    out_shapes = []
    sems = []
    for value, axes, scatter in jobs:
        sizes = tuple(lax.axis_size(axis) for axis in axes)
        n = math.prod(sizes)
        specs.append((tuple(axes), sizes, scatter))
        values.append(value)
        shape = value.shape if scatter else (n,) + value.shape
        out_shapes.append(jax.ShapeDtypeStruct(shape, value.dtype))
        sems.append(pltpu.SemaphoreType.DMA((n,)))
    vmem = pl.BlockSpec(memory_space=pltpu.VMEM)
    return pl.pallas_call(
        functools.partial(exchange_kernel, tuple(specs)),
        out_shape=tuple(out_shapes),
        in_specs=[vmem] * len(jobs),
        out_specs=tuple([vmem] * len(jobs)),
        scratch_shapes=sems + sems,
        compiler_params=pltpu.CompilerParams(collective_id=collective_id, has_side_effects=True),
    )(*values)


def reduce_kernel(sizes, part_ref, fwd_ref, bwd_ref, out_ref, fwd_out, bwd_out,
                  first_buf, first_sum, second_buf, third_buf, sems):
    nx, ny, nz = sizes
    plane = ("gx", "gy")
    plane_sizes = (nx, ny)
    n_plane = nx * ny
    me_x = lax.axis_index("gx")
    me_y = lax.axis_index("gy")
    me_z = lax.axis_index("gz")
    me_p = me_x * ny + me_y
    barrier = pltpu.get_barrier_semaphore()
    for step in range(1, nz):
        peer = {"gz": lax.rem(me_z + step, nz)}
        pl.semaphore_signal(barrier, inc=1, device_id=peer, device_id_type=MESH_ID)
    for step in range(1, n_plane):
        peer = job_peer(plane, plane_sizes, lax.rem(me_p + step, n_plane))
        pl.semaphore_signal(barrier, inc=1, device_id=peer, device_id_type=MESH_ID)
    pl.semaphore_wait(barrier, nz - 1 + n_plane - 1)

    def send_all(axes, axis_sizes, me, src_of, dst_of, slot):
        n = math.prod(axis_sizes)
        copies = []
        local = pltpu.make_async_copy(src_of(me), dst_of(me), sems.at[slot, 0, 0])
        local.start()
        copies.append(local)
        for step in range(1, n):
            linear = lax.rem(me + step, n)
            copy = pltpu.make_async_remote_copy(
                src_ref=src_of(linear),
                dst_ref=dst_of(me),
                send_sem=sems.at[slot, 0, step],
                recv_sem=sems.at[slot, 1, step],
                device_id=job_peer(axes, axis_sizes, linear),
                device_id_type=MESH_ID,
            )
            copy.start()
            copies.append(copy)
        return copies

    gathers = send_all(("gy",), (ny,), me_y, lambda k: fwd_ref, lambda k: fwd_out.at[k], 4)
    gathers += send_all(("gx",), (nx,), me_x, lambda k: bwd_ref, lambda k: bwd_out.at[k], 5)
    stage = send_all(("gz",), (nz,), me_z, lambda k: part_ref.at[k], lambda k: first_buf.at[k], 0)
    for copy in stage:
        copy.wait()
    first_sum[...] = jnp.sum(first_buf[...], axis=0)
    stage = send_all(plane, plane_sizes, me_p, lambda k: first_sum.at[k], lambda k: second_buf.at[k], 1)
    for copy in stage:
        copy.wait()
    first_sum[0] = jnp.sum(second_buf[...], axis=0)
    stage = send_all(plane, plane_sizes, me_p, lambda k: first_sum.at[0], lambda k: third_buf.at[k], 2)
    for copy in stage:
        copy.wait()
    stage = send_all(("gz",), (nz,), me_z, lambda k: third_buf, lambda k: out_ref.at[k], 3)
    for copy in stage:
        copy.wait()
    for copy in gathers:
        copy.wait()


def reduce_everywhere(parts, forward_peram, backward_peram):
    nx, ny, nz = lax.axis_size("gx"), lax.axis_size("gy"), lax.axis_size("gz")
    widest = max(nx * ny, nz)
    piece = parts.shape[1:]
    vmem = pl.BlockSpec(memory_space=pltpu.VMEM)
    return pl.pallas_call(
        functools.partial(reduce_kernel, (nx, ny, nz)),
        out_shape=(
            jax.ShapeDtypeStruct(parts.shape, parts.dtype),
            jax.ShapeDtypeStruct((ny,) + forward_peram.shape, forward_peram.dtype),
            jax.ShapeDtypeStruct((nx,) + backward_peram.shape, backward_peram.dtype),
        ),
        in_specs=[vmem] * 3,
        out_specs=(vmem, vmem, vmem),
        scratch_shapes=[
            pltpu.VMEM(parts.shape, parts.dtype),
            pltpu.VMEM(piece, parts.dtype),
            pltpu.VMEM(piece, parts.dtype),
            pltpu.VMEM(piece, parts.dtype),
            pltpu.SemaphoreType.DMA((6, 2, widest)),
        ],
        compiler_params=pltpu.CompilerParams(collective_id=0, has_side_effects=True),
    )(parts, forward_peram, backward_peram)


def halo_kernel(sizes, one_ref, two_ref, three_ref, one_out, two_out, three_out, send_sem, recv_sem):
    axes = ("gx", "gy", "gz")
    barrier = pltpu.get_barrier_semaphore()
    for axis, n in zip(axes, sizes):
        me = lax.axis_index(axis)
        for peer in (lax.rem(me + n - 1, n), lax.rem(me + 1, n)):
            pl.semaphore_signal(barrier, inc=1, device_id={axis: peer}, device_id_type=MESH_ID)
    pl.semaphore_wait(barrier, 2 * len(axes))
    copies = []
    for slot, (axis, n, src, dst) in enumerate(
        zip(axes, sizes, (one_ref, two_ref, three_ref), (one_out, two_out, three_out))
    ):
        me = lax.axis_index(axis)
        copy = pltpu.make_async_remote_copy(
            src_ref=src,
            dst_ref=dst,
            send_sem=send_sem.at[slot],
            recv_sem=recv_sem.at[slot],
            device_id={axis: lax.rem(me + n - 1, n)},
            device_id_type=MESH_ID,
        )
        copy.start()
        copies.append(copy)
    for copy in copies:
        copy.wait()


def halo_exchange(faces):
    sizes = tuple(lax.axis_size(axis) for axis in ("gx", "gy", "gz"))
    flat = [face.reshape(-1, face.shape[-1]) for face in faces]
    vmem = pl.BlockSpec(memory_space=pltpu.VMEM)
    got = pl.pallas_call(
        functools.partial(halo_kernel, sizes),
        out_shape=tuple(jax.ShapeDtypeStruct(face.shape, face.dtype) for face in flat),
        in_specs=[vmem] * 3,
        out_specs=(vmem, vmem, vmem),
        scratch_shapes=[pltpu.SemaphoreType.DMA((3,)), pltpu.SemaphoreType.DMA((3,))],
        compiler_params=pltpu.CompilerParams(collective_id=3, has_side_effects=True),
    )(*flat)
    return [value.reshape(face.shape) for value, face in zip(got, faces)]


def transport(link_dir, shifted):
    highest = lax.Precision.HIGHEST
    real_v = shifted[..., 0, :, :].astype(jnp.float32)
    imag_v = shifted[..., 1, :, :].astype(jnp.float32)
    real_u = link_dir[..., 0, :, :]
    imag_u = link_dir[..., 1, :, :]

    def apply_link(matrix, vector):
        return jnp.einsum("...ab,...bn->...an", matrix, vector, precision=highest)

    moved_re = apply_link(real_u, real_v) - apply_link(imag_u, imag_v)
    moved_im = apply_link(real_u, imag_v) + apply_link(imag_u, real_v)
    moved = jnp.stack([moved_re, moved_im], axis=-3).astype(jnp.bfloat16)
    turned = jnp.stack([moved_im, -moved_re], axis=-3).astype(jnp.bfloat16)
    return (moved, turned)


def correlation(vec_part, moved, turned):
    width = vec_part.shape[-1]
    left_side = vec_part.reshape(-1, width)
    right_side = jnp.concatenate([moved.reshape(-1, width), turned.reshape(-1, width)], axis=1)
    product = lax.dot_general(
        left_side, right_side, (((0,), (0,)), ((), ())), preferred_element_type=jnp.float32
    )
    return jnp.stack([product[:, :width], product[:, width:]])


def complex_product(left_mat, right_mat):
    row_count = left_mat.shape[1]
    stacked = left_mat.reshape(2 * row_count, left_mat.shape[2])
    first_half = jnp.dot(stacked, right_mat[0], preferred_element_type=jnp.float32)
    second_half = jnp.dot(stacked, right_mat[1], preferred_element_type=jnp.float32)
    return jnp.stack(
        [
            first_half[:row_count] - second_half[row_count:],
            second_half[:row_count] + first_half[row_count:],
        ]
    )


def spin_block(elem, spin):
    highest = lax.Precision.HIGHEST
    rows, cols = elem.shape[1], elem.shape[2]
    big_rows = lax.broadcasted_iota(jnp.int32, (4 * rows, rows), 0)
    row_expand = (big_rows // 4 == lax.broadcasted_iota(jnp.int32, (4 * rows, rows), 1)).astype(jnp.float32)
    big_cols = lax.broadcasted_iota(jnp.int32, (cols, 4 * cols), 1)
    col_expand = (big_cols // 4 == lax.broadcasted_iota(jnp.int32, (cols, 4 * cols), 0)).astype(jnp.float32)
    spin_rows = (
        lax.broadcasted_iota(jnp.int32, (4 * rows, 4), 0) % 4
        == lax.broadcasted_iota(jnp.int32, (4 * rows, 4), 1)
    ).astype(jnp.float32)
    spin_cols = (
        lax.broadcasted_iota(jnp.int32, (4, 4 * cols), 1) % 4
        == lax.broadcasted_iota(jnp.int32, (4, 4 * cols), 0)
    ).astype(jnp.float32)
    repeated = jnp.einsum("ar,crq->caq", row_expand, elem, precision=highest)
    repeated = jnp.einsum("caq,qb->cab", repeated, col_expand, precision=highest)
    tiled = jnp.dot(jnp.dot(spin_rows, spin, precision=highest), spin_cols, precision=highest)
    return (repeated * tiled[None]).astype(jnp.bfloat16)


def spin_times(elem, spin, right):
    n = elem.shape[1]
    highest = lax.Precision.HIGHEST
    wide = 4 * n
    pick = (
        lax.broadcasted_iota(jnp.int32, (4, n, wide), 2)
        == 4 * lax.broadcasted_iota(jnp.int32, (4, n, wide), 1) + lax.broadcasted_iota(jnp.int32, (4, n, wide), 0)
    ).astype(right.dtype)
    split = jnp.einsum("tcm,xmn->xtcn", pick, right, preferred_element_type=jnp.float32).astype(right.dtype)
    split = split.astype(jnp.float32)

    def mul(a, b):
        return jnp.einsum("rc,tcn->trn", a, b, precision=highest)

    real = mul(elem[0], split[0]) - mul(elem[1], split[1])
    imag = mul(elem[0], split[1]) + mul(elem[1], split[0])
    mixed = jnp.einsum("st,xtrn->xsrn", spin, jnp.stack([real, imag]), precision=highest)
    place = (
        lax.broadcasted_iota(jnp.int32, (wide, 4, n), 0)
        == 4 * lax.broadcasted_iota(jnp.int32, (wide, 4, n), 2) + lax.broadcasted_iota(jnp.int32, (wide, 4, n), 1)
    ).astype(jnp.float32)
    placed = jnp.einsum("msr,xsrn->xmn", place, mixed, precision=highest)
    return placed.astype(jnp.bfloat16)


def on_device(eigvecs, links, directions, spin_mats, forward_peram, backward_peram, chain_order):
    face_one, face_two, face_three = halo_exchange(
        [
            lax.slice_in_dim(eigvecs, 0, 1, axis=0),
            lax.slice_in_dim(eigvecs, 0, 1, axis=1),
            lax.slice_in_dim(eigvecs, 0, 1, axis=2),
        ]
    )
    shifted = [
        jnp.concatenate([eigvecs[1:], face_one], axis=0),
        jnp.concatenate([eigvecs[:, 1:], face_two], axis=1),
        jnp.concatenate([eigvecs[:, :, 1:], face_three], axis=2),
    ]
    terms = []
    for direction in range(3):
        moved, turned = transport(links[:, :, :, direction], shifted[direction])
        terms.append(correlation(eigvecs, moved, turned))
    num_vecs = eigvecs.shape[-1]
    nx, ny, nz = lax.axis_size("gx"), lax.axis_size("gy"), lax.axis_size("gz")
    volume = eigvecs.shape[0] * eigvecs.shape[1] * eigvecs.shape[2] * nx * ny * nz
    partial_dirs = jnp.stack(terms) * (1.0 / math.sqrt(12.0 * volume))

    full_shape = partial_dirs.shape
    lanes = 128
    rows = partial_dirs.size // lanes
    parts = partial_dirs.reshape(nz, nx * ny, rows // (nz * nx * ny), lanes)
    tile = forward_peram.shape[1]
    summed, forward_rows, backward_cols = reduce_everywhere(parts, forward_peram, backward_peram)
    elem_dirs = summed.reshape(full_shape)

    row_tile = num_vecs // nx
    col_tile = num_vecs // ny
    row_start = lax.axis_index("gx") * row_tile
    col_start = lax.axis_index("gy") * col_tile
    inverse = 1.0 / math.sqrt(4 * num_vecs)

    forward_rows = jnp.transpose(forward_rows, (1, 2, 0, 3)).reshape(2, tile, ny * tile)
    backward_cols = jnp.transpose(backward_cols, (1, 0, 2, 3)).reshape(2, nx * tile, tile)

    op_count = chain_order.shape[0]
    lefts = []
    tails = []
    for op_index in range(op_count):
        left_k = chain_order[op_index, 0]
        right_k = chain_order[op_index, 1]
        left_dir = lax.dynamic_index_in_dim(elem_dirs, directions[left_k], 0, keepdims=False)
        right_dir = lax.dynamic_index_in_dim(elem_dirs, directions[right_k], 0, keepdims=False)
        left_spin = lax.dynamic_index_in_dim(spin_mats, left_k, 0, keepdims=False)
        right_spin = lax.dynamic_index_in_dim(spin_mats, right_k, 0, keepdims=False)
        left_rows = lax.dynamic_slice_in_dim(left_dir, row_start, row_tile, axis=1)
        lefts.append(spin_block(left_rows, left_spin))
        right_back = spin_times(right_dir, right_spin, backward_cols)
        tails.append(complex_product(forward_rows, right_back).astype(jnp.bfloat16))
    (tail_cols,) = exchange([(jnp.stack(tails), ("gx",), False)], 1)
    tail_cols = jnp.transpose(tail_cols, (1, 2, 0, 3, 4)).reshape(op_count, 2, nx * tile, tile)
    results = []
    for op_index in range(op_count):
        final = complex_product(lefts[op_index], tail_cols[op_index]) * inverse
        results.append(final.astype(jnp.bfloat16))
    return jnp.stack(results)


def solution(mesh):
    in_specs = (
        P("gx", "gy", "gz", None, None, None),
        P("gx", "gy", "gz", None, None, None, None),
        P(),
        P(),
        P(None, "gx", "gy"),
        P(None, "gx", "gy"),
        P("gz", None),
    )
    out_specs = P("gz", None, "gx", "gy")
    return jax.shard_map(
        on_device, mesh=mesh, in_specs=in_specs, out_specs=out_specs, check_vma=False
    )
```

```python
import functools
import math

import jax
import jax.numpy as jnp
from jax import lax
from jax.experimental import pallas as pl
from jax.experimental.pallas import tpu as pltpu
from jax.sharding import PartitionSpec as P

MESH_ID = pl.DeviceIdType.MESH


def job_peer(axes, sizes, linear):
    coords = {}
    for axis, size in zip(reversed(axes), reversed(sizes)):
        coords[axis] = lax.rem(linear, size)
        linear = linear // size
    return coords


def exchange_kernel(jobs, *refs):
    count = len(jobs)
    in_refs = refs[:count]
    out_refs = refs[count : 2 * count]
    send_sems = refs[2 * count : 3 * count]
    recv_sems = refs[3 * count :]
    barrier = pltpu.get_barrier_semaphore()
    places = []
    expected = 0
    for axes, sizes, _ in jobs:
        n = math.prod(sizes)
        me = 0
        for axis, size in zip(axes, sizes):
            me = me * size + lax.axis_index(axis)
        places.append((n, me))
        for step in range(1, n):
            peer = job_peer(axes, sizes, lax.rem(me + step, n))
            pl.semaphore_signal(barrier, inc=1, device_id=peer, device_id_type=MESH_ID)
        expected += n - 1
    pl.semaphore_wait(barrier, expected)
    waits = []
    for job, (axes, sizes, scatter) in enumerate(jobs):
        n, me = places[job]
        x_ref, o_ref = in_refs[job], out_refs[job]
        own = x_ref.at[me] if scatter else x_ref
        local = pltpu.make_async_copy(own, o_ref.at[me], send_sems[job].at[0])
        local.start()
        waits.append(local)
        for step in range(1, n):
            linear = lax.rem(me + step, n)
            source = x_ref.at[linear] if scatter else x_ref
            copy = pltpu.make_async_remote_copy(
                src_ref=source,
                dst_ref=o_ref.at[me],
                send_sem=send_sems[job].at[step],
                recv_sem=recv_sems[job].at[step],
                device_id=job_peer(axes, sizes, linear),
                device_id_type=MESH_ID,
            )
            copy.start()
            waits.append(copy)
    for copy in waits:
        copy.wait()


def exchange(jobs, collective_id):
    specs = []
    values = []
    out_shapes = []
    sems = []
    for value, axes, scatter in jobs:
        sizes = tuple(lax.axis_size(axis) for axis in axes)
        n = math.prod(sizes)
        specs.append((tuple(axes), sizes, scatter))
        values.append(value)
        shape = value.shape if scatter else (n,) + value.shape
        out_shapes.append(jax.ShapeDtypeStruct(shape, value.dtype))
        sems.append(pltpu.SemaphoreType.DMA((n,)))
    vmem = pl.BlockSpec(memory_space=pltpu.VMEM)
    return pl.pallas_call(
        functools.partial(exchange_kernel, tuple(specs)),
        out_shape=tuple(out_shapes),
        in_specs=[vmem] * len(jobs),
        out_specs=tuple([vmem] * len(jobs)),
        scratch_shapes=sems + sems,
        compiler_params=pltpu.CompilerParams(collective_id=collective_id, has_side_effects=True),
    )(*values)


def reduce_kernel(sizes, part_ref, fwd_ref, bwd_ref, out_ref, fwd_out, bwd_out,
                  first_buf, first_sum, second_buf, third_buf, sems):
    nx, ny, nz = sizes
    plane = ("gx", "gy")
    plane_sizes = (nx, ny)
    n_plane = nx * ny
    me_x = lax.axis_index("gx")
    me_y = lax.axis_index("gy")
    me_z = lax.axis_index("gz")
    me_p = me_x * ny + me_y
    barrier = pltpu.get_barrier_semaphore()
    for step in range(1, nz):
        peer = {"gz": lax.rem(me_z + step, nz)}
        pl.semaphore_signal(barrier, inc=1, device_id=peer, device_id_type=MESH_ID)
    for step in range(1, n_plane):
        peer = job_peer(plane, plane_sizes, lax.rem(me_p + step, n_plane))
        pl.semaphore_signal(barrier, inc=1, device_id=peer, device_id_type=MESH_ID)
    pl.semaphore_wait(barrier, nz - 1 + n_plane - 1)

    def send_all(axes, axis_sizes, me, src_of, dst_of, slot):
        n = math.prod(axis_sizes)
        copies = []
        local = pltpu.make_async_copy(src_of(me), dst_of(me), sems.at[slot, 0, 0])
        local.start()
        copies.append(local)
        for step in range(1, n):
            linear = lax.rem(me + step, n)
            copy = pltpu.make_async_remote_copy(
                src_ref=src_of(linear),
                dst_ref=dst_of(me),
                send_sem=sems.at[slot, 0, step],
                recv_sem=sems.at[slot, 1, step],
                device_id=job_peer(axes, axis_sizes, linear),
                device_id_type=MESH_ID,
            )
            copy.start()
            copies.append(copy)
        return copies

    stage = send_all(("gz",), (nz,), me_z, lambda k: part_ref.at[k], lambda k: first_buf.at[k], 0)
    gathers = send_all(("gy",), (ny,), me_y, lambda k: fwd_ref, lambda k: fwd_out.at[k], 4)
    gathers += send_all(("gx",), (nx,), me_x, lambda k: bwd_ref, lambda k: bwd_out.at[k], 5)
    for copy in stage:
        copy.wait()
    first_sum[...] = jnp.sum(first_buf[...], axis=0)
    stage = send_all(plane, plane_sizes, me_p, lambda k: first_sum.at[k], lambda k: second_buf.at[k], 1)
    for copy in stage:
        copy.wait()
    first_sum[0] = jnp.sum(second_buf[...], axis=0)
    stage = send_all(plane, plane_sizes, me_p, lambda k: first_sum.at[0], lambda k: third_buf.at[k], 2)
    for copy in stage:
        copy.wait()
    stage = send_all(("gz",), (nz,), me_z, lambda k: third_buf, lambda k: out_ref.at[k], 3)
    for copy in stage:
        copy.wait()
    for copy in gathers:
        copy.wait()


def reduce_everywhere(parts, forward_peram, backward_peram):
    nx, ny, nz = lax.axis_size("gx"), lax.axis_size("gy"), lax.axis_size("gz")
    widest = max(nx * ny, nz)
    piece = parts.shape[1:]
    vmem = pl.BlockSpec(memory_space=pltpu.VMEM)
    return pl.pallas_call(
        functools.partial(reduce_kernel, (nx, ny, nz)),
        out_shape=(
            jax.ShapeDtypeStruct(parts.shape, parts.dtype),
            jax.ShapeDtypeStruct((ny,) + forward_peram.shape, forward_peram.dtype),
            jax.ShapeDtypeStruct((nx,) + backward_peram.shape, backward_peram.dtype),
        ),
        in_specs=[vmem] * 3,
        out_specs=(vmem, vmem, vmem),
        scratch_shapes=[
            pltpu.VMEM(parts.shape, parts.dtype),
            pltpu.VMEM(piece, parts.dtype),
            pltpu.VMEM(piece, parts.dtype),
            pltpu.VMEM(piece, parts.dtype),
            pltpu.SemaphoreType.DMA((6, 2, widest)),
        ],
        compiler_params=pltpu.CompilerParams(collective_id=0, has_side_effects=True),
    )(parts, forward_peram, backward_peram)


def halo_kernel(sizes, one_ref, two_ref, three_ref, one_out, two_out, three_out, send_sem, recv_sem):
    axes = ("gx", "gy", "gz")
    barrier = pltpu.get_barrier_semaphore()
    for axis, n in zip(axes, sizes):
        me = lax.axis_index(axis)
        for peer in (lax.rem(me + n - 1, n), lax.rem(me + 1, n)):
            pl.semaphore_signal(barrier, inc=1, device_id={axis: peer}, device_id_type=MESH_ID)
    pl.semaphore_wait(barrier, 2 * len(axes))
    copies = []
    for slot, (axis, n, src, dst) in enumerate(
        zip(axes, sizes, (one_ref, two_ref, three_ref), (one_out, two_out, three_out))
    ):
        me = lax.axis_index(axis)
        copy = pltpu.make_async_remote_copy(
            src_ref=src,
            dst_ref=dst,
            send_sem=send_sem.at[slot],
            recv_sem=recv_sem.at[slot],
            device_id={axis: lax.rem(me + n - 1, n)},
            device_id_type=MESH_ID,
        )
        copy.start()
        copies.append(copy)
    for copy in copies:
        copy.wait()


def halo_exchange(faces):
    sizes = tuple(lax.axis_size(axis) for axis in ("gx", "gy", "gz"))
    flat = [face.reshape(-1, face.shape[-1]) for face in faces]
    vmem = pl.BlockSpec(memory_space=pltpu.VMEM)
    got = pl.pallas_call(
        functools.partial(halo_kernel, sizes),
        out_shape=tuple(jax.ShapeDtypeStruct(face.shape, face.dtype) for face in flat),
        in_specs=[vmem] * 3,
        out_specs=(vmem, vmem, vmem),
        scratch_shapes=[pltpu.SemaphoreType.DMA((3,)), pltpu.SemaphoreType.DMA((3,))],
        compiler_params=pltpu.CompilerParams(collective_id=3, has_side_effects=True),
    )(*flat)
    return [value.reshape(face.shape) for value, face in zip(got, faces)]


def transport(link_dir, shifted):
    highest = lax.Precision.HIGHEST
    real_v = shifted[..., 0, :, :].astype(jnp.float32)
    imag_v = shifted[..., 1, :, :].astype(jnp.float32)
    real_u = link_dir[..., 0, :, :]
    imag_u = link_dir[..., 1, :, :]

    def apply_link(matrix, vector):
        return jnp.einsum("...ab,...bn->...an", matrix, vector, precision=highest)

    moved_re = apply_link(real_u, real_v) - apply_link(imag_u, imag_v)
    moved_im = apply_link(real_u, imag_v) + apply_link(imag_u, real_v)
    moved = jnp.stack([moved_re, moved_im], axis=-3).astype(jnp.bfloat16)
    turned = jnp.stack([moved_im, -moved_re], axis=-3).astype(jnp.bfloat16)
    return (moved, turned)


def correlation(vec_part, moved, turned):
    width = vec_part.shape[-1]
    left_side = vec_part.reshape(-1, width)
    right_side = jnp.concatenate([moved.reshape(-1, width), turned.reshape(-1, width)], axis=1)
    product = lax.dot_general(
        left_side, right_side, (((0,), (0,)), ((), ())), preferred_element_type=jnp.float32
    )
    return jnp.stack([product[:, :width], product[:, width:]])


def complex_product(left_mat, right_mat):
    row_count = left_mat.shape[1]
    stacked = left_mat.reshape(2 * row_count, left_mat.shape[2])
    first_half = jnp.dot(stacked, right_mat[0], preferred_element_type=jnp.float32)
    second_half = jnp.dot(stacked, right_mat[1], preferred_element_type=jnp.float32)
    return jnp.stack(
        [
            first_half[:row_count] - second_half[row_count:],
            second_half[:row_count] + first_half[row_count:],
        ]
    )


def spin_block(elem, spin):
    highest = lax.Precision.HIGHEST
    rows, cols = elem.shape[1], elem.shape[2]
    big_rows = lax.broadcasted_iota(jnp.int32, (4 * rows, rows), 0)
    row_expand = (big_rows // 4 == lax.broadcasted_iota(jnp.int32, (4 * rows, rows), 1)).astype(jnp.float32)
    big_cols = lax.broadcasted_iota(jnp.int32, (cols, 4 * cols), 1)
    col_expand = (big_cols // 4 == lax.broadcasted_iota(jnp.int32, (cols, 4 * cols), 0)).astype(jnp.float32)
    spin_rows = (
        lax.broadcasted_iota(jnp.int32, (4 * rows, 4), 0) % 4
        == lax.broadcasted_iota(jnp.int32, (4 * rows, 4), 1)
    ).astype(jnp.float32)
    spin_cols = (
        lax.broadcasted_iota(jnp.int32, (4, 4 * cols), 1) % 4
        == lax.broadcasted_iota(jnp.int32, (4, 4 * cols), 0)
    ).astype(jnp.float32)
    repeated = jnp.einsum("ar,crq->caq", row_expand, elem, precision=highest)
    repeated = jnp.einsum("caq,qb->cab", repeated, col_expand, precision=highest)
    tiled = jnp.dot(jnp.dot(spin_rows, spin, precision=highest), spin_cols, precision=highest)
    return (repeated * tiled[None]).astype(jnp.bfloat16)


def spin_times(elem, spin, right):
    n = elem.shape[1]
    highest = lax.Precision.HIGHEST
    wide = 4 * n
    pick = (
        lax.broadcasted_iota(jnp.int32, (4, n, wide), 2)
        == 4 * lax.broadcasted_iota(jnp.int32, (4, n, wide), 1) + lax.broadcasted_iota(jnp.int32, (4, n, wide), 0)
    ).astype(right.dtype)
    split = jnp.einsum("tcm,xmn->xtcn", pick, right, preferred_element_type=jnp.float32).astype(right.dtype)
    split = split.astype(jnp.float32)

    def mul(a, b):
        return jnp.einsum("rc,tcn->trn", a, b, precision=highest)

    real = mul(elem[0], split[0]) - mul(elem[1], split[1])
    imag = mul(elem[0], split[1]) + mul(elem[1], split[0])
    parts = [real, imag]
    mixed = jnp.stack(
        [
            jnp.stack(
                [
                    spin[s, 0] * part[0] + spin[s, 1] * part[1] + spin[s, 2] * part[2] + spin[s, 3] * part[3]
                    for s in range(4)
                ]
            )
            for part in parts
        ]
    ).astype(jnp.bfloat16)
    place = (
        lax.broadcasted_iota(jnp.int32, (wide, 4, n), 0)
        == 4 * lax.broadcasted_iota(jnp.int32, (wide, 4, n), 2) + lax.broadcasted_iota(jnp.int32, (wide, 4, n), 1)
    ).astype(jnp.bfloat16)
    placed = jnp.einsum("msr,xsrn->xmn", place, mixed, preferred_element_type=jnp.float32)
    return placed.astype(jnp.bfloat16)


def on_device(eigvecs, links, directions, spin_mats, forward_peram, backward_peram, chain_order):
    face_one, face_two, face_three = halo_exchange(
        [
            lax.slice_in_dim(eigvecs, 0, 1, axis=0),
            lax.slice_in_dim(eigvecs, 0, 1, axis=1),
            lax.slice_in_dim(eigvecs, 0, 1, axis=2),
        ]
    )
    shifted = [
        jnp.concatenate([eigvecs[1:], face_one], axis=0),
        jnp.concatenate([eigvecs[:, 1:], face_two], axis=1),
        jnp.concatenate([eigvecs[:, :, 1:], face_three], axis=2),
    ]
    terms = []
    for direction in range(3):
        moved, turned = transport(links[:, :, :, direction], shifted[direction])
        terms.append(correlation(eigvecs, moved, turned))
    num_vecs = eigvecs.shape[-1]
    nx, ny, nz = lax.axis_size("gx"), lax.axis_size("gy"), lax.axis_size("gz")
    volume = eigvecs.shape[0] * eigvecs.shape[1] * eigvecs.shape[2] * nx * ny * nz
    partial_dirs = jnp.stack(terms) * (1.0 / math.sqrt(12.0 * volume))

    full_shape = partial_dirs.shape
    lanes = 128
    rows = partial_dirs.size // lanes
    parts = partial_dirs.reshape(nz, nx * ny, rows // (nz * nx * ny), lanes)
    tile = forward_peram.shape[1]
    summed, forward_rows, backward_cols = reduce_everywhere(parts, forward_peram, backward_peram)
    elem_dirs = summed.reshape(full_shape)

    row_tile = num_vecs // nx
    col_tile = num_vecs // ny
    row_start = lax.axis_index("gx") * row_tile
    col_start = lax.axis_index("gy") * col_tile
    inverse = 1.0 / math.sqrt(4 * num_vecs)

    forward_rows = jnp.transpose(forward_rows, (1, 2, 0, 3)).reshape(2, tile, ny * tile)
    backward_cols = jnp.transpose(backward_cols, (1, 0, 2, 3)).reshape(2, nx * tile, tile)

    op_count = chain_order.shape[0]
    lefts = []
    tails = []
    for op_index in range(op_count):
        left_k = chain_order[op_index, 0]
        right_k = chain_order[op_index, 1]
        left_dir = lax.dynamic_index_in_dim(elem_dirs, directions[left_k], 0, keepdims=False)
        right_dir = lax.dynamic_index_in_dim(elem_dirs, directions[right_k], 0, keepdims=False)
        left_spin = lax.dynamic_index_in_dim(spin_mats, left_k, 0, keepdims=False)
        right_spin = lax.dynamic_index_in_dim(spin_mats, right_k, 0, keepdims=False)
        left_rows = lax.dynamic_slice_in_dim(left_dir, row_start, row_tile, axis=1)
        lefts.append(spin_block(left_rows, left_spin))
        right_back = spin_times(right_dir, right_spin, backward_cols)
        tails.append(complex_product(forward_rows, right_back).astype(jnp.bfloat16))
    (tail_cols,) = exchange([(jnp.stack(tails), ("gx",), False)], 1)
    tail_cols = jnp.transpose(tail_cols, (1, 2, 0, 3, 4)).reshape(op_count, 2, nx * tile, tile)
    results = []
    for op_index in range(op_count):
        final = complex_product(lefts[op_index], tail_cols[op_index]) * inverse
        results.append(final.astype(jnp.bfloat16))
    return jnp.stack(results)


def solution(mesh):
    in_specs = (
        P("gx", "gy", "gz", None, None, None),
        P("gx", "gy", "gz", None, None, None, None),
        P(),
        P(),
        P(None, "gx", "gy"),
        P(None, "gx", "gy"),
        P("gz", None),
    )
    out_specs = P("gz", None, "gx", "gy")
    return jax.shard_map(
        on_device, mesh=mesh, in_specs=in_specs, out_specs=out_specs, check_vma=False
    )
```

```python
import functools
import math

import jax
import jax.numpy as jnp
from jax import lax
from jax.experimental import pallas as pl
from jax.experimental.pallas import tpu as pltpu
from jax.sharding import PartitionSpec as P

MESH_ID = pl.DeviceIdType.MESH


def job_peer(axes, sizes, linear):
    coords = {}
    for axis, size in zip(reversed(axes), reversed(sizes)):
        coords[axis] = lax.rem(linear, size)
        linear = linear // size
    return coords


def exchange_kernel(jobs, *refs):
    count = len(jobs)
    in_refs = refs[:count]
    out_refs = refs[count : 2 * count]
    send_sems = refs[2 * count : 3 * count]
    recv_sems = refs[3 * count :]
    barrier = pltpu.get_barrier_semaphore()
    places = []
    expected = 0
    for axes, sizes, _ in jobs:
        n = math.prod(sizes)
        me = 0
        for axis, size in zip(axes, sizes):
            me = me * size + lax.axis_index(axis)
        places.append((n, me))
        for step in range(1, n):
            peer = job_peer(axes, sizes, lax.rem(me + step, n))
            pl.semaphore_signal(barrier, inc=1, device_id=peer, device_id_type=MESH_ID)
        expected += n - 1
    pl.semaphore_wait(barrier, expected)
    waits = []
    for job, (axes, sizes, scatter) in enumerate(jobs):
        n, me = places[job]
        x_ref, o_ref = in_refs[job], out_refs[job]
        own = x_ref.at[me] if scatter else x_ref
        local = pltpu.make_async_copy(own, o_ref.at[me], send_sems[job].at[0])
        local.start()
        waits.append(local)
        for step in range(1, n):
            linear = lax.rem(me + step, n)
            source = x_ref.at[linear] if scatter else x_ref
            copy = pltpu.make_async_remote_copy(
                src_ref=source,
                dst_ref=o_ref.at[me],
                send_sem=send_sems[job].at[step],
                recv_sem=recv_sems[job].at[step],
                device_id=job_peer(axes, sizes, linear),
                device_id_type=MESH_ID,
            )
            copy.start()
            waits.append(copy)
    for copy in waits:
        copy.wait()


def exchange(jobs, collective_id):
    specs = []
    values = []
    out_shapes = []
    sems = []
    for value, axes, scatter in jobs:
        sizes = tuple(lax.axis_size(axis) for axis in axes)
        n = math.prod(sizes)
        specs.append((tuple(axes), sizes, scatter))
        values.append(value)
        shape = value.shape if scatter else (n,) + value.shape
        out_shapes.append(jax.ShapeDtypeStruct(shape, value.dtype))
        sems.append(pltpu.SemaphoreType.DMA((n,)))
    vmem = pl.BlockSpec(memory_space=pltpu.VMEM)
    return pl.pallas_call(
        functools.partial(exchange_kernel, tuple(specs)),
        out_shape=tuple(out_shapes),
        in_specs=[vmem] * len(jobs),
        out_specs=tuple([vmem] * len(jobs)),
        scratch_shapes=sems + sems,
        compiler_params=pltpu.CompilerParams(collective_id=collective_id, has_side_effects=True),
    )(*values)


def reduce_kernel(sizes, part_ref, fwd_ref, bwd_ref, out_ref, fwd_out, bwd_out,
                  first_buf, first_sum, second_buf, third_buf, sems):
    nx, ny, nz = sizes
    plane = ("gx", "gy")
    plane_sizes = (nx, ny)
    n_plane = nx * ny
    me_x = lax.axis_index("gx")
    me_y = lax.axis_index("gy")
    me_z = lax.axis_index("gz")
    me_p = me_x * ny + me_y
    barrier = pltpu.get_barrier_semaphore()
    for step in range(1, nz):
        peer = {"gz": lax.rem(me_z + step, nz)}
        pl.semaphore_signal(barrier, inc=1, device_id=peer, device_id_type=MESH_ID)
    for step in range(1, n_plane):
        peer = job_peer(plane, plane_sizes, lax.rem(me_p + step, n_plane))
        pl.semaphore_signal(barrier, inc=1, device_id=peer, device_id_type=MESH_ID)
    pl.semaphore_wait(barrier, nz - 1 + n_plane - 1)

    def send_all(axes, axis_sizes, me, src_of, dst_of, slot):
        n = math.prod(axis_sizes)
        copies = []
        local = pltpu.make_async_copy(src_of(me), dst_of(me), sems.at[slot, 0, 0])
        local.start()
        copies.append(local)
        for step in range(1, n):
            linear = lax.rem(me + step, n)
            copy = pltpu.make_async_remote_copy(
                src_ref=src_of(linear),
                dst_ref=dst_of(me),
                send_sem=sems.at[slot, 0, step],
                recv_sem=sems.at[slot, 1, step],
                device_id=job_peer(axes, axis_sizes, linear),
                device_id_type=MESH_ID,
            )
            copy.start()
            copies.append(copy)
        return copies

    gathers = send_all(("gy",), (ny,), me_y, lambda k: fwd_ref, lambda k: fwd_out.at[k], 4)
    gathers += send_all(("gx",), (nx,), me_x, lambda k: bwd_ref, lambda k: bwd_out.at[k], 5)
    stage = send_all(("gz",), (nz,), me_z, lambda k: part_ref.at[k], lambda k: first_buf.at[k], 0)
    for copy in stage:
        copy.wait()
    first_sum[...] = jnp.sum(first_buf[...], axis=0)
    stage = send_all(plane, plane_sizes, me_p, lambda k: first_sum.at[k], lambda k: second_buf.at[k], 1)
    for copy in stage:
        copy.wait()
    first_sum[0] = jnp.sum(second_buf[...], axis=0)
    stage = send_all(plane, plane_sizes, me_p, lambda k: first_sum.at[0], lambda k: third_buf.at[k], 2)
    for copy in stage:
        copy.wait()
    stage = send_all(("gz",), (nz,), me_z, lambda k: third_buf, lambda k: out_ref.at[k], 3)
    for copy in stage:
        copy.wait()
    for copy in gathers:
        copy.wait()


def reduce_everywhere(parts, forward_peram, backward_peram):
    nx, ny, nz = lax.axis_size("gx"), lax.axis_size("gy"), lax.axis_size("gz")
    widest = max(nx * ny, nz)
    piece = parts.shape[1:]
    vmem = pl.BlockSpec(memory_space=pltpu.VMEM)
    return pl.pallas_call(
        functools.partial(reduce_kernel, (nx, ny, nz)),
        out_shape=(
            jax.ShapeDtypeStruct(parts.shape, parts.dtype),
            jax.ShapeDtypeStruct((ny,) + forward_peram.shape, forward_peram.dtype),
            jax.ShapeDtypeStruct((nx,) + backward_peram.shape, backward_peram.dtype),
        ),
        in_specs=[vmem] * 3,
        out_specs=(vmem, vmem, vmem),
        scratch_shapes=[
            pltpu.VMEM(parts.shape, parts.dtype),
            pltpu.VMEM(piece, parts.dtype),
            pltpu.VMEM(piece, parts.dtype),
            pltpu.VMEM(piece, parts.dtype),
            pltpu.SemaphoreType.DMA((6, 2, widest)),
        ],
        compiler_params=pltpu.CompilerParams(collective_id=0, has_side_effects=True),
    )(parts, forward_peram, backward_peram)


def halo_kernel(sizes, one_ref, two_ref, three_ref, one_out, two_out, three_out, send_sem, recv_sem):
    axes = ("gx", "gy", "gz")
    barrier = pltpu.get_barrier_semaphore()
    for axis, n in zip(axes, sizes):
        me = lax.axis_index(axis)
        for peer in (lax.rem(me + n - 1, n), lax.rem(me + 1, n)):
            pl.semaphore_signal(barrier, inc=1, device_id={axis: peer}, device_id_type=MESH_ID)
    pl.semaphore_wait(barrier, 2 * len(axes))
    copies = []
    for slot, (axis, n, src, dst) in enumerate(
        zip(axes, sizes, (one_ref, two_ref, three_ref), (one_out, two_out, three_out))
    ):
        me = lax.axis_index(axis)
        copy = pltpu.make_async_remote_copy(
            src_ref=src,
            dst_ref=dst,
            send_sem=send_sem.at[slot],
            recv_sem=recv_sem.at[slot],
            device_id={axis: lax.rem(me + n - 1, n)},
            device_id_type=MESH_ID,
        )
        copy.start()
        copies.append(copy)
    for copy in copies:
        copy.wait()


def halo_exchange(faces):
    sizes = tuple(lax.axis_size(axis) for axis in ("gx", "gy", "gz"))
    flat = [face.reshape(-1, face.shape[-1]) for face in faces]
    vmem = pl.BlockSpec(memory_space=pltpu.VMEM)
    got = pl.pallas_call(
        functools.partial(halo_kernel, sizes),
        out_shape=tuple(jax.ShapeDtypeStruct(face.shape, face.dtype) for face in flat),
        in_specs=[vmem] * 3,
        out_specs=(vmem, vmem, vmem),
        scratch_shapes=[pltpu.SemaphoreType.DMA((3,)), pltpu.SemaphoreType.DMA((3,))],
        compiler_params=pltpu.CompilerParams(collective_id=3, has_side_effects=True),
    )(*flat)
    return [value.reshape(face.shape) for value, face in zip(got, faces)]


def transport(link_dir, shifted):
    highest = lax.Precision.HIGHEST
    real_v = shifted[..., 0, :, :].astype(jnp.float32)
    imag_v = shifted[..., 1, :, :].astype(jnp.float32)
    real_u = link_dir[..., 0, :, :]
    imag_u = link_dir[..., 1, :, :]

    def apply_link(matrix, vector):
        return jnp.einsum("...ab,...bn->...an", matrix, vector, precision=highest)

    moved_re = apply_link(real_u, real_v) - apply_link(imag_u, imag_v)
    moved_im = apply_link(real_u, imag_v) + apply_link(imag_u, real_v)
    moved = jnp.stack([moved_re, moved_im], axis=-3).astype(jnp.bfloat16)
    turned = jnp.stack([moved_im, -moved_re], axis=-3).astype(jnp.bfloat16)
    return (moved, turned)


def correlation(vec_part, moved, turned):
    width = vec_part.shape[-1]
    left_side = vec_part.reshape(-1, width)
    right_side = jnp.concatenate([moved.reshape(-1, width), turned.reshape(-1, width)], axis=1)
    product = lax.dot_general(
        left_side, right_side, (((0,), (0,)), ((), ())), preferred_element_type=jnp.float32
    )
    return jnp.stack([product[:, :width], product[:, width:]])


def complex_product(left_mat, right_mat):
    row_count = left_mat.shape[1]
    stacked = left_mat.reshape(2 * row_count, left_mat.shape[2])
    first_half = jnp.dot(stacked, right_mat[0], preferred_element_type=jnp.float32)
    second_half = jnp.dot(stacked, right_mat[1], preferred_element_type=jnp.float32)
    return jnp.stack(
        [
            first_half[:row_count] - second_half[row_count:],
            second_half[:row_count] + first_half[row_count:],
        ]
    )


def spin_block(elem, spin):
    highest = lax.Precision.HIGHEST
    rows, cols = elem.shape[1], elem.shape[2]
    big_rows = lax.broadcasted_iota(jnp.int32, (4 * rows, rows), 0)
    row_expand = (big_rows // 4 == lax.broadcasted_iota(jnp.int32, (4 * rows, rows), 1)).astype(jnp.float32)
    big_cols = lax.broadcasted_iota(jnp.int32, (cols, 4 * cols), 1)
    col_expand = (big_cols // 4 == lax.broadcasted_iota(jnp.int32, (cols, 4 * cols), 0)).astype(jnp.float32)
    spin_rows = (
        lax.broadcasted_iota(jnp.int32, (4 * rows, 4), 0) % 4
        == lax.broadcasted_iota(jnp.int32, (4 * rows, 4), 1)
    ).astype(jnp.float32)
    spin_cols = (
        lax.broadcasted_iota(jnp.int32, (4, 4 * cols), 1) % 4
        == lax.broadcasted_iota(jnp.int32, (4, 4 * cols), 0)
    ).astype(jnp.float32)
    repeated = jnp.einsum("ar,crq->caq", row_expand, elem, precision=highest)
    repeated = jnp.einsum("caq,qb->cab", repeated, col_expand, precision=highest)
    tiled = jnp.dot(jnp.dot(spin_rows, spin, precision=highest), spin_cols, precision=highest)
    return (repeated * tiled[None]).astype(jnp.bfloat16)


def spin_times(elem, spin, right):
    n = elem.shape[1]
    highest = lax.Precision.HIGHEST
    wide = 4 * n
    pick = (
        lax.broadcasted_iota(jnp.int32, (4, n, wide), 2)
        == 4 * lax.broadcasted_iota(jnp.int32, (4, n, wide), 1) + lax.broadcasted_iota(jnp.int32, (4, n, wide), 0)
    ).astype(right.dtype)
    split = jnp.einsum("tcm,xmn->xtcn", pick, right, preferred_element_type=jnp.float32).astype(right.dtype)
    split = split.astype(jnp.float32)

    def mul(a, b):
        return jnp.einsum("rc,tcn->trn", a, b, precision=highest)

    real = mul(elem[0], split[0]) - mul(elem[1], split[1])
    imag = mul(elem[0], split[1]) + mul(elem[1], split[0])
    mixed = jnp.einsum("st,xtrn->xsrn", spin, jnp.stack([real, imag]), precision=highest)
    place = (
        lax.broadcasted_iota(jnp.int32, (wide, 4, n), 0)
        == 4 * lax.broadcasted_iota(jnp.int32, (wide, 4, n), 2) + lax.broadcasted_iota(jnp.int32, (wide, 4, n), 1)
    ).astype(jnp.bfloat16)
    placed = jnp.einsum(
        "msr,xsrn->xmn", place, mixed.astype(jnp.bfloat16), preferred_element_type=jnp.float32
    )
    return placed.astype(jnp.bfloat16)


def on_device(eigvecs, links, directions, spin_mats, forward_peram, backward_peram, chain_order):
    face_one, face_two, face_three = halo_exchange(
        [
            lax.slice_in_dim(eigvecs, 0, 1, axis=0),
            lax.slice_in_dim(eigvecs, 0, 1, axis=1),
            lax.slice_in_dim(eigvecs, 0, 1, axis=2),
        ]
    )
    shifted = [
        jnp.concatenate([eigvecs[1:], face_one], axis=0),
        jnp.concatenate([eigvecs[:, 1:], face_two], axis=1),
        jnp.concatenate([eigvecs[:, :, 1:], face_three], axis=2),
    ]
    terms = []
    for direction in range(3):
        moved, turned = transport(links[:, :, :, direction], shifted[direction])
        terms.append(correlation(eigvecs, moved, turned))
    num_vecs = eigvecs.shape[-1]
    nx, ny, nz = lax.axis_size("gx"), lax.axis_size("gy"), lax.axis_size("gz")
    volume = eigvecs.shape[0] * eigvecs.shape[1] * eigvecs.shape[2] * nx * ny * nz
    partial_dirs = jnp.stack(terms) * (1.0 / math.sqrt(12.0 * volume))

    full_shape = partial_dirs.shape
    lanes = 128
    rows = partial_dirs.size // lanes
    parts = partial_dirs.reshape(nz, nx * ny, rows // (nz * nx * ny), lanes)
    tile = forward_peram.shape[1]
    summed, forward_rows, backward_cols = reduce_everywhere(parts, forward_peram, backward_peram)
    elem_dirs = summed.reshape(full_shape)

    row_tile = num_vecs // nx
    col_tile = num_vecs // ny
    row_start = lax.axis_index("gx") * row_tile
    col_start = lax.axis_index("gy") * col_tile
    inverse = 1.0 / math.sqrt(4 * num_vecs)

    forward_rows = jnp.transpose(forward_rows, (1, 2, 0, 3)).reshape(2, tile, ny * tile)
    backward_cols = jnp.transpose(backward_cols, (1, 0, 2, 3)).reshape(2, nx * tile, tile)

    op_count = chain_order.shape[0]
    lefts = []
    tails = []
    for op_index in range(op_count):
        left_k = chain_order[op_index, 0]
        right_k = chain_order[op_index, 1]
        left_dir = lax.dynamic_index_in_dim(elem_dirs, directions[left_k], 0, keepdims=False)
        right_dir = lax.dynamic_index_in_dim(elem_dirs, directions[right_k], 0, keepdims=False)
        left_spin = lax.dynamic_index_in_dim(spin_mats, left_k, 0, keepdims=False)
        right_spin = lax.dynamic_index_in_dim(spin_mats, right_k, 0, keepdims=False)
        left_rows = lax.dynamic_slice_in_dim(left_dir, row_start, row_tile, axis=1)
        lefts.append(spin_block(left_rows, left_spin))
        right_back = spin_times(right_dir, right_spin, backward_cols)
        tails.append(complex_product(forward_rows, right_back).astype(jnp.bfloat16))
    (tail_cols,) = exchange([(jnp.stack(tails), ("gx",), False)], 1)
    tail_cols = jnp.transpose(tail_cols, (1, 2, 0, 3, 4)).reshape(op_count, 2, nx * tile, tile)
    results = []
    for op_index in range(op_count):
        final = complex_product(lefts[op_index], tail_cols[op_index]) * inverse
        results.append(final.astype(jnp.bfloat16))
    return jnp.stack(results)


def solution(mesh):
    in_specs = (
        P("gx", "gy", "gz", None, None, None),
        P("gx", "gy", "gz", None, None, None, None),
        P(),
        P(),
        P(None, "gx", "gy"),
        P(None, "gx", "gy"),
        P("gz", None),
    )
    out_specs = P("gz", None, "gx", "gy")
    return jax.shard_map(
        on_device, mesh=mesh, in_specs=in_specs, out_specs=out_specs, check_vma=False
    )
```

```python
import functools
import math

import jax
import jax.numpy as jnp
from jax import lax
from jax.experimental import pallas as pl
from jax.experimental.pallas import tpu as pltpu
from jax.sharding import PartitionSpec as P

MESH_ID = pl.DeviceIdType.MESH


def job_peer(axes, sizes, linear):
    coords = {}
    for axis, size in zip(reversed(axes), reversed(sizes)):
        coords[axis] = lax.rem(linear, size)
        linear = linear // size
    return coords


def exchange_kernel(jobs, *refs):
    count = len(jobs)
    in_refs = refs[:count]
    out_refs = refs[count : 2 * count]
    send_sems = refs[2 * count : 3 * count]
    recv_sems = refs[3 * count :]
    barrier = pltpu.get_barrier_semaphore()
    places = []
    expected = 0
    for axes, sizes, _ in jobs:
        n = math.prod(sizes)
        me = 0
        for axis, size in zip(axes, sizes):
            me = me * size + lax.axis_index(axis)
        places.append((n, me))
        for step in range(1, n):
            peer = job_peer(axes, sizes, lax.rem(me + step, n))
            pl.semaphore_signal(barrier, inc=1, device_id=peer, device_id_type=MESH_ID)
        expected += n - 1
    pl.semaphore_wait(barrier, expected)
    waits = []
    for job, (axes, sizes, scatter) in enumerate(jobs):
        n, me = places[job]
        x_ref, o_ref = in_refs[job], out_refs[job]
        own = x_ref.at[me] if scatter else x_ref
        local = pltpu.make_async_copy(own, o_ref.at[me], send_sems[job].at[0])
        local.start()
        waits.append(local)
        for step in range(1, n):
            linear = lax.rem(me + step, n)
            source = x_ref.at[linear] if scatter else x_ref
            copy = pltpu.make_async_remote_copy(
                src_ref=source,
                dst_ref=o_ref.at[me],
                send_sem=send_sems[job].at[step],
                recv_sem=recv_sems[job].at[step],
                device_id=job_peer(axes, sizes, linear),
                device_id_type=MESH_ID,
            )
            copy.start()
            waits.append(copy)
    for copy in waits:
        copy.wait()


def exchange(jobs, collective_id):
    specs = []
    values = []
    out_shapes = []
    sems = []
    for value, axes, scatter in jobs:
        sizes = tuple(lax.axis_size(axis) for axis in axes)
        n = math.prod(sizes)
        specs.append((tuple(axes), sizes, scatter))
        values.append(value)
        shape = value.shape if scatter else (n,) + value.shape
        out_shapes.append(jax.ShapeDtypeStruct(shape, value.dtype))
        sems.append(pltpu.SemaphoreType.DMA((n,)))
    vmem = pl.BlockSpec(memory_space=pltpu.VMEM)
    return pl.pallas_call(
        functools.partial(exchange_kernel, tuple(specs)),
        out_shape=tuple(out_shapes),
        in_specs=[vmem] * len(jobs),
        out_specs=tuple([vmem] * len(jobs)),
        scratch_shapes=sems + sems,
        compiler_params=pltpu.CompilerParams(collective_id=collective_id, has_side_effects=True),
    )(*values)


def reduce_kernel(sizes, part_ref, fwd_ref, bwd_ref, out_ref, fwd_out, bwd_out,
                  first_buf, first_sum, second_buf, third_buf, sems):
    nx, ny, nz = sizes
    plane = ("gx", "gy")
    plane_sizes = (nx, ny)
    n_plane = nx * ny
    me_x = lax.axis_index("gx")
    me_y = lax.axis_index("gy")
    me_z = lax.axis_index("gz")
    me_p = me_x * ny + me_y
    barrier = pltpu.get_barrier_semaphore()
    for step in range(1, nz):
        peer = {"gz": lax.rem(me_z + step, nz)}
        pl.semaphore_signal(barrier, inc=1, device_id=peer, device_id_type=MESH_ID)
    for step in range(1, n_plane):
        peer = job_peer(plane, plane_sizes, lax.rem(me_p + step, n_plane))
        pl.semaphore_signal(barrier, inc=1, device_id=peer, device_id_type=MESH_ID)
    pl.semaphore_wait(barrier, nz - 1 + n_plane - 1)

    def send_all(axes, axis_sizes, me, src_of, dst_of, slot):
        n = math.prod(axis_sizes)
        copies = []
        local = pltpu.make_async_copy(src_of(me), dst_of(me), sems.at[slot, 0, 0])
        local.start()
        copies.append(local)
        for step in range(1, n):
            linear = lax.rem(me + step, n)
            copy = pltpu.make_async_remote_copy(
                src_ref=src_of(linear),
                dst_ref=dst_of(me),
                send_sem=sems.at[slot, 0, step],
                recv_sem=sems.at[slot, 1, step],
                device_id=job_peer(axes, axis_sizes, linear),
                device_id_type=MESH_ID,
            )
            copy.start()
            copies.append(copy)
        return copies

    gathers = send_all(("gy",), (ny,), me_y, lambda k: fwd_ref, lambda k: fwd_out.at[k], 4)
    gathers += send_all(("gx",), (nx,), me_x, lambda k: bwd_ref, lambda k: bwd_out.at[k], 5)
    stage = send_all(("gz",), (nz,), me_z, lambda k: part_ref.at[k], lambda k: first_buf.at[k], 0)
    for copy in stage:
        copy.wait()
    first_sum[...] = jnp.sum(first_buf[...], axis=0)
    stage = send_all(plane, plane_sizes, me_p, lambda k: first_sum.at[k], lambda k: second_buf.at[k], 1)
    for copy in stage:
        copy.wait()
    first_sum[0] = jnp.sum(second_buf[...], axis=0)
    stage = send_all(plane, plane_sizes, me_p, lambda k: first_sum.at[0], lambda k: third_buf.at[k], 2)
    for copy in stage:
        copy.wait()
    stage = send_all(("gz",), (nz,), me_z, lambda k: third_buf, lambda k: out_ref.at[k], 3)
    for copy in stage:
        copy.wait()
    for copy in gathers:
        copy.wait()


def reduce_everywhere(parts, forward_peram, backward_peram):
    nx, ny, nz = lax.axis_size("gx"), lax.axis_size("gy"), lax.axis_size("gz")
    widest = max(nx * ny, nz)
    piece = parts.shape[1:]
    vmem = pl.BlockSpec(memory_space=pltpu.VMEM)
    return pl.pallas_call(
        functools.partial(reduce_kernel, (nx, ny, nz)),
        out_shape=(
            jax.ShapeDtypeStruct(parts.shape, parts.dtype),
            jax.ShapeDtypeStruct((ny,) + forward_peram.shape, forward_peram.dtype),
            jax.ShapeDtypeStruct((nx,) + backward_peram.shape, backward_peram.dtype),
        ),
        in_specs=[vmem] * 3,
        out_specs=(vmem, vmem, vmem),
        scratch_shapes=[
            pltpu.VMEM(parts.shape, parts.dtype),
            pltpu.VMEM(piece, parts.dtype),
            pltpu.VMEM(piece, parts.dtype),
            pltpu.VMEM(piece, parts.dtype),
            pltpu.SemaphoreType.DMA((6, 2, widest)),
        ],
        compiler_params=pltpu.CompilerParams(collective_id=0, has_side_effects=True),
    )(parts, forward_peram, backward_peram)


def halo_kernel(sizes, one_ref, two_ref, three_ref, one_out, two_out, three_out, send_sem, recv_sem):
    axes = ("gx", "gy", "gz")
    barrier = pltpu.get_barrier_semaphore()
    for axis, n in zip(axes, sizes):
        me = lax.axis_index(axis)
        for peer in (lax.rem(me + n - 1, n), lax.rem(me + 1, n)):
            pl.semaphore_signal(barrier, inc=1, device_id={axis: peer}, device_id_type=MESH_ID)
    pl.semaphore_wait(barrier, 2 * len(axes))
    copies = []
    for slot, (axis, n, src, dst) in enumerate(
        zip(axes, sizes, (one_ref, two_ref, three_ref), (one_out, two_out, three_out))
    ):
        me = lax.axis_index(axis)
        copy = pltpu.make_async_remote_copy(
            src_ref=src,
            dst_ref=dst,
            send_sem=send_sem.at[slot],
            recv_sem=recv_sem.at[slot],
            device_id={axis: lax.rem(me + n - 1, n)},
            device_id_type=MESH_ID,
        )
        copy.start()
        copies.append(copy)
    for copy in copies:
        copy.wait()


def halo_exchange(faces):
    sizes = tuple(lax.axis_size(axis) for axis in ("gx", "gy", "gz"))
    flat = [face.reshape(-1, face.shape[-1]) for face in faces]
    vmem = pl.BlockSpec(memory_space=pltpu.VMEM)
    got = pl.pallas_call(
        functools.partial(halo_kernel, sizes),
        out_shape=tuple(jax.ShapeDtypeStruct(face.shape, face.dtype) for face in flat),
        in_specs=[vmem] * 3,
        out_specs=(vmem, vmem, vmem),
        scratch_shapes=[pltpu.SemaphoreType.DMA((3,)), pltpu.SemaphoreType.DMA((3,))],
        compiler_params=pltpu.CompilerParams(collective_id=3, has_side_effects=True),
    )(*flat)
    return [value.reshape(face.shape) for value, face in zip(got, faces)]


def transport(link_dir, shifted):
    highest = lax.Precision.HIGHEST
    real_v = shifted[..., 0, :, :].astype(jnp.float32)
    imag_v = shifted[..., 1, :, :].astype(jnp.float32)
    real_u = link_dir[..., 0, :, :]
    imag_u = link_dir[..., 1, :, :]

    def apply_link(matrix, vector):
        return jnp.einsum("...ab,...bn->...an", matrix, vector, precision=highest)

    moved_re = apply_link(real_u, real_v) - apply_link(imag_u, imag_v)
    moved_im = apply_link(real_u, imag_v) + apply_link(imag_u, real_v)
    moved = jnp.stack([moved_re, moved_im], axis=-3).astype(jnp.bfloat16)
    turned = jnp.stack([moved_im, -moved_re], axis=-3).astype(jnp.bfloat16)
    return (moved, turned)


def correlation(vec_part, moved, turned):
    width = vec_part.shape[-1]
    left_side = vec_part.reshape(-1, width)
    right_side = jnp.concatenate([moved.reshape(-1, width), turned.reshape(-1, width)], axis=1)
    product = lax.dot_general(
        left_side, right_side, (((0,), (0,)), ((), ())), preferred_element_type=jnp.float32
    )
    return jnp.stack([product[:, :width], product[:, width:]])


def complex_product(left_mat, right_mat):
    row_count = left_mat.shape[1]
    stacked = left_mat.reshape(2 * row_count, left_mat.shape[2])
    first_half = jnp.dot(stacked, right_mat[0], preferred_element_type=jnp.float32)
    second_half = jnp.dot(stacked, right_mat[1], preferred_element_type=jnp.float32)
    return jnp.stack(
        [
            first_half[:row_count] - second_half[row_count:],
            second_half[:row_count] + first_half[row_count:],
        ]
    )


def spin_block(elem, spin):
    highest = lax.Precision.HIGHEST
    rows, cols = elem.shape[1], elem.shape[2]
    big_rows = lax.broadcasted_iota(jnp.int32, (4 * rows, rows), 0)
    row_expand = (big_rows // 4 == lax.broadcasted_iota(jnp.int32, (4 * rows, rows), 1)).astype(jnp.float32)
    big_cols = lax.broadcasted_iota(jnp.int32, (cols, 4 * cols), 1)
    col_expand = (big_cols // 4 == lax.broadcasted_iota(jnp.int32, (cols, 4 * cols), 0)).astype(jnp.float32)
    spin_rows = (
        lax.broadcasted_iota(jnp.int32, (4 * rows, 4), 0) % 4
        == lax.broadcasted_iota(jnp.int32, (4 * rows, 4), 1)
    ).astype(jnp.float32)
    spin_cols = (
        lax.broadcasted_iota(jnp.int32, (4, 4 * cols), 1) % 4
        == lax.broadcasted_iota(jnp.int32, (4, 4 * cols), 0)
    ).astype(jnp.float32)
    repeated = jnp.einsum("ar,crq->caq", row_expand, elem, precision=highest)
    repeated = jnp.einsum("caq,qb->cab", repeated, col_expand, precision=highest)
    tiled = jnp.dot(jnp.dot(spin_rows, spin, precision=highest), spin_cols, precision=highest)
    return (repeated * tiled[None]).astype(jnp.bfloat16)


def spin_times(elem, spin, right):
    n = elem.shape[1]
    highest = lax.Precision.HIGHEST
    wide = 4 * n
    pick = (
        lax.broadcasted_iota(jnp.int32, (4, n, wide), 2)
        == 4 * lax.broadcasted_iota(jnp.int32, (4, n, wide), 1) + lax.broadcasted_iota(jnp.int32, (4, n, wide), 0)
    ).astype(right.dtype)
    split = jnp.einsum("tcm,xmn->xtcn", pick, right, preferred_element_type=jnp.float32).astype(right.dtype)
    low = elem.astype(jnp.bfloat16)

    def mul(a, b):
        return jnp.einsum("rc,tcn->trn", a, b, preferred_element_type=jnp.float32)

    real = mul(low[0], split[0]) - mul(low[1], split[1])
    imag = mul(low[0], split[1]) + mul(low[1], split[0])
    mixed = jnp.einsum("st,xtrn->xsrn", spin, jnp.stack([real, imag]), precision=highest)
    place = (
        lax.broadcasted_iota(jnp.int32, (wide, 4, n), 0)
        == 4 * lax.broadcasted_iota(jnp.int32, (wide, 4, n), 2) + lax.broadcasted_iota(jnp.int32, (wide, 4, n), 1)
    ).astype(jnp.bfloat16)
    placed = jnp.einsum(
        "msr,xsrn->xmn", place, mixed.astype(jnp.bfloat16), preferred_element_type=jnp.float32
    )
    return placed.astype(jnp.bfloat16)


def on_device(eigvecs, links, directions, spin_mats, forward_peram, backward_peram, chain_order):
    face_one, face_two, face_three = halo_exchange(
        [
            lax.slice_in_dim(eigvecs, 0, 1, axis=0),
            lax.slice_in_dim(eigvecs, 0, 1, axis=1),
            lax.slice_in_dim(eigvecs, 0, 1, axis=2),
        ]
    )
    shifted = [
        jnp.concatenate([eigvecs[1:], face_one], axis=0),
        jnp.concatenate([eigvecs[:, 1:], face_two], axis=1),
        jnp.concatenate([eigvecs[:, :, 1:], face_three], axis=2),
    ]
    terms = []
    for direction in range(3):
        moved, turned = transport(links[:, :, :, direction], shifted[direction])
        terms.append(correlation(eigvecs, moved, turned))
    num_vecs = eigvecs.shape[-1]
    nx, ny, nz = lax.axis_size("gx"), lax.axis_size("gy"), lax.axis_size("gz")
    volume = eigvecs.shape[0] * eigvecs.shape[1] * eigvecs.shape[2] * nx * ny * nz
    partial_dirs = jnp.stack(terms) * (1.0 / math.sqrt(12.0 * volume))

    full_shape = partial_dirs.shape
    lanes = 128
    rows = partial_dirs.size // lanes
    parts = partial_dirs.reshape(nz, nx * ny, rows // (nz * nx * ny), lanes)
    tile = forward_peram.shape[1]
    summed, forward_rows, backward_cols = reduce_everywhere(parts, forward_peram, backward_peram)
    elem_dirs = summed.reshape(full_shape)

    row_tile = num_vecs // nx
    col_tile = num_vecs // ny
    row_start = lax.axis_index("gx") * row_tile
    col_start = lax.axis_index("gy") * col_tile
    inverse = 1.0 / math.sqrt(4 * num_vecs)

    forward_rows = jnp.transpose(forward_rows, (1, 2, 0, 3)).reshape(2, tile, ny * tile)
    backward_cols = jnp.transpose(backward_cols, (1, 0, 2, 3)).reshape(2, nx * tile, tile)

    op_count = chain_order.shape[0]
    lefts = []
    tails = []
    for op_index in range(op_count):
        left_k = chain_order[op_index, 0]
        right_k = chain_order[op_index, 1]
        left_dir = lax.dynamic_index_in_dim(elem_dirs, directions[left_k], 0, keepdims=False)
        right_dir = lax.dynamic_index_in_dim(elem_dirs, directions[right_k], 0, keepdims=False)
        left_spin = lax.dynamic_index_in_dim(spin_mats, left_k, 0, keepdims=False)
        right_spin = lax.dynamic_index_in_dim(spin_mats, right_k, 0, keepdims=False)
        left_rows = lax.dynamic_slice_in_dim(left_dir, row_start, row_tile, axis=1)
        lefts.append(spin_block(left_rows, left_spin))
        right_back = spin_times(right_dir, right_spin, backward_cols)
        tails.append(complex_product(forward_rows, right_back).astype(jnp.bfloat16))
    (tail_cols,) = exchange([(jnp.stack(tails), ("gx",), False)], 1)
    tail_cols = jnp.transpose(tail_cols, (1, 2, 0, 3, 4)).reshape(op_count, 2, nx * tile, tile)
    results = []
    for op_index in range(op_count):
        final = complex_product(lefts[op_index], tail_cols[op_index]) * inverse
        results.append(final.astype(jnp.bfloat16))
    return jnp.stack(results)


def solution(mesh):
    in_specs = (
        P("gx", "gy", "gz", None, None, None),
        P("gx", "gy", "gz", None, None, None, None),
        P(),
        P(),
        P(None, "gx", "gy"),
        P(None, "gx", "gy"),
        P("gz", None),
    )
    out_specs = P("gz", None, "gx", "gy")
    return jax.shard_map(
        on_device, mesh=mesh, in_specs=in_specs, out_specs=out_specs, check_vma=False
    )
```

```python
import functools
import math

import jax
import jax.numpy as jnp
from jax import lax
from jax.experimental import pallas as pl
from jax.experimental.pallas import tpu as pltpu
from jax.sharding import PartitionSpec as P

MESH_ID = pl.DeviceIdType.MESH


def job_peer(axes, sizes, linear):
    coords = {}
    for axis, size in zip(reversed(axes), reversed(sizes)):
        coords[axis] = lax.rem(linear, size)
        linear = linear // size
    return coords


def exchange_kernel(jobs, *refs):
    count = len(jobs)
    in_refs = refs[:count]
    out_refs = refs[count : 2 * count]
    send_sems = refs[2 * count : 3 * count]
    recv_sems = refs[3 * count :]
    barrier = pltpu.get_barrier_semaphore()
    places = []
    expected = 0
    for axes, sizes, _ in jobs:
        n = math.prod(sizes)
        me = 0
        for axis, size in zip(axes, sizes):
            me = me * size + lax.axis_index(axis)
        places.append((n, me))
        for step in range(1, n):
            peer = job_peer(axes, sizes, lax.rem(me + step, n))
            pl.semaphore_signal(barrier, inc=1, device_id=peer, device_id_type=MESH_ID)
        expected += n - 1
    pl.semaphore_wait(barrier, expected)
    waits = []
    for job, (axes, sizes, scatter) in enumerate(jobs):
        n, me = places[job]
        x_ref, o_ref = in_refs[job], out_refs[job]
        own = x_ref.at[me] if scatter else x_ref
        local = pltpu.make_async_copy(own, o_ref.at[me], send_sems[job].at[0])
        local.start()
        waits.append(local)
        for step in range(1, n):
            linear = lax.rem(me + step, n)
            source = x_ref.at[linear] if scatter else x_ref
            copy = pltpu.make_async_remote_copy(
                src_ref=source,
                dst_ref=o_ref.at[me],
                send_sem=send_sems[job].at[step],
                recv_sem=recv_sems[job].at[step],
                device_id=job_peer(axes, sizes, linear),
                device_id_type=MESH_ID,
            )
            copy.start()
            waits.append(copy)
    for copy in waits:
        copy.wait()


def exchange(jobs, collective_id):
    specs = []
    values = []
    out_shapes = []
    sems = []
    for value, axes, scatter in jobs:
        sizes = tuple(lax.axis_size(axis) for axis in axes)
        n = math.prod(sizes)
        specs.append((tuple(axes), sizes, scatter))
        values.append(value)
        shape = value.shape if scatter else (n,) + value.shape
        out_shapes.append(jax.ShapeDtypeStruct(shape, value.dtype))
        sems.append(pltpu.SemaphoreType.DMA((n,)))
    vmem = pl.BlockSpec(memory_space=pltpu.VMEM)
    return pl.pallas_call(
        functools.partial(exchange_kernel, tuple(specs)),
        out_shape=tuple(out_shapes),
        in_specs=[vmem] * len(jobs),
        out_specs=tuple([vmem] * len(jobs)),
        scratch_shapes=sems + sems,
        compiler_params=pltpu.CompilerParams(collective_id=collective_id, has_side_effects=True),
    )(*values)


def relay_kernel(axis, n, x_ref, o_ref, send_sem, recv_sem, local_sem):
    me = lax.axis_index(axis)
    right = lax.rem(me + 1, n)
    left = lax.rem(me + n - 1, n)
    barrier = pltpu.get_barrier_semaphore()
    for peer in (left, right):
        pl.semaphore_signal(barrier, inc=1, device_id={axis: peer}, device_id_type=MESH_ID)
    pl.semaphore_wait(barrier, 2)
    local = pltpu.make_async_copy(x_ref, o_ref.at[me], local_sem.at[0])
    local.start()

    def hop(way, step):
        if way == 0:
            origin = jnp.maximum(me - step, 0)
            target = right
            sends = (me - step >= 0) & (me + 1 <= n - 1)
            arrives = me - 1 - step >= 0
        else:
            origin = jnp.minimum(me + step, n - 1)
            target = left
            sends = (me + step <= n - 1) & (me - 1 >= 0)
            arrives = me + 1 + step <= n - 1
        incoming = jnp.maximum(me - 1 - step, 0) if way == 0 else jnp.minimum(me + 1 + step, n - 1)
        source = x_ref if step == 0 else o_ref.at[origin]
        copy = pltpu.make_async_remote_copy(
            src_ref=source,
            dst_ref=o_ref.at[origin],
            send_sem=send_sem.at[way, step],
            recv_sem=recv_sem.at[way, step],
            device_id={axis: target},
            device_id_type=MESH_ID,
        )
        landing = pltpu.make_async_remote_copy(
            src_ref=x_ref,
            dst_ref=o_ref.at[incoming],
            send_sem=send_sem.at[way, step],
            recv_sem=recv_sem.at[way, step],
            device_id={axis: target},
            device_id_type=MESH_ID,
        )
        return copy, sends, landing, arrives

    for step in range(n - 1):
        for way in (0, 1):
            if step > 0:
                _, _, landing, arrives = hop(way, step - 1)

                @pl.when(arrives)
                def _():
                    landing.wait_recv()

            copy, sends, _, _ = hop(way, step)

            @pl.when(sends)
            def _():
                copy.start()

    for way in (0, 1):
        _, _, landing, arrives = hop(way, n - 2)

        @pl.when(arrives)
        def _():
            landing.wait_recv()

        for step in range(n - 1):
            copy, sends, _, _ = hop(way, step)

            @pl.when(sends)
            def _():
                copy.wait_send()
    local.wait()


def relay_gather(value, axis, collective_id):
    n = lax.axis_size(axis)
    vmem = pl.BlockSpec(memory_space=pltpu.VMEM)
    return pl.pallas_call(
        functools.partial(relay_kernel, axis, n),
        out_shape=jax.ShapeDtypeStruct((n,) + value.shape, value.dtype),
        in_specs=[vmem],
        out_specs=vmem,
        scratch_shapes=[
            pltpu.SemaphoreType.DMA((2, n)),
            pltpu.SemaphoreType.DMA((2, n)),
            pltpu.SemaphoreType.DMA((1,)),
        ],
        compiler_params=pltpu.CompilerParams(collective_id=collective_id, has_side_effects=True),
    )(value)


def reduce_kernel(sizes, part_ref, fwd_ref, bwd_ref, out_ref, fwd_out, bwd_out,
                  first_buf, first_sum, second_buf, third_buf, sems):
    nx, ny, nz = sizes
    plane = ("gx", "gy")
    plane_sizes = (nx, ny)
    n_plane = nx * ny
    me_x = lax.axis_index("gx")
    me_y = lax.axis_index("gy")
    me_z = lax.axis_index("gz")
    me_p = me_x * ny + me_y
    barrier = pltpu.get_barrier_semaphore()
    for step in range(1, nz):
        peer = {"gz": lax.rem(me_z + step, nz)}
        pl.semaphore_signal(barrier, inc=1, device_id=peer, device_id_type=MESH_ID)
    for step in range(1, n_plane):
        peer = job_peer(plane, plane_sizes, lax.rem(me_p + step, n_plane))
        pl.semaphore_signal(barrier, inc=1, device_id=peer, device_id_type=MESH_ID)
    pl.semaphore_wait(barrier, nz - 1 + n_plane - 1)

    def send_all(axes, axis_sizes, me, src_of, dst_of, slot):
        n = math.prod(axis_sizes)
        copies = []
        local = pltpu.make_async_copy(src_of(me), dst_of(me), sems.at[slot, 0, 0])
        local.start()
        copies.append(local)
        for step in range(1, n):
            linear = lax.rem(me + step, n)
            copy = pltpu.make_async_remote_copy(
                src_ref=src_of(linear),
                dst_ref=dst_of(me),
                send_sem=sems.at[slot, 0, step],
                recv_sem=sems.at[slot, 1, step],
                device_id=job_peer(axes, axis_sizes, linear),
                device_id_type=MESH_ID,
            )
            copy.start()
            copies.append(copy)
        return copies

    gathers = send_all(("gy",), (ny,), me_y, lambda k: fwd_ref, lambda k: fwd_out.at[k], 4)
    gathers += send_all(("gx",), (nx,), me_x, lambda k: bwd_ref, lambda k: bwd_out.at[k], 5)
    stage = send_all(("gz",), (nz,), me_z, lambda k: part_ref.at[k], lambda k: first_buf.at[k], 0)
    for copy in stage:
        copy.wait()
    first_sum[...] = jnp.sum(first_buf[...], axis=0)
    stage = send_all(plane, plane_sizes, me_p, lambda k: first_sum.at[k], lambda k: second_buf.at[k], 1)
    for copy in stage:
        copy.wait()
    first_sum[0] = jnp.sum(second_buf[...], axis=0)
    stage = send_all(plane, plane_sizes, me_p, lambda k: first_sum.at[0], lambda k: third_buf.at[k], 2)
    for copy in stage:
        copy.wait()
    stage = send_all(("gz",), (nz,), me_z, lambda k: third_buf, lambda k: out_ref.at[k], 3)
    for copy in stage:
        copy.wait()
    for copy in gathers:
        copy.wait()


def reduce_everywhere(parts, forward_peram, backward_peram):
    nx, ny, nz = lax.axis_size("gx"), lax.axis_size("gy"), lax.axis_size("gz")
    widest = max(nx * ny, nz)
    piece = parts.shape[1:]
    vmem = pl.BlockSpec(memory_space=pltpu.VMEM)
    return pl.pallas_call(
        functools.partial(reduce_kernel, (nx, ny, nz)),
        out_shape=(
            jax.ShapeDtypeStruct(parts.shape, parts.dtype),
            jax.ShapeDtypeStruct((ny,) + forward_peram.shape, forward_peram.dtype),
            jax.ShapeDtypeStruct((nx,) + backward_peram.shape, backward_peram.dtype),
        ),
        in_specs=[vmem] * 3,
        out_specs=(vmem, vmem, vmem),
        scratch_shapes=[
            pltpu.VMEM(parts.shape, parts.dtype),
            pltpu.VMEM(piece, parts.dtype),
            pltpu.VMEM(piece, parts.dtype),
            pltpu.VMEM(piece, parts.dtype),
            pltpu.SemaphoreType.DMA((6, 2, widest)),
        ],
        compiler_params=pltpu.CompilerParams(collective_id=0, has_side_effects=True),
    )(parts, forward_peram, backward_peram)


def halo_kernel(sizes, one_ref, two_ref, three_ref, one_out, two_out, three_out, send_sem, recv_sem):
    axes = ("gx", "gy", "gz")
    barrier = pltpu.get_barrier_semaphore()
    for axis, n in zip(axes, sizes):
        me = lax.axis_index(axis)
        for peer in (lax.rem(me + n - 1, n), lax.rem(me + 1, n)):
            pl.semaphore_signal(barrier, inc=1, device_id={axis: peer}, device_id_type=MESH_ID)
    pl.semaphore_wait(barrier, 2 * len(axes))
    copies = []
    for slot, (axis, n, src, dst) in enumerate(
        zip(axes, sizes, (one_ref, two_ref, three_ref), (one_out, two_out, three_out))
    ):
        me = lax.axis_index(axis)
        copy = pltpu.make_async_remote_copy(
            src_ref=src,
            dst_ref=dst,
            send_sem=send_sem.at[slot],
            recv_sem=recv_sem.at[slot],
            device_id={axis: lax.rem(me + n - 1, n)},
            device_id_type=MESH_ID,
        )
        copy.start()
        copies.append(copy)
    for copy in copies:
        copy.wait()


def halo_exchange(faces):
    sizes = tuple(lax.axis_size(axis) for axis in ("gx", "gy", "gz"))
    flat = [face.reshape(-1, face.shape[-1]) for face in faces]
    vmem = pl.BlockSpec(memory_space=pltpu.VMEM)
    got = pl.pallas_call(
        functools.partial(halo_kernel, sizes),
        out_shape=tuple(jax.ShapeDtypeStruct(face.shape, face.dtype) for face in flat),
        in_specs=[vmem] * 3,
        out_specs=(vmem, vmem, vmem),
        scratch_shapes=[pltpu.SemaphoreType.DMA((3,)), pltpu.SemaphoreType.DMA((3,))],
        compiler_params=pltpu.CompilerParams(collective_id=3, has_side_effects=True),
    )(*flat)
    return [value.reshape(face.shape) for value, face in zip(got, faces)]


def transport(link_dir, shifted):
    highest = lax.Precision.HIGHEST
    real_v = shifted[..., 0, :, :].astype(jnp.float32)
    imag_v = shifted[..., 1, :, :].astype(jnp.float32)
    real_u = link_dir[..., 0, :, :]
    imag_u = link_dir[..., 1, :, :]

    def apply_link(matrix, vector):
        return jnp.einsum("...ab,...bn->...an", matrix, vector, precision=highest)

    moved_re = apply_link(real_u, real_v) - apply_link(imag_u, imag_v)
    moved_im = apply_link(real_u, imag_v) + apply_link(imag_u, real_v)
    moved = jnp.stack([moved_re, moved_im], axis=-3).astype(jnp.bfloat16)
    turned = jnp.stack([moved_im, -moved_re], axis=-3).astype(jnp.bfloat16)
    return (moved, turned)


def correlation(vec_part, moved, turned):
    width = vec_part.shape[-1]
    left_side = vec_part.reshape(-1, width)
    right_side = jnp.concatenate([moved.reshape(-1, width), turned.reshape(-1, width)], axis=1)
    product = lax.dot_general(
        left_side, right_side, (((0,), (0,)), ((), ())), preferred_element_type=jnp.float32
    )
    return jnp.stack([product[:, :width], product[:, width:]])


def complex_product(left_mat, right_mat):
    row_count = left_mat.shape[1]
    stacked = left_mat.reshape(2 * row_count, left_mat.shape[2])
    first_half = jnp.dot(stacked, right_mat[0], preferred_element_type=jnp.float32)
    second_half = jnp.dot(stacked, right_mat[1], preferred_element_type=jnp.float32)
    return jnp.stack(
        [
            first_half[:row_count] - second_half[row_count:],
            second_half[:row_count] + first_half[row_count:],
        ]
    )


def spin_block(elem, spin):
    highest = lax.Precision.HIGHEST
    rows, cols = elem.shape[1], elem.shape[2]
    big_rows = lax.broadcasted_iota(jnp.int32, (4 * rows, rows), 0)
    row_expand = (big_rows // 4 == lax.broadcasted_iota(jnp.int32, (4 * rows, rows), 1)).astype(jnp.float32)
    big_cols = lax.broadcasted_iota(jnp.int32, (cols, 4 * cols), 1)
    col_expand = (big_cols // 4 == lax.broadcasted_iota(jnp.int32, (cols, 4 * cols), 0)).astype(jnp.float32)
    spin_rows = (
        lax.broadcasted_iota(jnp.int32, (4 * rows, 4), 0) % 4
        == lax.broadcasted_iota(jnp.int32, (4 * rows, 4), 1)
    ).astype(jnp.float32)
    spin_cols = (
        lax.broadcasted_iota(jnp.int32, (4, 4 * cols), 1) % 4
        == lax.broadcasted_iota(jnp.int32, (4, 4 * cols), 0)
    ).astype(jnp.float32)
    repeated = jnp.einsum("ar,crq->caq", row_expand, elem, precision=highest)
    repeated = jnp.einsum("caq,qb->cab", repeated, col_expand, precision=highest)
    tiled = jnp.dot(jnp.dot(spin_rows, spin, precision=highest), spin_cols, precision=highest)
    return (repeated * tiled[None]).astype(jnp.bfloat16)


def spin_times(elem, spin, right):
    n = elem.shape[1]
    highest = lax.Precision.HIGHEST
    wide = 4 * n
    pick = (
        lax.broadcasted_iota(jnp.int32, (4, n, wide), 2)
        == 4 * lax.broadcasted_iota(jnp.int32, (4, n, wide), 1) + lax.broadcasted_iota(jnp.int32, (4, n, wide), 0)
    ).astype(right.dtype)
    split = jnp.einsum("tcm,xmn->xtcn", pick, right, preferred_element_type=jnp.float32).astype(right.dtype)
    low = elem.astype(jnp.bfloat16)

    def mul(a, b):
        return jnp.einsum("rc,tcn->trn", a, b, preferred_element_type=jnp.float32)

    real = mul(low[0], split[0]) - mul(low[1], split[1])
    imag = mul(low[0], split[1]) + mul(low[1], split[0])
    mixed = jnp.einsum("st,xtrn->xsrn", spin, jnp.stack([real, imag]), precision=highest)
    place = (
        lax.broadcasted_iota(jnp.int32, (wide, 4, n), 0)
        == 4 * lax.broadcasted_iota(jnp.int32, (wide, 4, n), 2) + lax.broadcasted_iota(jnp.int32, (wide, 4, n), 1)
    ).astype(jnp.bfloat16)
    placed = jnp.einsum(
        "msr,xsrn->xmn", place, mixed.astype(jnp.bfloat16), preferred_element_type=jnp.float32
    )
    return placed.astype(jnp.bfloat16)


def on_device(eigvecs, links, directions, spin_mats, forward_peram, backward_peram, chain_order):
    face_one, face_two, face_three = halo_exchange(
        [
            lax.slice_in_dim(eigvecs, 0, 1, axis=0),
            lax.slice_in_dim(eigvecs, 0, 1, axis=1),
            lax.slice_in_dim(eigvecs, 0, 1, axis=2),
        ]
    )
    shifted = [
        jnp.concatenate([eigvecs[1:], face_one], axis=0),
        jnp.concatenate([eigvecs[:, 1:], face_two], axis=1),
        jnp.concatenate([eigvecs[:, :, 1:], face_three], axis=2),
    ]
    terms = []
    for direction in range(3):
        moved, turned = transport(links[:, :, :, direction], shifted[direction])
        terms.append(correlation(eigvecs, moved, turned))
    num_vecs = eigvecs.shape[-1]
    nx, ny, nz = lax.axis_size("gx"), lax.axis_size("gy"), lax.axis_size("gz")
    volume = eigvecs.shape[0] * eigvecs.shape[1] * eigvecs.shape[2] * nx * ny * nz
    partial_dirs = jnp.stack(terms) * (1.0 / math.sqrt(12.0 * volume))

    full_shape = partial_dirs.shape
    lanes = 128
    rows = partial_dirs.size // lanes
    parts = partial_dirs.reshape(nz, nx * ny, rows // (nz * nx * ny), lanes)
    tile = forward_peram.shape[1]
    summed, forward_rows, backward_cols = reduce_everywhere(parts, forward_peram, backward_peram)
    elem_dirs = summed.reshape(full_shape)

    row_tile = num_vecs // nx
    col_tile = num_vecs // ny
    row_start = lax.axis_index("gx") * row_tile
    col_start = lax.axis_index("gy") * col_tile
    inverse = 1.0 / math.sqrt(4 * num_vecs)

    forward_rows = jnp.transpose(forward_rows, (1, 2, 0, 3)).reshape(2, tile, ny * tile)
    backward_cols = jnp.transpose(backward_cols, (1, 0, 2, 3)).reshape(2, nx * tile, tile)

    op_count = chain_order.shape[0]
    lefts = []
    tails = []
    for op_index in range(op_count):
        left_k = chain_order[op_index, 0]
        right_k = chain_order[op_index, 1]
        left_dir = lax.dynamic_index_in_dim(elem_dirs, directions[left_k], 0, keepdims=False)
        right_dir = lax.dynamic_index_in_dim(elem_dirs, directions[right_k], 0, keepdims=False)
        left_spin = lax.dynamic_index_in_dim(spin_mats, left_k, 0, keepdims=False)
        right_spin = lax.dynamic_index_in_dim(spin_mats, right_k, 0, keepdims=False)
        left_rows = lax.dynamic_slice_in_dim(left_dir, row_start, row_tile, axis=1)
        lefts.append(spin_block(left_rows, left_spin))
        right_back = spin_times(right_dir, right_spin, backward_cols)
        tails.append(complex_product(forward_rows, right_back).astype(jnp.bfloat16))
    tail_cols = relay_gather(jnp.stack(tails), "gx", 1)
    tail_cols = jnp.transpose(tail_cols, (1, 2, 0, 3, 4)).reshape(op_count, 2, nx * tile, tile)
    results = []
    for op_index in range(op_count):
        final = complex_product(lefts[op_index], tail_cols[op_index]) * inverse
        results.append(final.astype(jnp.bfloat16))
    return jnp.stack(results)


def solution(mesh):
    in_specs = (
        P("gx", "gy", "gz", None, None, None),
        P("gx", "gy", "gz", None, None, None, None),
        P(),
        P(),
        P(None, "gx", "gy"),
        P(None, "gx", "gy"),
        P("gz", None),
    )
    out_specs = P("gz", None, "gx", "gy")
    return jax.shard_map(
        on_device, mesh=mesh, in_specs=in_specs, out_specs=out_specs, check_vma=False
    )
```

```python
import functools
import math

import jax
import jax.numpy as jnp
from jax import lax
from jax.experimental import pallas as pl
from jax.experimental.pallas import tpu as pltpu
from jax.sharding import PartitionSpec as P

MESH_ID = pl.DeviceIdType.MESH


def job_peer(axes, sizes, linear):
    coords = {}
    for axis, size in zip(reversed(axes), reversed(sizes)):
        coords[axis] = lax.rem(linear, size)
        linear = linear // size
    return coords


def exchange_kernel(jobs, *refs):
    count = len(jobs)
    in_refs = refs[:count]
    out_refs = refs[count : 2 * count]
    send_sems = refs[2 * count : 3 * count]
    recv_sems = refs[3 * count :]
    barrier = pltpu.get_barrier_semaphore()
    places = []
    expected = 0
    for axes, sizes, _ in jobs:
        n = math.prod(sizes)
        me = 0
        for axis, size in zip(axes, sizes):
            me = me * size + lax.axis_index(axis)
        places.append((n, me))
        for step in range(1, n):
            peer = job_peer(axes, sizes, lax.rem(me + step, n))
            pl.semaphore_signal(barrier, inc=1, device_id=peer, device_id_type=MESH_ID)
        expected += n - 1
    pl.semaphore_wait(barrier, expected)
    waits = []
    for job, (axes, sizes, scatter) in enumerate(jobs):
        n, me = places[job]
        x_ref, o_ref = in_refs[job], out_refs[job]
        own = x_ref.at[me] if scatter else x_ref
        local = pltpu.make_async_copy(own, o_ref.at[me], send_sems[job].at[0])
        local.start()
        waits.append(local)
        for step in range(1, n):
            linear = lax.rem(me + step, n)
            source = x_ref.at[linear] if scatter else x_ref
            copy = pltpu.make_async_remote_copy(
                src_ref=source,
                dst_ref=o_ref.at[me],
                send_sem=send_sems[job].at[step],
                recv_sem=recv_sems[job].at[step],
                device_id=job_peer(axes, sizes, linear),
                device_id_type=MESH_ID,
            )
            copy.start()
            waits.append(copy)
    for copy in waits:
        copy.wait()


def exchange(jobs, collective_id):
    specs = []
    values = []
    out_shapes = []
    sems = []
    for value, axes, scatter in jobs:
        sizes = tuple(lax.axis_size(axis) for axis in axes)
        n = math.prod(sizes)
        specs.append((tuple(axes), sizes, scatter))
        values.append(value)
        shape = value.shape if scatter else (n,) + value.shape
        out_shapes.append(jax.ShapeDtypeStruct(shape, value.dtype))
        sems.append(pltpu.SemaphoreType.DMA((n,)))
    vmem = pl.BlockSpec(memory_space=pltpu.VMEM)
    return pl.pallas_call(
        functools.partial(exchange_kernel, tuple(specs)),
        out_shape=tuple(out_shapes),
        in_specs=[vmem] * len(jobs),
        out_specs=tuple([vmem] * len(jobs)),
        scratch_shapes=sems + sems,
        compiler_params=pltpu.CompilerParams(collective_id=collective_id, has_side_effects=True),
    )(*values)


def relay_kernel(axis, n, chunks, x_ref, o_ref, send_sem, recv_sem, local_sem):
    me = lax.axis_index(axis)
    right = lax.rem(me + 1, n)
    left = lax.rem(me + n - 1, n)
    barrier = pltpu.get_barrier_semaphore()
    for peer in (left, right):
        pl.semaphore_signal(barrier, inc=1, device_id={axis: peer}, device_id_type=MESH_ID)
    pl.semaphore_wait(barrier, 2)
    local = pltpu.make_async_copy(x_ref, o_ref.at[me], local_sem.at[0])
    local.start()

    def hop(way, step, chunk):
        if way == 0:
            origin = jnp.maximum(me - step, 0)
            incoming = jnp.maximum(me - 1 - step, 0)
            target = right
            sends = (me - step >= 0) & (me + 1 <= n - 1)
            arrives = me - 1 - step >= 0
        else:
            origin = jnp.minimum(me + step, n - 1)
            incoming = jnp.minimum(me + 1 + step, n - 1)
            target = left
            sends = (me + step <= n - 1) & (me - 1 >= 0)
            arrives = me + 1 + step <= n - 1
        source = x_ref.at[chunk] if step == 0 else o_ref.at[origin, chunk]
        copy = pltpu.make_async_remote_copy(
            src_ref=source,
            dst_ref=o_ref.at[origin, chunk],
            send_sem=send_sem.at[way, step, chunk],
            recv_sem=recv_sem.at[way, step, chunk],
            device_id={axis: target},
            device_id_type=MESH_ID,
        )
        landing = pltpu.make_async_remote_copy(
            src_ref=x_ref.at[chunk],
            dst_ref=o_ref.at[incoming, chunk],
            send_sem=send_sem.at[way, step, chunk],
            recv_sem=recv_sem.at[way, step, chunk],
            device_id={axis: target},
            device_id_type=MESH_ID,
        )
        return copy, sends, landing, arrives

    for step in range(n - 1):
        for chunk in range(chunks):
            for way in (0, 1):
                if step > 0:
                    _, _, landing, arrives = hop(way, step - 1, chunk)

                    @pl.when(arrives)
                    def _():
                        landing.wait_recv()

                copy, sends, _, _ = hop(way, step, chunk)

                @pl.when(sends)
                def _():
                    copy.start()

    for way in (0, 1):
        for chunk in range(chunks):
            _, _, landing, arrives = hop(way, n - 2, chunk)

            @pl.when(arrives)
            def _():
                landing.wait_recv()

            for step in range(n - 1):
                copy, sends, _, _ = hop(way, step, chunk)

                @pl.when(sends)
                def _():
                    copy.wait_send()
    local.wait()


def relay_gather(value, axis, collective_id):
    n = lax.axis_size(axis)
    chunks = value.shape[0]
    vmem = pl.BlockSpec(memory_space=pltpu.VMEM)
    return pl.pallas_call(
        functools.partial(relay_kernel, axis, n, chunks),
        out_shape=jax.ShapeDtypeStruct((n,) + value.shape, value.dtype),
        in_specs=[vmem],
        out_specs=vmem,
        scratch_shapes=[
            pltpu.SemaphoreType.DMA((2, n, chunks)),
            pltpu.SemaphoreType.DMA((2, n, chunks)),
            pltpu.SemaphoreType.DMA((1,)),
        ],
        compiler_params=pltpu.CompilerParams(collective_id=collective_id, has_side_effects=True),
    )(value)


def reduce_kernel(sizes, part_ref, fwd_ref, bwd_ref, out_ref, fwd_out, bwd_out,
                  first_buf, first_sum, second_buf, third_buf, sems):
    nx, ny, nz = sizes
    plane = ("gx", "gy")
    plane_sizes = (nx, ny)
    n_plane = nx * ny
    me_x = lax.axis_index("gx")
    me_y = lax.axis_index("gy")
    me_z = lax.axis_index("gz")
    me_p = me_x * ny + me_y
    barrier = pltpu.get_barrier_semaphore()
    for step in range(1, nz):
        peer = {"gz": lax.rem(me_z + step, nz)}
        pl.semaphore_signal(barrier, inc=1, device_id=peer, device_id_type=MESH_ID)
    for step in range(1, n_plane):
        peer = job_peer(plane, plane_sizes, lax.rem(me_p + step, n_plane))
        pl.semaphore_signal(barrier, inc=1, device_id=peer, device_id_type=MESH_ID)
    pl.semaphore_wait(barrier, nz - 1 + n_plane - 1)

    def send_all(axes, axis_sizes, me, src_of, dst_of, slot):
        n = math.prod(axis_sizes)
        copies = []
        local = pltpu.make_async_copy(src_of(me), dst_of(me), sems.at[slot, 0, 0])
        local.start()
        copies.append(local)
        for step in range(1, n):
            linear = lax.rem(me + step, n)
            copy = pltpu.make_async_remote_copy(
                src_ref=src_of(linear),
                dst_ref=dst_of(me),
                send_sem=sems.at[slot, 0, step],
                recv_sem=sems.at[slot, 1, step],
                device_id=job_peer(axes, axis_sizes, linear),
                device_id_type=MESH_ID,
            )
            copy.start()
            copies.append(copy)
        return copies

    gathers = send_all(("gy",), (ny,), me_y, lambda k: fwd_ref, lambda k: fwd_out.at[k], 4)
    gathers += send_all(("gx",), (nx,), me_x, lambda k: bwd_ref, lambda k: bwd_out.at[k], 5)
    stage = send_all(("gz",), (nz,), me_z, lambda k: part_ref.at[k], lambda k: first_buf.at[k], 0)
    for copy in stage:
        copy.wait()
    first_sum[...] = jnp.sum(first_buf[...], axis=0)
    stage = send_all(plane, plane_sizes, me_p, lambda k: first_sum.at[k], lambda k: second_buf.at[k], 1)
    for copy in stage:
        copy.wait()
    first_sum[0] = jnp.sum(second_buf[...], axis=0)
    stage = send_all(plane, plane_sizes, me_p, lambda k: first_sum.at[0], lambda k: third_buf.at[k], 2)
    for copy in stage:
        copy.wait()
    stage = send_all(("gz",), (nz,), me_z, lambda k: third_buf, lambda k: out_ref.at[k], 3)
    for copy in stage:
        copy.wait()
    for copy in gathers:
        copy.wait()


def reduce_everywhere(parts, forward_peram, backward_peram):
    nx, ny, nz = lax.axis_size("gx"), lax.axis_size("gy"), lax.axis_size("gz")
    widest = max(nx * ny, nz)
    piece = parts.shape[1:]
    vmem = pl.BlockSpec(memory_space=pltpu.VMEM)
    return pl.pallas_call(
        functools.partial(reduce_kernel, (nx, ny, nz)),
        out_shape=(
            jax.ShapeDtypeStruct(parts.shape, parts.dtype),
            jax.ShapeDtypeStruct((ny,) + forward_peram.shape, forward_peram.dtype),
            jax.ShapeDtypeStruct((nx,) + backward_peram.shape, backward_peram.dtype),
        ),
        in_specs=[vmem] * 3,
        out_specs=(vmem, vmem, vmem),
        scratch_shapes=[
            pltpu.VMEM(parts.shape, parts.dtype),
            pltpu.VMEM(piece, parts.dtype),
            pltpu.VMEM(piece, parts.dtype),
            pltpu.VMEM(piece, parts.dtype),
            pltpu.SemaphoreType.DMA((6, 2, widest)),
        ],
        compiler_params=pltpu.CompilerParams(collective_id=0, has_side_effects=True),
    )(parts, forward_peram, backward_peram)


def halo_kernel(sizes, one_ref, two_ref, three_ref, one_out, two_out, three_out, send_sem, recv_sem):
    axes = ("gx", "gy", "gz")
    barrier = pltpu.get_barrier_semaphore()
    for axis, n in zip(axes, sizes):
        me = lax.axis_index(axis)
        for peer in (lax.rem(me + n - 1, n), lax.rem(me + 1, n)):
            pl.semaphore_signal(barrier, inc=1, device_id={axis: peer}, device_id_type=MESH_ID)
    pl.semaphore_wait(barrier, 2 * len(axes))
    copies = []
    for slot, (axis, n, src, dst) in enumerate(
        zip(axes, sizes, (one_ref, two_ref, three_ref), (one_out, two_out, three_out))
    ):
        me = lax.axis_index(axis)
        copy = pltpu.make_async_remote_copy(
            src_ref=src,
            dst_ref=dst,
            send_sem=send_sem.at[slot],
            recv_sem=recv_sem.at[slot],
            device_id={axis: lax.rem(me + n - 1, n)},
            device_id_type=MESH_ID,
        )
        copy.start()
        copies.append(copy)
    for copy in copies:
        copy.wait()


def halo_exchange(faces):
    sizes = tuple(lax.axis_size(axis) for axis in ("gx", "gy", "gz"))
    flat = [face.reshape(-1, face.shape[-1]) for face in faces]
    vmem = pl.BlockSpec(memory_space=pltpu.VMEM)
    got = pl.pallas_call(
        functools.partial(halo_kernel, sizes),
        out_shape=tuple(jax.ShapeDtypeStruct(face.shape, face.dtype) for face in flat),
        in_specs=[vmem] * 3,
        out_specs=(vmem, vmem, vmem),
        scratch_shapes=[pltpu.SemaphoreType.DMA((3,)), pltpu.SemaphoreType.DMA((3,))],
        compiler_params=pltpu.CompilerParams(collective_id=3, has_side_effects=True),
    )(*flat)
    return [value.reshape(face.shape) for value, face in zip(got, faces)]


def transport(link_dir, shifted):
    highest = lax.Precision.HIGHEST
    real_v = shifted[..., 0, :, :].astype(jnp.float32)
    imag_v = shifted[..., 1, :, :].astype(jnp.float32)
    real_u = link_dir[..., 0, :, :]
    imag_u = link_dir[..., 1, :, :]

    def apply_link(matrix, vector):
        return jnp.einsum("...ab,...bn->...an", matrix, vector, precision=highest)

    moved_re = apply_link(real_u, real_v) - apply_link(imag_u, imag_v)
    moved_im = apply_link(real_u, imag_v) + apply_link(imag_u, real_v)
    moved = jnp.stack([moved_re, moved_im], axis=-3).astype(jnp.bfloat16)
    turned = jnp.stack([moved_im, -moved_re], axis=-3).astype(jnp.bfloat16)
    return (moved, turned)


def correlation(vec_part, moved, turned):
    width = vec_part.shape[-1]
    left_side = vec_part.reshape(-1, width)
    right_side = jnp.concatenate([moved.reshape(-1, width), turned.reshape(-1, width)], axis=1)
    product = lax.dot_general(
        left_side, right_side, (((0,), (0,)), ((), ())), preferred_element_type=jnp.float32
    )
    return jnp.stack([product[:, :width], product[:, width:]])


def complex_product(left_mat, right_mat):
    row_count = left_mat.shape[1]
    stacked = left_mat.reshape(2 * row_count, left_mat.shape[2])
    first_half = jnp.dot(stacked, right_mat[0], preferred_element_type=jnp.float32)
    second_half = jnp.dot(stacked, right_mat[1], preferred_element_type=jnp.float32)
    return jnp.stack(
        [
            first_half[:row_count] - second_half[row_count:],
            second_half[:row_count] + first_half[row_count:],
        ]
    )


def spin_block(elem, spin):
    highest = lax.Precision.HIGHEST
    rows, cols = elem.shape[1], elem.shape[2]
    big_rows = lax.broadcasted_iota(jnp.int32, (4 * rows, rows), 0)
    row_expand = (big_rows // 4 == lax.broadcasted_iota(jnp.int32, (4 * rows, rows), 1)).astype(jnp.float32)
    big_cols = lax.broadcasted_iota(jnp.int32, (cols, 4 * cols), 1)
    col_expand = (big_cols // 4 == lax.broadcasted_iota(jnp.int32, (cols, 4 * cols), 0)).astype(jnp.float32)
    spin_rows = (
        lax.broadcasted_iota(jnp.int32, (4 * rows, 4), 0) % 4
        == lax.broadcasted_iota(jnp.int32, (4 * rows, 4), 1)
    ).astype(jnp.float32)
    spin_cols = (
        lax.broadcasted_iota(jnp.int32, (4, 4 * cols), 1) % 4
        == lax.broadcasted_iota(jnp.int32, (4, 4 * cols), 0)
    ).astype(jnp.float32)
    repeated = jnp.einsum("ar,crq->caq", row_expand, elem, precision=highest)
    repeated = jnp.einsum("caq,qb->cab", repeated, col_expand, precision=highest)
    tiled = jnp.dot(jnp.dot(spin_rows, spin, precision=highest), spin_cols, precision=highest)
    return (repeated * tiled[None]).astype(jnp.bfloat16)


def spin_times(elem, spin, right):
    n = elem.shape[1]
    highest = lax.Precision.HIGHEST
    wide = 4 * n
    pick = (
        lax.broadcasted_iota(jnp.int32, (4, n, wide), 2)
        == 4 * lax.broadcasted_iota(jnp.int32, (4, n, wide), 1) + lax.broadcasted_iota(jnp.int32, (4, n, wide), 0)
    ).astype(right.dtype)
    split = jnp.einsum("tcm,xmn->xtcn", pick, right, preferred_element_type=jnp.float32).astype(right.dtype)
    low = elem.astype(jnp.bfloat16)

    def mul(a, b):
        return jnp.einsum("rc,tcn->trn", a, b, preferred_element_type=jnp.float32)

    real = mul(low[0], split[0]) - mul(low[1], split[1])
    imag = mul(low[0], split[1]) + mul(low[1], split[0])
    mixed = jnp.einsum("st,xtrn->xsrn", spin, jnp.stack([real, imag]), precision=highest)
    place = (
        lax.broadcasted_iota(jnp.int32, (wide, 4, n), 0)
        == 4 * lax.broadcasted_iota(jnp.int32, (wide, 4, n), 2) + lax.broadcasted_iota(jnp.int32, (wide, 4, n), 1)
    ).astype(jnp.bfloat16)
    placed = jnp.einsum(
        "msr,xsrn->xmn", place, mixed.astype(jnp.bfloat16), preferred_element_type=jnp.float32
    )
    return placed.astype(jnp.bfloat16)


def on_device(eigvecs, links, directions, spin_mats, forward_peram, backward_peram, chain_order):
    face_one, face_two, face_three = halo_exchange(
        [
            lax.slice_in_dim(eigvecs, 0, 1, axis=0),
            lax.slice_in_dim(eigvecs, 0, 1, axis=1),
            lax.slice_in_dim(eigvecs, 0, 1, axis=2),
        ]
    )
    shifted = [
        jnp.concatenate([eigvecs[1:], face_one], axis=0),
        jnp.concatenate([eigvecs[:, 1:], face_two], axis=1),
        jnp.concatenate([eigvecs[:, :, 1:], face_three], axis=2),
    ]
    terms = []
    for direction in range(3):
        moved, turned = transport(links[:, :, :, direction], shifted[direction])
        terms.append(correlation(eigvecs, moved, turned))
    num_vecs = eigvecs.shape[-1]
    nx, ny, nz = lax.axis_size("gx"), lax.axis_size("gy"), lax.axis_size("gz")
    volume = eigvecs.shape[0] * eigvecs.shape[1] * eigvecs.shape[2] * nx * ny * nz
    partial_dirs = jnp.stack(terms) * (1.0 / math.sqrt(12.0 * volume))

    full_shape = partial_dirs.shape
    lanes = 128
    rows = partial_dirs.size // lanes
    parts = partial_dirs.reshape(nz, nx * ny, rows // (nz * nx * ny), lanes)
    tile = forward_peram.shape[1]
    summed, forward_rows, backward_cols = reduce_everywhere(parts, forward_peram, backward_peram)
    elem_dirs = summed.reshape(full_shape)

    row_tile = num_vecs // nx
    col_tile = num_vecs // ny
    row_start = lax.axis_index("gx") * row_tile
    col_start = lax.axis_index("gy") * col_tile
    inverse = 1.0 / math.sqrt(4 * num_vecs)

    forward_rows = jnp.transpose(forward_rows, (1, 2, 0, 3)).reshape(2, tile, ny * tile)
    backward_cols = jnp.transpose(backward_cols, (1, 0, 2, 3)).reshape(2, nx * tile, tile)

    op_count = chain_order.shape[0]
    lefts = []
    tails = []
    for op_index in range(op_count):
        left_k = chain_order[op_index, 0]
        right_k = chain_order[op_index, 1]
        left_dir = lax.dynamic_index_in_dim(elem_dirs, directions[left_k], 0, keepdims=False)
        right_dir = lax.dynamic_index_in_dim(elem_dirs, directions[right_k], 0, keepdims=False)
        left_spin = lax.dynamic_index_in_dim(spin_mats, left_k, 0, keepdims=False)
        right_spin = lax.dynamic_index_in_dim(spin_mats, right_k, 0, keepdims=False)
        left_rows = lax.dynamic_slice_in_dim(left_dir, row_start, row_tile, axis=1)
        lefts.append(spin_block(left_rows, left_spin))
        right_back = spin_times(right_dir, right_spin, backward_cols)
        tails.append(complex_product(forward_rows, right_back).astype(jnp.bfloat16))
    tail_cols = relay_gather(jnp.stack(tails), "gx", 1)
    tail_cols = jnp.transpose(tail_cols, (1, 2, 0, 3, 4)).reshape(op_count, 2, nx * tile, tile)
    results = []
    for op_index in range(op_count):
        final = complex_product(lefts[op_index], tail_cols[op_index]) * inverse
        results.append(final.astype(jnp.bfloat16))
    return jnp.stack(results)


def solution(mesh):
    in_specs = (
        P("gx", "gy", "gz", None, None, None),
        P("gx", "gy", "gz", None, None, None, None),
        P(),
        P(),
        P(None, "gx", "gy"),
        P(None, "gx", "gy"),
        P("gz", None),
    )
    out_specs = P("gz", None, "gx", "gy")
    return jax.shard_map(
        on_device, mesh=mesh, in_specs=in_specs, out_specs=out_specs, check_vma=False
    )
```

```python
import functools
import math

import jax
import jax.numpy as jnp
from jax import lax
from jax.experimental import pallas as pl
from jax.experimental.pallas import tpu as pltpu
from jax.sharding import PartitionSpec as P

MESH_ID = pl.DeviceIdType.MESH


def job_peer(axes, sizes, linear):
    coords = {}
    for axis, size in zip(reversed(axes), reversed(sizes)):
        coords[axis] = lax.rem(linear, size)
        linear = linear // size
    return coords


def exchange_kernel(jobs, *refs):
    count = len(jobs)
    in_refs = refs[:count]
    out_refs = refs[count : 2 * count]
    send_sems = refs[2 * count : 3 * count]
    recv_sems = refs[3 * count :]
    barrier = pltpu.get_barrier_semaphore()
    places = []
    expected = 0
    for axes, sizes, _ in jobs:
        n = math.prod(sizes)
        me = 0
        for axis, size in zip(axes, sizes):
            me = me * size + lax.axis_index(axis)
        places.append((n, me))
        for step in range(1, n):
            peer = job_peer(axes, sizes, lax.rem(me + step, n))
            pl.semaphore_signal(barrier, inc=1, device_id=peer, device_id_type=MESH_ID)
        expected += n - 1
    pl.semaphore_wait(barrier, expected)
    waits = []
    for job, (axes, sizes, scatter) in enumerate(jobs):
        n, me = places[job]
        x_ref, o_ref = in_refs[job], out_refs[job]
        own = x_ref.at[me] if scatter else x_ref
        local = pltpu.make_async_copy(own, o_ref.at[me], send_sems[job].at[0])
        local.start()
        waits.append(local)
        for step in range(1, n):
            linear = lax.rem(me + step, n)
            source = x_ref.at[linear] if scatter else x_ref
            copy = pltpu.make_async_remote_copy(
                src_ref=source,
                dst_ref=o_ref.at[me],
                send_sem=send_sems[job].at[step],
                recv_sem=recv_sems[job].at[step],
                device_id=job_peer(axes, sizes, linear),
                device_id_type=MESH_ID,
            )
            copy.start()
            waits.append(copy)
    for copy in waits:
        copy.wait()


def exchange(jobs, collective_id):
    specs = []
    values = []
    out_shapes = []
    sems = []
    for value, axes, scatter in jobs:
        sizes = tuple(lax.axis_size(axis) for axis in axes)
        n = math.prod(sizes)
        specs.append((tuple(axes), sizes, scatter))
        values.append(value)
        shape = value.shape if scatter else (n,) + value.shape
        out_shapes.append(jax.ShapeDtypeStruct(shape, value.dtype))
        sems.append(pltpu.SemaphoreType.DMA((n,)))
    vmem = pl.BlockSpec(memory_space=pltpu.VMEM)
    return pl.pallas_call(
        functools.partial(exchange_kernel, tuple(specs)),
        out_shape=tuple(out_shapes),
        in_specs=[vmem] * len(jobs),
        out_specs=tuple([vmem] * len(jobs)),
        scratch_shapes=sems + sems,
        compiler_params=pltpu.CompilerParams(collective_id=collective_id, has_side_effects=True),
    )(*values)


def relay_kernel(axis, n, chunks, x_ref, o_ref, send_sem, recv_sem, local_sem):
    me = lax.axis_index(axis)
    right = lax.rem(me + 1, n)
    left = lax.rem(me + n - 1, n)
    barrier = pltpu.get_barrier_semaphore()
    for peer in (left, right):
        pl.semaphore_signal(barrier, inc=1, device_id={axis: peer}, device_id_type=MESH_ID)
    pl.semaphore_wait(barrier, 2)
    local = pltpu.make_async_copy(x_ref, o_ref.at[me], local_sem.at[0])
    local.start()

    def hop(way, step, chunk):
        if way == 0:
            origin = jnp.maximum(me - step, 0)
            incoming = jnp.maximum(me - 1 - step, 0)
            target = right
            sends = (me - step >= 0) & (me + 1 <= n - 1)
            arrives = me - 1 - step >= 0
        else:
            origin = jnp.minimum(me + step, n - 1)
            incoming = jnp.minimum(me + 1 + step, n - 1)
            target = left
            sends = (me + step <= n - 1) & (me - 1 >= 0)
            arrives = me + 1 + step <= n - 1
        source = x_ref.at[chunk] if step == 0 else o_ref.at[origin, chunk]
        copy = pltpu.make_async_remote_copy(
            src_ref=source,
            dst_ref=o_ref.at[origin, chunk],
            send_sem=send_sem.at[way, step, chunk],
            recv_sem=recv_sem.at[way, step, chunk],
            device_id={axis: target},
            device_id_type=MESH_ID,
        )
        landing = pltpu.make_async_remote_copy(
            src_ref=x_ref.at[chunk],
            dst_ref=o_ref.at[incoming, chunk],
            send_sem=send_sem.at[way, step, chunk],
            recv_sem=recv_sem.at[way, step, chunk],
            device_id={axis: target},
            device_id_type=MESH_ID,
        )
        return copy, sends, landing, arrives

    for step in range(n - 1):
        for chunk in range(chunks):
            for way in (0, 1):
                if step > 0:
                    _, _, landing, arrives = hop(way, step - 1, chunk)

                    @pl.when(arrives)
                    def _():
                        landing.wait_recv()

                copy, sends, _, _ = hop(way, step, chunk)

                @pl.when(sends)
                def _():
                    copy.start()

    for way in (0, 1):
        for chunk in range(chunks):
            _, _, landing, arrives = hop(way, n - 2, chunk)

            @pl.when(arrives)
            def _():
                landing.wait_recv()

            for step in range(n - 1):
                copy, sends, _, _ = hop(way, step, chunk)

                @pl.when(sends)
                def _():
                    copy.wait_send()
    local.wait()


def relay_gather(value, axis, collective_id):
    n = lax.axis_size(axis)
    chunks = value.shape[0]
    vmem = pl.BlockSpec(memory_space=pltpu.VMEM)
    return pl.pallas_call(
        functools.partial(relay_kernel, axis, n, chunks),
        out_shape=jax.ShapeDtypeStruct((n,) + value.shape, value.dtype),
        in_specs=[vmem],
        out_specs=vmem,
        scratch_shapes=[
            pltpu.SemaphoreType.DMA((2, n, chunks)),
            pltpu.SemaphoreType.DMA((2, n, chunks)),
            pltpu.SemaphoreType.DMA((1,)),
        ],
        compiler_params=pltpu.CompilerParams(collective_id=collective_id, has_side_effects=True),
    )(value)


def reduce_kernel(sizes, part_ref, fwd_ref, bwd_ref, out_ref, fwd_out, bwd_out,
                  first_buf, first_sum, second_buf, third_buf, sems):
    nx, ny, nz = sizes
    plane = ("gx", "gy")
    plane_sizes = (nx, ny)
    n_plane = nx * ny
    me_x = lax.axis_index("gx")
    me_y = lax.axis_index("gy")
    me_z = lax.axis_index("gz")
    me_p = me_x * ny + me_y
    barrier = pltpu.get_barrier_semaphore()
    for step in range(1, nz):
        peer = {"gz": lax.rem(me_z + step, nz)}
        pl.semaphore_signal(barrier, inc=1, device_id=peer, device_id_type=MESH_ID)
    for step in range(1, n_plane):
        peer = job_peer(plane, plane_sizes, lax.rem(me_p + step, n_plane))
        pl.semaphore_signal(barrier, inc=1, device_id=peer, device_id_type=MESH_ID)
    pl.semaphore_wait(barrier, nz - 1 + n_plane - 1)

    def send_all(axes, axis_sizes, me, src_of, dst_of, slot):
        n = math.prod(axis_sizes)
        copies = []
        local = pltpu.make_async_copy(src_of(me), dst_of(me), sems.at[slot, 0, 0])
        local.start()
        copies.append(local)
        for step in range(1, n):
            linear = lax.rem(me + step, n)
            copy = pltpu.make_async_remote_copy(
                src_ref=src_of(linear),
                dst_ref=dst_of(me),
                send_sem=sems.at[slot, 0, step],
                recv_sem=sems.at[slot, 1, step],
                device_id=job_peer(axes, axis_sizes, linear),
                device_id_type=MESH_ID,
            )
            copy.start()
            copies.append(copy)
        return copies

    gathers = send_all(("gy",), (ny,), me_y, lambda k: fwd_ref, lambda k: fwd_out.at[k], 4)
    gathers += send_all(("gx",), (nx,), me_x, lambda k: bwd_ref, lambda k: bwd_out.at[k], 5)
    stage = send_all(("gz",), (nz,), me_z, lambda k: part_ref.at[k], lambda k: first_buf.at[k], 0)
    for copy in stage:
        copy.wait()
    first_sum[...] = jnp.sum(first_buf[...], axis=0)
    stage = send_all(plane, plane_sizes, me_p, lambda k: first_sum.at[k], lambda k: second_buf.at[k], 1)
    for copy in stage:
        copy.wait()
    first_sum[0] = jnp.sum(second_buf[...], axis=0)
    stage = send_all(plane, plane_sizes, me_p, lambda k: first_sum.at[0], lambda k: third_buf.at[k], 2)
    for copy in stage:
        copy.wait()
    stage = send_all(("gz",), (nz,), me_z, lambda k: third_buf, lambda k: out_ref.at[k], 3)
    for copy in stage:
        copy.wait()
    for copy in gathers:
        copy.wait()


def reduce_everywhere(parts, forward_peram, backward_peram):
    nx, ny, nz = lax.axis_size("gx"), lax.axis_size("gy"), lax.axis_size("gz")
    widest = max(nx * ny, nz)
    piece = parts.shape[1:]
    vmem = pl.BlockSpec(memory_space=pltpu.VMEM)
    return pl.pallas_call(
        functools.partial(reduce_kernel, (nx, ny, nz)),
        out_shape=(
            jax.ShapeDtypeStruct(parts.shape, parts.dtype),
            jax.ShapeDtypeStruct((ny,) + forward_peram.shape, forward_peram.dtype),
            jax.ShapeDtypeStruct((nx,) + backward_peram.shape, backward_peram.dtype),
        ),
        in_specs=[vmem] * 3,
        out_specs=(vmem, vmem, vmem),
        scratch_shapes=[
            pltpu.VMEM(parts.shape, parts.dtype),
            pltpu.VMEM(piece, parts.dtype),
            pltpu.VMEM(piece, parts.dtype),
            pltpu.VMEM(piece, parts.dtype),
            pltpu.SemaphoreType.DMA((6, 2, widest)),
        ],
        compiler_params=pltpu.CompilerParams(collective_id=0, has_side_effects=True),
    )(parts, forward_peram, backward_peram)


def halo_kernel(sizes, one_ref, two_ref, three_ref, one_out, two_out, three_out, send_sem, recv_sem):
    axes = ("gx", "gy", "gz")
    barrier = pltpu.get_barrier_semaphore()
    for axis, n in zip(axes, sizes):
        me = lax.axis_index(axis)
        for peer in (lax.rem(me + n - 1, n), lax.rem(me + 1, n)):
            pl.semaphore_signal(barrier, inc=1, device_id={axis: peer}, device_id_type=MESH_ID)
    pl.semaphore_wait(barrier, 2 * len(axes))
    copies = []
    for slot, (axis, n, src, dst) in enumerate(
        zip(axes, sizes, (one_ref, two_ref, three_ref), (one_out, two_out, three_out))
    ):
        me = lax.axis_index(axis)
        copy = pltpu.make_async_remote_copy(
            src_ref=src,
            dst_ref=dst,
            send_sem=send_sem.at[slot],
            recv_sem=recv_sem.at[slot],
            device_id={axis: lax.rem(me + n - 1, n)},
            device_id_type=MESH_ID,
        )
        copy.start()
        copies.append(copy)
    for copy in copies:
        copy.wait()


def halo_exchange(faces):
    sizes = tuple(lax.axis_size(axis) for axis in ("gx", "gy", "gz"))
    flat = [face.reshape(-1, face.shape[-1]) for face in faces]
    vmem = pl.BlockSpec(memory_space=pltpu.VMEM)
    got = pl.pallas_call(
        functools.partial(halo_kernel, sizes),
        out_shape=tuple(jax.ShapeDtypeStruct(face.shape, face.dtype) for face in flat),
        in_specs=[vmem] * 3,
        out_specs=(vmem, vmem, vmem),
        scratch_shapes=[pltpu.SemaphoreType.DMA((3,)), pltpu.SemaphoreType.DMA((3,))],
        compiler_params=pltpu.CompilerParams(collective_id=3, has_side_effects=True),
    )(*flat)
    return [value.reshape(face.shape) for value, face in zip(got, faces)]


def transport(link_dir, shifted):
    highest = lax.Precision.HIGHEST
    real_v = shifted[..., 0, :, :].astype(jnp.float32)
    imag_v = shifted[..., 1, :, :].astype(jnp.float32)
    real_u = link_dir[..., 0, :, :]
    imag_u = link_dir[..., 1, :, :]

    def apply_link(matrix, vector):
        return jnp.einsum("...ab,...bn->...an", matrix, vector, precision=highest)

    moved_re = apply_link(real_u, real_v) - apply_link(imag_u, imag_v)
    moved_im = apply_link(real_u, imag_v) + apply_link(imag_u, real_v)
    moved = jnp.stack([moved_re, moved_im], axis=-3).astype(jnp.bfloat16)
    turned = jnp.stack([moved_im, -moved_re], axis=-3).astype(jnp.bfloat16)
    return (moved, turned)


def correlation(vec_part, moved, turned):
    width = vec_part.shape[-1]
    left_side = vec_part.reshape(-1, width)
    right_side = jnp.concatenate([moved.reshape(-1, width), turned.reshape(-1, width)], axis=1)
    product = lax.dot_general(
        left_side, right_side, (((0,), (0,)), ((), ())), preferred_element_type=jnp.float32
    )
    return jnp.stack([product[:, :width], product[:, width:]])


def complex_product(left_mat, right_mat):
    row_count = left_mat.shape[1]
    stacked = left_mat.reshape(2 * row_count, left_mat.shape[2])
    first_half = jnp.dot(stacked, right_mat[0], preferred_element_type=jnp.float32)
    second_half = jnp.dot(stacked, right_mat[1], preferred_element_type=jnp.float32)
    return jnp.stack(
        [
            first_half[:row_count] - second_half[row_count:],
            second_half[:row_count] + first_half[row_count:],
        ]
    )


def spin_block(elem, spin):
    highest = lax.Precision.HIGHEST
    rows, cols = elem.shape[1], elem.shape[2]
    big_rows = lax.broadcasted_iota(jnp.int32, (4 * rows, rows), 0)
    row_expand = (big_rows // 4 == lax.broadcasted_iota(jnp.int32, (4 * rows, rows), 1)).astype(jnp.float32)
    big_cols = lax.broadcasted_iota(jnp.int32, (cols, 4 * cols), 1)
    col_expand = (big_cols // 4 == lax.broadcasted_iota(jnp.int32, (cols, 4 * cols), 0)).astype(jnp.float32)
    spin_rows = (
        lax.broadcasted_iota(jnp.int32, (4 * rows, 4), 0) % 4
        == lax.broadcasted_iota(jnp.int32, (4 * rows, 4), 1)
    ).astype(jnp.float32)
    spin_cols = (
        lax.broadcasted_iota(jnp.int32, (4, 4 * cols), 1) % 4
        == lax.broadcasted_iota(jnp.int32, (4, 4 * cols), 0)
    ).astype(jnp.float32)
    repeated = jnp.einsum("ar,crq->caq", row_expand, elem, precision=highest)
    repeated = jnp.einsum("caq,qb->cab", repeated, col_expand, precision=highest)
    tiled = jnp.dot(jnp.dot(spin_rows, spin, precision=highest), spin_cols, precision=highest)
    return (repeated * tiled[None]).astype(jnp.bfloat16)


def spin_times(elem, spin, right):
    n = elem.shape[1]
    highest = lax.Precision.HIGHEST
    wide = 4 * n
    pick = (
        lax.broadcasted_iota(jnp.int32, (4, n, wide), 2)
        == 4 * lax.broadcasted_iota(jnp.int32, (4, n, wide), 1) + lax.broadcasted_iota(jnp.int32, (4, n, wide), 0)
    ).astype(right.dtype)
    split = jnp.einsum("tcm,xmn->xtcn", pick, right, preferred_element_type=jnp.float32).astype(right.dtype)
    low = elem.astype(jnp.bfloat16)

    def mul(a, b):
        return jnp.einsum("rc,tcn->trn", a, b, preferred_element_type=jnp.float32)

    real = mul(low[0], split[0]) - mul(low[1], split[1])
    imag = mul(low[0], split[1]) + mul(low[1], split[0])
    mixed = jnp.einsum("st,xtrn->xsrn", spin, jnp.stack([real, imag]), precision=highest)
    place = (
        lax.broadcasted_iota(jnp.int32, (wide, 4, n), 0)
        == 4 * lax.broadcasted_iota(jnp.int32, (wide, 4, n), 2) + lax.broadcasted_iota(jnp.int32, (wide, 4, n), 1)
    ).astype(jnp.bfloat16)
    placed = jnp.einsum(
        "msr,xsrn->xmn", place, mixed.astype(jnp.bfloat16), preferred_element_type=jnp.float32
    )
    return placed.astype(jnp.bfloat16)


def on_device(eigvecs, links, directions, spin_mats, forward_peram, backward_peram, chain_order):
    face_one, face_two, face_three = halo_exchange(
        [
            lax.slice_in_dim(eigvecs, 0, 1, axis=0),
            lax.slice_in_dim(eigvecs, 0, 1, axis=1),
            lax.slice_in_dim(eigvecs, 0, 1, axis=2),
        ]
    )
    shifted = [
        jnp.concatenate([eigvecs[1:], face_one], axis=0),
        jnp.concatenate([eigvecs[:, 1:], face_two], axis=1),
        jnp.concatenate([eigvecs[:, :, 1:], face_three], axis=2),
    ]
    terms = []
    for direction in range(3):
        moved, turned = transport(links[:, :, :, direction], shifted[direction])
        terms.append(correlation(eigvecs, moved, turned))
    num_vecs = eigvecs.shape[-1]
    nx, ny, nz = lax.axis_size("gx"), lax.axis_size("gy"), lax.axis_size("gz")
    volume = eigvecs.shape[0] * eigvecs.shape[1] * eigvecs.shape[2] * nx * ny * nz
    partial_dirs = jnp.stack(terms) * (1.0 / math.sqrt(12.0 * volume))

    full_shape = partial_dirs.shape
    lanes = 128
    rows = partial_dirs.size // lanes
    parts = partial_dirs.reshape(nz, nx * ny, rows // (nz * nx * ny), lanes)
    tile = forward_peram.shape[1]
    summed, forward_rows, backward_cols = reduce_everywhere(parts, forward_peram, backward_peram)
    elem_dirs = summed.reshape(full_shape)

    row_tile = num_vecs // nx
    col_tile = num_vecs // ny
    row_start = lax.axis_index("gx") * row_tile
    col_start = lax.axis_index("gy") * col_tile
    inverse = 1.0 / math.sqrt(4 * num_vecs)

    forward_rows = jnp.transpose(forward_rows, (1, 2, 0, 3)).reshape(2, tile, ny * tile)
    backward_cols = jnp.transpose(backward_cols, (1, 0, 2, 3)).reshape(2, nx * tile, tile)

    op_count = chain_order.shape[0]
    lefts = []
    tails = []
    for op_index in range(op_count):
        left_k = chain_order[op_index, 0]
        right_k = chain_order[op_index, 1]
        left_dir = lax.dynamic_index_in_dim(elem_dirs, directions[left_k], 0, keepdims=False)
        right_dir = lax.dynamic_index_in_dim(elem_dirs, directions[right_k], 0, keepdims=False)
        left_spin = lax.dynamic_index_in_dim(spin_mats, left_k, 0, keepdims=False)
        right_spin = lax.dynamic_index_in_dim(spin_mats, right_k, 0, keepdims=False)
        left_rows = lax.dynamic_slice_in_dim(left_dir, row_start, row_tile, axis=1)
        lefts.append(spin_block(left_rows, left_spin))
        right_back = spin_times(right_dir, right_spin, backward_cols)
        tails.append(complex_product(forward_rows, right_back).astype(jnp.bfloat16))
    tail_cols = relay_gather(jnp.stack(tails).reshape(op_count * 2, tile, tile), "gx", 1)
    tail_cols = tail_cols.reshape(nx, op_count, 2, tile, tile)
    tail_cols = jnp.transpose(tail_cols, (1, 2, 0, 3, 4)).reshape(op_count, 2, nx * tile, tile)
    results = []
    for op_index in range(op_count):
        final = complex_product(lefts[op_index], tail_cols[op_index]) * inverse
        results.append(final.astype(jnp.bfloat16))
    return jnp.stack(results)


def solution(mesh):
    in_specs = (
        P("gx", "gy", "gz", None, None, None),
        P("gx", "gy", "gz", None, None, None, None),
        P(),
        P(),
        P(None, "gx", "gy"),
        P(None, "gx", "gy"),
        P("gz", None),
    )
    out_specs = P("gz", None, "gx", "gy")
    return jax.shard_map(
        on_device, mesh=mesh, in_specs=in_specs, out_specs=out_specs, check_vma=False
    )
```

```python
import functools
import math

import jax
import jax.numpy as jnp
from jax import lax
from jax.experimental import pallas as pl
from jax.experimental.pallas import tpu as pltpu
from jax.sharding import PartitionSpec as P

MESH_ID = pl.DeviceIdType.MESH


def job_peer(axes, sizes, linear):
    coords = {}
    for axis, size in zip(reversed(axes), reversed(sizes)):
        coords[axis] = lax.rem(linear, size)
        linear = linear // size
    return coords


def exchange_kernel(jobs, *refs):
    count = len(jobs)
    in_refs = refs[:count]
    out_refs = refs[count : 2 * count]
    send_sems = refs[2 * count : 3 * count]
    recv_sems = refs[3 * count :]
    barrier = pltpu.get_barrier_semaphore()
    places = []
    expected = 0
    for axes, sizes, _ in jobs:
        n = math.prod(sizes)
        me = 0
        for axis, size in zip(axes, sizes):
            me = me * size + lax.axis_index(axis)
        places.append((n, me))
        for step in range(1, n):
            peer = job_peer(axes, sizes, lax.rem(me + step, n))
            pl.semaphore_signal(barrier, inc=1, device_id=peer, device_id_type=MESH_ID)
        expected += n - 1
    pl.semaphore_wait(barrier, expected)
    waits = []
    for job, (axes, sizes, scatter) in enumerate(jobs):
        n, me = places[job]
        x_ref, o_ref = in_refs[job], out_refs[job]
        own = x_ref.at[me] if scatter else x_ref
        local = pltpu.make_async_copy(own, o_ref.at[me], send_sems[job].at[0])
        local.start()
        waits.append(local)
        for step in range(1, n):
            linear = lax.rem(me + step, n)
            source = x_ref.at[linear] if scatter else x_ref
            copy = pltpu.make_async_remote_copy(
                src_ref=source,
                dst_ref=o_ref.at[me],
                send_sem=send_sems[job].at[step],
                recv_sem=recv_sems[job].at[step],
                device_id=job_peer(axes, sizes, linear),
                device_id_type=MESH_ID,
            )
            copy.start()
            waits.append(copy)
    for copy in waits:
        copy.wait()


def exchange(jobs, collective_id):
    specs = []
    values = []
    out_shapes = []
    sems = []
    for value, axes, scatter in jobs:
        sizes = tuple(lax.axis_size(axis) for axis in axes)
        n = math.prod(sizes)
        specs.append((tuple(axes), sizes, scatter))
        values.append(value)
        shape = value.shape if scatter else (n,) + value.shape
        out_shapes.append(jax.ShapeDtypeStruct(shape, value.dtype))
        sems.append(pltpu.SemaphoreType.DMA((n,)))
    vmem = pl.BlockSpec(memory_space=pltpu.VMEM)
    return pl.pallas_call(
        functools.partial(exchange_kernel, tuple(specs)),
        out_shape=tuple(out_shapes),
        in_specs=[vmem] * len(jobs),
        out_specs=tuple([vmem] * len(jobs)),
        scratch_shapes=sems + sems,
        compiler_params=pltpu.CompilerParams(collective_id=collective_id, has_side_effects=True),
    )(*values)


def relay_kernel(axis, n, chunks, x_ref, o_ref, send_sem, recv_sem, local_sem):
    me = lax.axis_index(axis)
    right = lax.rem(me + 1, n)
    left = lax.rem(me + n - 1, n)
    barrier = pltpu.get_barrier_semaphore()
    for peer in (left, right):
        pl.semaphore_signal(barrier, inc=1, device_id={axis: peer}, device_id_type=MESH_ID)
    pl.semaphore_wait(barrier, 2)
    local = pltpu.make_async_copy(x_ref, o_ref.at[me], local_sem.at[0])
    local.start()

    def hop(way, step, chunk):
        if way == 0:
            origin = jnp.maximum(me - step, 0)
            incoming = jnp.maximum(me - 1 - step, 0)
            target = right
            sends = (me - step >= 0) & (me + 1 <= n - 1)
            arrives = me - 1 - step >= 0
        else:
            origin = jnp.minimum(me + step, n - 1)
            incoming = jnp.minimum(me + 1 + step, n - 1)
            target = left
            sends = (me + step <= n - 1) & (me - 1 >= 0)
            arrives = me + 1 + step <= n - 1
        source = x_ref.at[chunk] if step == 0 else o_ref.at[origin, chunk]
        copy = pltpu.make_async_remote_copy(
            src_ref=source,
            dst_ref=o_ref.at[origin, chunk],
            send_sem=send_sem.at[way, step, chunk],
            recv_sem=recv_sem.at[way, step, chunk],
            device_id={axis: target},
            device_id_type=MESH_ID,
        )
        landing = pltpu.make_async_remote_copy(
            src_ref=x_ref.at[chunk],
            dst_ref=o_ref.at[incoming, chunk],
            send_sem=send_sem.at[way, step, chunk],
            recv_sem=recv_sem.at[way, step, chunk],
            device_id={axis: target},
            device_id_type=MESH_ID,
        )
        return copy, sends, landing, arrives

    for step in range(n - 1):
        for chunk in range(chunks):
            for way in (0, 1):
                if step > 0:
                    _, _, landing, arrives = hop(way, step - 1, chunk)

                    @pl.when(arrives)
                    def _():
                        landing.wait_recv()

                copy, sends, _, _ = hop(way, step, chunk)

                @pl.when(sends)
                def _():
                    copy.start()

    for way in (0, 1):
        for chunk in range(chunks):
            _, _, landing, arrives = hop(way, n - 2, chunk)

            @pl.when(arrives)
            def _():
                landing.wait_recv()

            for step in range(n - 1):
                copy, sends, _, _ = hop(way, step, chunk)

                @pl.when(sends)
                def _():
                    copy.wait_send()
    local.wait()


def relay_gather(value, axis, collective_id):
    n = lax.axis_size(axis)
    chunks = value.shape[0]
    vmem = pl.BlockSpec(memory_space=pltpu.VMEM)
    return pl.pallas_call(
        functools.partial(relay_kernel, axis, n, chunks),
        out_shape=jax.ShapeDtypeStruct((n,) + value.shape, value.dtype),
        in_specs=[vmem],
        out_specs=vmem,
        scratch_shapes=[
            pltpu.SemaphoreType.DMA((2, n, chunks)),
            pltpu.SemaphoreType.DMA((2, n, chunks)),
            pltpu.SemaphoreType.DMA((1,)),
        ],
        compiler_params=pltpu.CompilerParams(collective_id=collective_id, has_side_effects=True),
    )(value)


def reduce_kernel(sizes, part_ref, fwd_ref, bwd_ref, out_ref, fwd_out, bwd_out,
                  first_buf, first_sum, second_buf, third_buf, sems):
    nx, ny, nz = sizes
    plane = ("gx", "gy")
    plane_sizes = (nx, ny)
    n_plane = nx * ny
    me_x = lax.axis_index("gx")
    me_y = lax.axis_index("gy")
    me_z = lax.axis_index("gz")
    me_p = me_x * ny + me_y
    barrier = pltpu.get_barrier_semaphore()
    for step in range(1, nz):
        peer = {"gz": lax.rem(me_z + step, nz)}
        pl.semaphore_signal(barrier, inc=1, device_id=peer, device_id_type=MESH_ID)
    for step in range(1, n_plane):
        peer = job_peer(plane, plane_sizes, lax.rem(me_p + step, n_plane))
        pl.semaphore_signal(barrier, inc=1, device_id=peer, device_id_type=MESH_ID)
    pl.semaphore_wait(barrier, nz - 1 + n_plane - 1)

    def send_all(axes, axis_sizes, me, src_of, dst_of, slot):
        n = math.prod(axis_sizes)
        copies = []
        local = pltpu.make_async_copy(src_of(me), dst_of(me), sems.at[slot, 0, 0])
        local.start()
        copies.append(local)
        for step in range(1, n):
            linear = lax.rem(me + step, n)
            copy = pltpu.make_async_remote_copy(
                src_ref=src_of(linear),
                dst_ref=dst_of(me),
                send_sem=sems.at[slot, 0, step],
                recv_sem=sems.at[slot, 1, step],
                device_id=job_peer(axes, axis_sizes, linear),
                device_id_type=MESH_ID,
            )
            copy.start()
            copies.append(copy)
        return copies

    gathers = send_all(("gy",), (ny,), me_y, lambda k: fwd_ref, lambda k: fwd_out.at[k], 4)
    gathers += send_all(("gx",), (nx,), me_x, lambda k: bwd_ref, lambda k: bwd_out.at[k], 5)
    stage = send_all(("gz",), (nz,), me_z, lambda k: part_ref.at[k], lambda k: first_buf.at[k], 0)
    for copy in stage:
        copy.wait()
    first_sum[...] = jnp.sum(first_buf[...], axis=0)
    stage = send_all(plane, plane_sizes, me_p, lambda k: first_sum.at[k], lambda k: second_buf.at[k], 1)
    for copy in stage:
        copy.wait()
    first_sum[0] = jnp.sum(second_buf[...], axis=0)
    stage = send_all(plane, plane_sizes, me_p, lambda k: first_sum.at[0], lambda k: third_buf.at[k], 2)
    for copy in stage:
        copy.wait()
    stage = send_all(("gz",), (nz,), me_z, lambda k: third_buf, lambda k: out_ref.at[k], 3)
    for copy in stage:
        copy.wait()
    for copy in gathers:
        copy.wait()


def reduce_everywhere(parts, forward_peram, backward_peram):
    nx, ny, nz = lax.axis_size("gx"), lax.axis_size("gy"), lax.axis_size("gz")
    widest = max(nx * ny, nz)
    piece = parts.shape[1:]
    vmem = pl.BlockSpec(memory_space=pltpu.VMEM)
    return pl.pallas_call(
        functools.partial(reduce_kernel, (nx, ny, nz)),
        out_shape=(
            jax.ShapeDtypeStruct(parts.shape, parts.dtype),
            jax.ShapeDtypeStruct((ny,) + forward_peram.shape, forward_peram.dtype),
            jax.ShapeDtypeStruct((nx,) + backward_peram.shape, backward_peram.dtype),
        ),
        in_specs=[vmem] * 3,
        out_specs=(vmem, vmem, vmem),
        scratch_shapes=[
            pltpu.VMEM(parts.shape, parts.dtype),
            pltpu.VMEM(piece, parts.dtype),
            pltpu.VMEM(piece, parts.dtype),
            pltpu.VMEM(piece, parts.dtype),
            pltpu.SemaphoreType.DMA((6, 2, widest)),
        ],
        compiler_params=pltpu.CompilerParams(collective_id=0, has_side_effects=True),
    )(parts, forward_peram, backward_peram)


def halo_kernel(sizes, one_ref, two_ref, three_ref, one_out, two_out, three_out, send_sem, recv_sem):
    axes = ("gx", "gy", "gz")
    barrier = pltpu.get_barrier_semaphore()
    for axis, n in zip(axes, sizes):
        me = lax.axis_index(axis)
        for peer in (lax.rem(me + n - 1, n), lax.rem(me + 1, n)):
            pl.semaphore_signal(barrier, inc=1, device_id={axis: peer}, device_id_type=MESH_ID)
    pl.semaphore_wait(barrier, 2 * len(axes))
    copies = []
    for slot, (axis, n, src, dst) in enumerate(
        zip(axes, sizes, (one_ref, two_ref, three_ref), (one_out, two_out, three_out))
    ):
        me = lax.axis_index(axis)
        copy = pltpu.make_async_remote_copy(
            src_ref=src,
            dst_ref=dst,
            send_sem=send_sem.at[slot],
            recv_sem=recv_sem.at[slot],
            device_id={axis: lax.rem(me + n - 1, n)},
            device_id_type=MESH_ID,
        )
        copy.start()
        copies.append(copy)
    for copy in copies:
        copy.wait()


def halo_exchange(faces):
    sizes = tuple(lax.axis_size(axis) for axis in ("gx", "gy", "gz"))
    flat = [face.reshape(-1, face.shape[-1]) for face in faces]
    vmem = pl.BlockSpec(memory_space=pltpu.VMEM)
    got = pl.pallas_call(
        functools.partial(halo_kernel, sizes),
        out_shape=tuple(jax.ShapeDtypeStruct(face.shape, face.dtype) for face in flat),
        in_specs=[vmem] * 3,
        out_specs=(vmem, vmem, vmem),
        scratch_shapes=[pltpu.SemaphoreType.DMA((3,)), pltpu.SemaphoreType.DMA((3,))],
        compiler_params=pltpu.CompilerParams(collective_id=3, has_side_effects=True),
    )(*flat)
    return [value.reshape(face.shape) for value, face in zip(got, faces)]


def transport(link_dir, shifted):
    highest = lax.Precision.HIGHEST
    real_v = shifted[..., 0, :, :].astype(jnp.float32)
    imag_v = shifted[..., 1, :, :].astype(jnp.float32)
    real_u = link_dir[..., 0, :, :]
    imag_u = link_dir[..., 1, :, :]

    def apply_link(matrix, vector):
        return jnp.einsum("...ab,...bn->...an", matrix, vector, precision=highest)

    moved_re = apply_link(real_u, real_v) - apply_link(imag_u, imag_v)
    moved_im = apply_link(real_u, imag_v) + apply_link(imag_u, real_v)
    moved = jnp.stack([moved_re, moved_im], axis=-3).astype(jnp.bfloat16)
    turned = jnp.stack([moved_im, -moved_re], axis=-3).astype(jnp.bfloat16)
    return (moved, turned)


def correlation(vec_part, moved, turned):
    width = vec_part.shape[-1]
    left_side = vec_part.reshape(-1, width)
    right_side = jnp.concatenate([moved.reshape(-1, width), turned.reshape(-1, width)], axis=1)
    product = lax.dot_general(
        left_side, right_side, (((0,), (0,)), ((), ())), preferred_element_type=jnp.float32
    )
    return jnp.stack([product[:, :width], product[:, width:]])


def complex_product(left_mat, right_mat):
    row_count = left_mat.shape[1]
    stacked = left_mat.reshape(2 * row_count, left_mat.shape[2])
    first_half = jnp.dot(stacked, right_mat[0], preferred_element_type=jnp.float32)
    second_half = jnp.dot(stacked, right_mat[1], preferred_element_type=jnp.float32)
    return jnp.stack(
        [
            first_half[:row_count] - second_half[row_count:],
            second_half[:row_count] + first_half[row_count:],
        ]
    )


def spin_block(elem, spin):
    highest = lax.Precision.HIGHEST
    rows, cols = elem.shape[1], elem.shape[2]
    big_rows = lax.broadcasted_iota(jnp.int32, (4 * rows, rows), 0)
    row_expand = (big_rows // 4 == lax.broadcasted_iota(jnp.int32, (4 * rows, rows), 1)).astype(jnp.float32)
    big_cols = lax.broadcasted_iota(jnp.int32, (cols, 4 * cols), 1)
    col_expand = (big_cols // 4 == lax.broadcasted_iota(jnp.int32, (cols, 4 * cols), 0)).astype(jnp.float32)
    spin_rows = (
        lax.broadcasted_iota(jnp.int32, (4 * rows, 4), 0) % 4
        == lax.broadcasted_iota(jnp.int32, (4 * rows, 4), 1)
    ).astype(jnp.float32)
    spin_cols = (
        lax.broadcasted_iota(jnp.int32, (4, 4 * cols), 1) % 4
        == lax.broadcasted_iota(jnp.int32, (4, 4 * cols), 0)
    ).astype(jnp.float32)
    repeated = jnp.einsum("ar,crq->caq", row_expand, elem, precision=highest)
    repeated = jnp.einsum("caq,qb->cab", repeated, col_expand, precision=highest)
    tiled = jnp.dot(jnp.dot(spin_rows, spin, precision=highest), spin_cols, precision=highest)
    return (repeated * tiled[None]).astype(jnp.bfloat16)


def spin_times(elem, spin, right):
    n = elem.shape[1]
    highest = lax.Precision.HIGHEST
    wide = 4 * n
    pick = (
        lax.broadcasted_iota(jnp.int32, (4, n, wide), 2)
        == 4 * lax.broadcasted_iota(jnp.int32, (4, n, wide), 1) + lax.broadcasted_iota(jnp.int32, (4, n, wide), 0)
    ).astype(right.dtype)
    split = jnp.einsum("tcm,xmn->xtcn", pick, right, preferred_element_type=jnp.float32).astype(right.dtype)
    low = elem.astype(jnp.bfloat16)

    def mul(a, b):
        return jnp.einsum("rc,tcn->trn", a, b, preferred_element_type=jnp.float32)

    real = mul(low[0], split[0]) - mul(low[1], split[1])
    imag = mul(low[0], split[1]) + mul(low[1], split[0])
    mixed = jnp.einsum("st,xtrn->xsrn", spin, jnp.stack([real, imag]), precision=highest)
    place = (
        lax.broadcasted_iota(jnp.int32, (wide, 4, n), 0)
        == 4 * lax.broadcasted_iota(jnp.int32, (wide, 4, n), 2) + lax.broadcasted_iota(jnp.int32, (wide, 4, n), 1)
    ).astype(jnp.bfloat16)
    placed = jnp.einsum(
        "msr,xsrn->xmn", place, mixed.astype(jnp.bfloat16), preferred_element_type=jnp.float32
    )
    return placed.astype(jnp.bfloat16)


def on_device(eigvecs, links, directions, spin_mats, forward_peram, backward_peram, chain_order):
    face_one, face_two, face_three = halo_exchange(
        [
            lax.slice_in_dim(eigvecs, 0, 1, axis=0),
            lax.slice_in_dim(eigvecs, 0, 1, axis=1),
            lax.slice_in_dim(eigvecs, 0, 1, axis=2),
        ]
    )
    shifted = [
        jnp.concatenate([eigvecs[1:], face_one], axis=0),
        jnp.concatenate([eigvecs[:, 1:], face_two], axis=1),
        jnp.concatenate([eigvecs[:, :, 1:], face_three], axis=2),
    ]
    terms = []
    for direction in range(3):
        moved, turned = transport(links[:, :, :, direction], shifted[direction])
        terms.append(correlation(eigvecs, moved, turned))
    num_vecs = eigvecs.shape[-1]
    nx, ny, nz = lax.axis_size("gx"), lax.axis_size("gy"), lax.axis_size("gz")
    volume = eigvecs.shape[0] * eigvecs.shape[1] * eigvecs.shape[2] * nx * ny * nz
    partial_dirs = jnp.stack(terms) * (1.0 / math.sqrt(12.0 * volume))

    full_shape = partial_dirs.shape
    lanes = 128
    rows = partial_dirs.size // lanes
    parts = partial_dirs.reshape(nz, nx * ny, rows // (nz * nx * ny), lanes)
    tile = forward_peram.shape[1]
    summed, forward_rows, backward_cols = reduce_everywhere(parts, forward_peram, backward_peram)
    elem_dirs = summed.reshape(full_shape)

    row_tile = num_vecs // nx
    col_tile = num_vecs // ny
    row_start = lax.axis_index("gx") * row_tile
    col_start = lax.axis_index("gy") * col_tile
    inverse = 1.0 / math.sqrt(4 * num_vecs)

    forward_rows = jnp.transpose(forward_rows, (1, 2, 0, 3)).reshape(2, tile, ny * tile)
    backward_cols = jnp.transpose(backward_cols, (1, 0, 2, 3)).reshape(2, nx * tile, tile)

    op_count = chain_order.shape[0]
    lefts = []
    tails = []
    for op_index in range(op_count):
        left_k = chain_order[op_index, 0]
        right_k = chain_order[op_index, 1]
        left_dir = lax.dynamic_index_in_dim(elem_dirs, directions[left_k], 0, keepdims=False)
        right_dir = lax.dynamic_index_in_dim(elem_dirs, directions[right_k], 0, keepdims=False)
        left_spin = lax.dynamic_index_in_dim(spin_mats, left_k, 0, keepdims=False)
        right_spin = lax.dynamic_index_in_dim(spin_mats, right_k, 0, keepdims=False)
        left_rows = lax.dynamic_slice_in_dim(left_dir, row_start, row_tile, axis=1)
        lefts.append(spin_block(left_rows, left_spin))
        right_back = spin_times(right_dir, right_spin, backward_cols)
        tails.append(complex_product(forward_rows, right_back).astype(jnp.bfloat16))
    tail_cols = relay_gather(jnp.stack(tails).reshape(op_count * 4, tile // 2, tile), "gx", 1)
    tail_cols = tail_cols.reshape(nx, op_count, 2, tile, tile)
    tail_cols = jnp.transpose(tail_cols, (1, 2, 0, 3, 4)).reshape(op_count, 2, nx * tile, tile)
    results = []
    for op_index in range(op_count):
        final = complex_product(lefts[op_index], tail_cols[op_index]) * inverse
        results.append(final.astype(jnp.bfloat16))
    return jnp.stack(results)


def solution(mesh):
    in_specs = (
        P("gx", "gy", "gz", None, None, None),
        P("gx", "gy", "gz", None, None, None, None),
        P(),
        P(),
        P(None, "gx", "gy"),
        P(None, "gx", "gy"),
        P("gz", None),
    )
    out_specs = P("gz", None, "gx", "gy")
    return jax.shard_map(
        on_device, mesh=mesh, in_specs=in_specs, out_specs=out_specs, check_vma=False
    )
```
